32 devices in a mesh: groups: 2 (over y), coef: 4 (over x, core), slab: 4 (over z).
Axes of the slice: x: 2, y: 2, z: 4, core: 2. Of those that a mesh axis runs over, the one named last changes fastest.
Arguments:
- coefficients: float32 [896, 32768], P('coef', ('groups', 'slab')), parts along dimension 1, may hold values from -6 to 6
- measured: float32 [16, 4, 64, 256], P('groups', 'slab'), parts along dimension 0, may hold values from -6 to 6
- ray_voxels: int32 [8, 64, 128], replicated, may hold values from 0 to 4095
- ray_weights: int32 [8, 64, 128], replicated, may hold values from 1 to 63
- angle_ids: int32 [8], replicated, may hold values from 0 to 15
- angle_table: bfloat16 [16, 896, 256], P(None, 'coef'), may hold values from -0.1875 to 0.1875
- harmonics: bfloat16 [896, 2048], P('coef'), may hold values from -0.1875 to 0.1875
Outputs:
- updated: float32 [896, 32768], P('coef', ('groups', 'slab')), parts along dimension 1
- residual: float32 [16, 4, 64, 256], P('groups', 'slab', None, 'coef'), parts along dimension 0
The draws below stay inside these ranges and needn't reach their ends.
There are 2 independent parts, one for each index of `groups`. The reference program is written for one: setup_inputs(seed, part) draws one part's arguments, and reference() takes and returns one part's arrays. A program takes and returns all parts, laid end to end along the dimension named above; an argument that names none is the same for every part. Nothing has to cross between parts.
All inputs are finite; a program needn't handle non-finite values.
Results may differ from the reference program's by a relative error of at most 0.0034.
Values may be sent and summed in bfloat16 or wider, within the bound.
No kernel may reach another device: no remote copies, remote signals or barrier semaphores. Data moves between devices by JAX's collectives and lax.ppermute only.
A program may use at most 64 MiB of HBM per device.

```python
import jax
import jax.numpy as jnp
from jax import lax

NG = 64
P_SIZE = 8
NA = 16
HARMONIC_COUNT = 896
CH = 256
O = 2048
SAMPLES = 128
NZ = 4
VOXEL_TOTAL = 16384


def set_ends(values, own_key, smallest, largest):
    place = [jax.random.randint(jax.random.fold_in(own_key, axis), (), 0, length) for axis, length in enumerate(values.shape)]
    main_axis = values.shape.index(max(values.shape))
    neighbour = place[:main_axis] + [(place[main_axis] + 1) % values.shape[main_axis]] + place[main_axis + 1:]
    return values.at[tuple(place)].set(smallest).at[tuple(neighbour)].set(largest)


def level_of(stream_key, dims, cuts, least, top_value):
    def one(axis_at, blocks):
        steps = jax.random.uniform(jax.random.fold_in(jax.random.fold_in(stream_key, 6), axis_at), (blocks,), jnp.float32, least / len(cuts), top_value / len(cuts))
        return jnp.repeat(jnp.exp(steps), dims[axis_at] // blocks).reshape((-1,) + (1,) * (len(dims) - axis_at - 1))

    gain = one(*cuts[0])
    for cut in cuts[1:]:
        gain = gain * one(*cut)
    return gain


def noise(stream_key, dims, deviation, limit, split=(), dtype=jnp.bfloat16):
    array = jax.random.normal(stream_key, dims, jnp.float32) * deviation
    if len(split) > 0:
        array = level_of(stream_key, dims, split, -0.22, 0.18) * array
    return jnp.clip(array, min=-limit, max=limit).astype(dtype)


def setup_inputs(seed: int = 0, part: int = 0) -> dict:
    arg_keys = jax.random.split(jax.random.key(seed), 8)
    own_keys = jax.random.split(jax.random.fold_in(arg_keys[7], part), 8)
    return {
        "coefficients": noise(own_keys[0], (HARMONIC_COUNT, VOXEL_TOTAL), 1.0, 6.0, ((0, 4), (1, 4)), jnp.float32),
        "measured": noise(own_keys[1], (P_SIZE, NZ, NG, CH), 1.0, 6.0, ((1, 4),), jnp.float32),
        "ray_voxels": set_ends(jax.random.randint(arg_keys[2], (P_SIZE, NG, SAMPLES), 0, NG * NG), jax.random.fold_in(arg_keys[2], 1), 0, (NG * NG) - 1).astype(jnp.int32),
        "ray_weights": set_ends(jax.random.randint(arg_keys[3], (P_SIZE, NG, SAMPLES), 1, 64), jax.random.fold_in(arg_keys[3], 1), 1, 63).astype(jnp.int32),
        "angle_ids": set_ends(jax.random.randint(arg_keys[4], (P_SIZE,), 0, NA), jax.random.fold_in(arg_keys[4], 1), 0, NA - 1).astype(jnp.int32),
        "angle_table": noise(arg_keys[5], (NA, HARMONIC_COUNT, CH), HARMONIC_COUNT ** -0.5, 0.1875, ((1, 4),)),
        "harmonics": noise(arg_keys[6], (HARMONIC_COUNT, O), HARMONIC_COUNT ** -0.5, 0.1875, ((0, 4),)),
    }


def build_matrix(ray_voxels, ray_weights):
    shape_all = ray_voxels.shape
    angle_pos = jnp.broadcast_to(jnp.arange(shape_all[0])[:, None, None], shape_all)
    ray_pos = jnp.broadcast_to(jnp.arange(shape_all[1])[None, :, None], shape_all)
    values = ray_weights.astype(jnp.float32) / 256.0
    system_matrix = jnp.zeros((shape_all[0], shape_all[1], NG * NG), jnp.float32).at[angle_pos, ray_pos, ray_voxels].add(values)
    return system_matrix.astype(jnp.bfloat16)


def select_angles(angle_ids, angle_table):
    entries = angle_table.shape[0]
    onehot = (angle_ids[:, None] == jnp.arange(entries)[None, :]).astype(jnp.bfloat16)
    flat_table = angle_table.reshape(entries, -1)
    picked = jnp.dot(onehot, flat_table, preferred_element_type=jnp.float32)
    return picked.astype(jnp.bfloat16).reshape((angle_ids.shape[0],) + angle_table.shape[1:])


def reference(coefficients, measured, ray_voxels, ray_weights, angle_ids, angle_table, harmonics):
    system_matrix = build_matrix(ray_voxels, ray_weights).astype(jnp.float32)
    chosen = select_angles(angle_ids, angle_table).astype(jnp.float32)
    coef_half = coefficients.astype(jnp.bfloat16)
    stacked_rows = coef_half.astype(jnp.float32).reshape(HARMONIC_COUNT, NZ, NG * NG)
    ray_totals = jnp.einsum('dmj,hqj->dqmh', system_matrix, stacked_rows).astype(jnp.bfloat16)
    ray_totals = lax.optimization_barrier(ray_totals).astype(jnp.float32)
    predicted = jnp.einsum('azrk,akc->azrc', ray_totals, chosen)
    residual = predicted - measured
    resid_half = lax.optimization_barrier(residual.astype(jnp.bfloat16)).astype(jnp.float32)
    backward_projection = jnp.einsum('azrc,akc->azrk', resid_half, chosen).astype(jnp.bfloat16)
    backward_projection = lax.optimization_barrier(backward_projection).astype(jnp.float32)
    misfit_gradient = jnp.einsum('qci,qbcy->ybi', system_matrix, backward_projection).reshape(HARMONIC_COUNT, VOXEL_TOTAL)

    def regular_layer(layer_coef):
        orient_field = lax.dot_general(layer_coef, harmonics, (((0,), (0,)), ((), ())), preferred_element_type=jnp.float32)
        slope_half = (-jax.nn.sigmoid(-orient_field)).astype(jnp.bfloat16)
        return lax.dot_general(harmonics, slope_half, (((1,), (1,)), ((), ())), preferred_element_type=jnp.float32)

    by_layer = jnp.transpose(coef_half.reshape(HARMONIC_COUNT, NZ, NG * NG), (1, 0, 2))
    reg_layers = lax.map(regular_layer, by_layer)
    reg_grad = jnp.transpose(reg_layers, (1, 0, 2)).reshape(HARMONIC_COUNT, VOXEL_TOTAL)
    updated = coefficients - 0.5 * misfit_gradient - 0.5 * reg_grad
    return updated, residual
```

```python
import jax
import jax.numpy as jnp
from jax import lax
from jax.experimental import pallas as pl
from jax.experimental.pallas import tpu as pltpu
from jax.sharding import PartitionSpec as P


LANES = 128
CHUNKS = 2
NT = (((1,), (1,)), ((), ()))
NN = (((1,), (0,)), ((), ()))
VMEM = pl.BlockSpec(memory_space=pltpu.VMEM)
SMEM = pl.BlockSpec(memory_space=pltpu.SMEM)


def dot(a, b, dims):
    return lax.dot_general(a, b, dims, preferred_element_type=jnp.float32)


def swap(value, axis, mask):
    count = lax.axis_size(axis)
    return lax.ppermute(value, axis, [(i, i ^ mask) for i in range(count)])


def forward_kernel(ids, side, vox_ref, wgt_ref, coef_ref, table_ref, matrix_ref, mine_ref, other_ref, tile_ref, sums_ref):
    rows, samples = vox_ref.shape
    cols = matrix_ref.shape[1]
    high_count = cols // LANES
    group = 16
    low_pos = lax.broadcasted_iota(jnp.int32, (LANES, samples), 0)
    high_pos = lax.broadcasted_iota(jnp.int32, (high_count, samples), 0)

    def build(step, carry):
        first = pl.multiple_of(step * group, group)
        vox = vox_ref[pl.ds(first, group), :]
        wgt = wgt_ref[pl.ds(first, group), :].astype(jnp.float32) * (1.0 / 256.0)
        low = vox & (LANES - 1)
        high = lax.shift_right_logical(vox, LANES.bit_length() - 1)
        for i in range(group):
            low_hot = (low_pos == low[i:i + 1]).astype(jnp.float32).astype(jnp.bfloat16)
            high_hot = jnp.where(high_pos == high[i:i + 1], wgt[i:i + 1], 0.0).astype(jnp.bfloat16)
            tile_ref[i * high_count:(i + 1) * high_count, :] = dot(high_hot, low_hot, NT)
        for h in range(high_count):
            part = tile_ref[pl.ds(h, group, stride=high_count), :]
            matrix_ref[pl.ds(first, group), h * LANES:(h + 1) * LANES] = part.astype(jnp.bfloat16)
        return carry

    lax.fori_loop(0, rows // group, build, 0)
    coef_half = coef_ref[...].astype(jnp.bfloat16)
    sums_ref[...] = dot(matrix_ref[...], coef_half, NT).astype(jnp.bfloat16)
    half, rays = mine_ref.shape[:2]
    for out_ref, start in ((mine_ref, side[0] * half), (other_ref, (1 - side[0]) * half)):
        for i in range(half):
            a = start + i
            sums = sums_ref[pl.ds(pl.multiple_of(a * rays, rays), rays), :]
            out_ref[i] = dot(sums, table_ref[ids[a]], NN)


def penalty_kernel(count, pieces, place, *refs):
    blocks = refs[:count]
    own, near = refs[count:count + 2]
    far = refs[count + 2:count + 2 + (count - 2) * pieces]
    outs = refs[count + 2 + (count - 2) * pieces:][:count]
    accs = refs[-count:]
    width = own.shape[1] // pieces
    turned = [jnp.swapaxes(b[...], 0, 1) for b in blocks]
    for r in range(pieces):
        at = pl.multiple_of((place[0] ^ r) * width, width)
        waves = [own[:, pl.ds(at, width)], near[:, pl.ds(at, width)]]
        waves += [far[j * pieces + r][...] for j in range(count - 2)]
        field = dot(turned[0], waves[0], NN)
        for j in range(1, count):
            field += dot(turned[j], waves[j], NN)
        slope = (0.5 * jnp.tanh(0.5 * field) - 0.5).astype(jnp.bfloat16)
        for j in range(count):
            part = dot(waves[j], slope, NT)
            if r > 0:
                part += accs[j][...]
            if r == pieces - 1:
                outs[j][...] = part.astype(outs[j].dtype)
            else:
                accs[j][...] = part


def data_kernel(ids, side, mine_ref, other_ref, table_ref, top_ref, low_ref, coef_ref, out_ref, back_a, back_b):
    half, rays = mine_ref.shape[:2]

    @pl.when(pl.program_id(0) == 0)
    def _():
        for back, ref, start in ((back_a, mine_ref, side[0] * half), (back_b, other_ref, (1 - side[0]) * half)):
            for i in range(half):
                part = dot(table_ref[ids[start + i]], ref[i].astype(jnp.bfloat16), NT)
                back[:, i * rays:(i + 1) * rays] = part.astype(jnp.bfloat16)

    grad = dot(back_a[...], top_ref[...], NN) + dot(back_b[...], low_ref[...], NN)
    out_ref[...] = coef_ref[...] - 0.5 * grad


def finish_kernel(count, place, base_ref, *refs):
    out_ref = refs[count]
    for j in range(count):
        @pl.when(pl.program_id(0) == j)
        def _():
            out_ref[...] = base_ref[...] - 0.5 * refs[j][...].astype(jnp.float32)


def body(coefficients, measured, ray_voxels, ray_weights, angle_ids, angle_table, harmonics):
    coef_local, cols = coefficients.shape
    projections, _, rays, channels = measured.shape
    rows = projections * rays
    samples = ray_voxels.shape[2]
    count = lax.axis_size("coef")
    me = lax.axis_index("coef")
    side = (me & 1).reshape(1)
    half = projections // 2
    block = cols // count
    chunk = block // CHUNKS
    bf16, f32 = jnp.bfloat16, jnp.float32
    params = pltpu.CompilerParams(vmem_limit_bytes=48 * 1024 * 1024)

    group_bits = 1 if lax.axis_size("groups") % 2 == 0 else 0
    slab_bits = 1 if lax.axis_size("slab") % 2 == 0 else 0
    pieces = 1 << (group_bits + slab_bits)
    place = jnp.zeros((), jnp.int32)
    if slab_bits:
        place = place + (lax.axis_index("slab") & 1)
    if group_bits:
        place = place + ((lax.axis_index("groups") & 1) << slab_bits)
    width = harmonics.shape[1] // pieces
    piece = lax.dynamic_slice_in_dim(harmonics, place * width, width, 1)
    fetched = {m: [swap(piece, "coef", m)] for m in range(2, count, 2)}

    def part_of(mask, t):
        start = (me ^ mask) * block + t * chunk
        return lax.dynamic_slice_in_dim(coefficients, start, chunk, 1).astype(bf16)

    order = [m for m in range(count) if m > 1] + [1]
    received = []
    for t in range(CHUNKS):
        got = {m: swap(part_of(m, t), "coef", m) for m in order}
        got[0] = part_of(0, t)
        received.append([got[m] for m in range(count)])

    near = swap(harmonics, "coef", 1)
    for m in fetched:
        if slab_bits:
            fetched[m] += [swap(v, "slab", 1) for v in fetched[m]]
        if group_bits:
            fetched[m] += [swap(v, "groups", 1) for v in fetched[m]]
    for m in list(fetched):
        fetched[m ^ 1] = [swap(v, "coef", 1) for v in fetched[m]]
    far = [v for m in range(2, count) for v in fetched[m]]

    matrix, mine, other = pl.pallas_call(
        forward_kernel,
        in_specs=[SMEM, SMEM, VMEM, VMEM, VMEM, VMEM],
        out_specs=[VMEM, VMEM, VMEM],
        out_shape=[
            jax.ShapeDtypeStruct((rows, cols), bf16),
            jax.ShapeDtypeStruct((half, rays, channels), f32),
            jax.ShapeDtypeStruct((half, rays, channels), f32),
        ],
        scratch_shapes=[pltpu.VMEM((16 * cols // LANES, LANES), f32), pltpu.VMEM((rows, coef_local), bf16)],
        compiler_params=params,
        name="forward",
    )(angle_ids, side, ray_voxels.reshape(rows, samples), ray_weights.reshape(rows, samples), coefficients, angle_table)

    total = mine + swap(other, "coef", 1)
    mask = 2
    while mask < count:
        total = total + swap(total, "coef", mask)
        mask *= 2
    target = lax.dynamic_slice_in_dim(measured.reshape(projections, rays, channels), side[0] * half, half, 0)
    resid_mine = total - target
    resid_other = swap(resid_mine, "coef", 1)
    is_low = side[0] == 0
    resid_all = jnp.concatenate(
        [jnp.where(is_low, resid_mine, resid_other), jnp.where(is_low, resid_other, resid_mine)], 0
    )
    own_width = channels // count
    residual = lax.dynamic_slice_in_dim(resid_all, me * own_width, own_width, 2)[:, None]

    returned = []
    for t in range(CHUNKS):
        outs = pl.pallas_call(
            lambda *refs: penalty_kernel(count, pieces, *refs),
            in_specs=[SMEM] + [VMEM] * (count + 2 + len(far)),
            out_specs=[VMEM] * count,
            out_shape=[jax.ShapeDtypeStruct((coef_local, chunk), bf16)] * count,
            scratch_shapes=[pltpu.VMEM((coef_local, chunk), f32)] * count,
            compiler_params=params,
            name=f"penalty{t}",
        )(place.reshape(1), *received[t], harmonics, near, *far)
        back = {m: swap(outs[m], "coef", m) for m in order}
        back[0] = outs[0]
        returned.append([back[m] for m in range(count)])

    step = min(512, cols)
    updated = pl.pallas_call(
        data_kernel,
        grid_spec=pltpu.PrefetchScalarGridSpec(
            num_scalar_prefetch=2,
            grid=(cols // step,),
            in_specs=[
                pl.BlockSpec((half, rays, channels), lambda i, ids, side: (0, 0, 0)),
                pl.BlockSpec((half, rays, channels), lambda i, ids, side: (0, 0, 0)),
                pl.BlockSpec(angle_table.shape, lambda i, ids, side: (0, 0, 0)),
                pl.BlockSpec((rows // 2, step), lambda i, ids, side: (side[0], i)),
                pl.BlockSpec((rows // 2, step), lambda i, ids, side: (1 - side[0], i)),
                pl.BlockSpec((coef_local, step), lambda i, ids, side: (0, i)),
            ],
            out_specs=pl.BlockSpec((coef_local, step), lambda i, ids, side: (0, i)),
            scratch_shapes=[pltpu.VMEM((coef_local, rows // 2), bf16)] * 2,
        ),
        out_shape=jax.ShapeDtypeStruct((coef_local, cols), f32),
        compiler_params=params,
        name="data",
    )(angle_ids, side, resid_mine, resid_other, angle_table, matrix, matrix, coefficients)

    for t in range(CHUNKS):
        where = lambda i, me, t=t: (0, (me[0] ^ i) * CHUNKS + t)
        updated = pl.pallas_call(
            lambda *refs: finish_kernel(count, *refs),
            grid_spec=pltpu.PrefetchScalarGridSpec(
                num_scalar_prefetch=1,
                grid=(count,),
                in_specs=[pl.BlockSpec((coef_local, chunk), where)]
                + [pl.BlockSpec((coef_local, chunk), lambda i, me: (0, 0))] * count,
                out_specs=pl.BlockSpec((coef_local, chunk), where),
            ),
            out_shape=jax.ShapeDtypeStruct((coef_local, cols), f32),
            input_output_aliases={1: 0},
            compiler_params=params,
            name=f"finish{t}",
        )(me.reshape(1), updated, *returned[t])
    return (updated, residual)


def solution(mesh):
    in_specs = (
        P("coef", ("groups", "slab")),
        P("groups", "slab", None, None),
        P(),
        P(),
        P(),
        P(None, "coef", None),
        P("coef", None),
    )
    out_specs = (P("coef", ("groups", "slab")), P("groups", "slab", None, "coef"))
    return jax.shard_map(body, mesh=mesh, in_specs=in_specs, out_specs=out_specs, check_vma=False)
```

```python
import jax
import jax.numpy as jnp
from jax import lax
from jax.experimental import pallas as pl
from jax.experimental.pallas import tpu as pltpu
from jax.sharding import PartitionSpec as P


LANES = 128
CHUNKS = 2
GROUP = 16
NT = (((1,), (1,)), ((), ()))
NN = (((1,), (0,)), ((), ()))
VMEM = pl.BlockSpec(memory_space=pltpu.VMEM)
SMEM = pl.BlockSpec(memory_space=pltpu.SMEM)
HBM = pl.BlockSpec(memory_space=pltpu.HBM)


def dot(a, b, dims):
    return lax.dot_general(a, b, dims, preferred_element_type=jnp.float32)


def swap(value, axis, mask):
    count = lax.axis_size(axis)
    return lax.ppermute(value, axis, [(i, i ^ mask) for i in range(count)])


def aligned(index, width):
    return pl.ds(pl.multiple_of(index * width, width), width)


def prepare_kernel(count, info, ids, coef, harm, vox, wgt, table, *refs):
    blocks, (piece, vox_out, wgt_out, chosen, stage, sems) = refs[:count], refs[count:]
    me, side, place = info[0], info[1], info[2]
    block, width = blocks[0].shape[1], piece.shape[1]
    half_rows, projections = vox_out.shape[0], chosen.shape[0]
    half = projections // 2
    order = list(range(2, count)) + [1, 0]
    copies = {}
    for m in order:
        copies[m] = pltpu.make_async_copy(coef.at[:, aligned(me ^ m, block)], stage.at[m], sems.at[m])
    rest = [
        pltpu.make_async_copy(harm.at[:, aligned(place, width)], piece, sems.at[count]),
        pltpu.make_async_copy(vox.at[aligned(side, half_rows)], vox_out, sems.at[count + 1]),
        pltpu.make_async_copy(wgt.at[aligned(side, half_rows)], wgt_out, sems.at[count + 2]),
    ]
    for i in range(projections):
        a = jnp.where(i < half, side, 1 - side) * half + i % half
        rest.append(pltpu.make_async_copy(table.at[ids[a]], chosen.at[i], sems.at[count + 3 + i]))
    for m in order:
        copies[m].start()
    for c in rest:
        c.start()
    for m in order:
        copies[m].wait()
        blocks[m][...] = stage[m].astype(jnp.bfloat16)
    for c in rest:
        c.wait()


def build_kernel(vox_ref, wgt_ref, matrix_ref, tile_ref):
    rows, samples = vox_ref.shape
    cols = matrix_ref.shape[1]
    high_count = cols // LANES
    low_pos = lax.broadcasted_iota(jnp.int32, (LANES, samples), 0)
    high_pos = lax.broadcasted_iota(jnp.int32, (high_count, samples), 0)

    def build(step, carry):
        first = pl.multiple_of(step * GROUP, GROUP)
        vox = vox_ref[pl.ds(first, GROUP), :]
        wgt = wgt_ref[pl.ds(first, GROUP), :].astype(jnp.float32) * (1.0 / 256.0)
        low = vox & (LANES - 1)
        high = lax.shift_right_logical(vox, LANES.bit_length() - 1)
        for i in range(GROUP):
            low_hot = (low_pos == low[i:i + 1]).astype(jnp.float32).astype(jnp.bfloat16)
            high_hot = jnp.where(high_pos == high[i:i + 1], wgt[i:i + 1], 0.0).astype(jnp.bfloat16)
            tile_ref[i * high_count:(i + 1) * high_count, :] = dot(high_hot, low_hot, NT)
        for h in range(high_count):
            part = tile_ref[pl.ds(h, GROUP, stride=high_count), :]
            matrix_ref[pl.ds(first, GROUP), h * LANES:(h + 1) * LANES] = part.astype(jnp.bfloat16)
        return carry

    lax.fori_loop(0, rows // GROUP, build, 0)


def sums_kernel(count, info, top_ref, low_ref, *refs):
    blocks = refs[:count]
    chosen, measured, mine_ref, other_ref, target, sem = refs[count:]
    half, rays = mine_ref.shape[:2]
    block = blocks[0].shape[1]
    me, side = info[0], info[1]
    fetch = pltpu.make_async_copy(measured.at[pl.ds(side * half, half)], target, sem)
    fetch.start()
    for out_ref, ref, start in ((other_ref, low_ref, half), (mine_ref, top_ref, 0)):
        sums = jnp.zeros((ref.shape[0], blocks[0].shape[0]), jnp.float32)
        for j in range(count):
            sums += dot(ref[:, aligned(me ^ j, block)], blocks[j][...], NT)
        sums = sums.astype(jnp.bfloat16)
        for i in range(half):
            out_ref[i] = dot(sums[i * rays:(i + 1) * rays], chosen[start + i], NN)
    fetch.wait()
    mine_ref[...] = mine_ref[...] - (2.0 / count) * target[...]


def gather_kernel(count, pieces, info, own, near, *refs):
    far, (out, sems) = refs[:-2], refs[-2:]
    place = info[2]
    height = own.shape[0]
    width = own.shape[1] // pieces
    copies = []
    for r in range(pieces):
        spot = out.at[0:height, r * width:(r + 1) * width]
        copies.append(pltpu.make_async_copy(own.at[:, aligned(place ^ r, width)], spot, sems.at[r]))
    for c in copies:
        c.start()
    for r in range(pieces):
        out[height:2 * height, r * width:(r + 1) * width] = near[:, aligned(place ^ r, width)]
        for j in range(count - 2):
            out[(j + 2) * height:(j + 3) * height, r * width:(r + 1) * width] = far[j * pieces + r][...]
    for c in copies:
        c.wait()


def penalty_kernel(count, pieces, t, waves, *refs):
    blocks, outs = refs[:count], refs[count:2 * count]
    stack, turned, acc = refs[2 * count:]
    height, chunk = outs[0].shape
    width = waves.shape[1] // pieces
    for j in range(count):
        stack[j * height:(j + 1) * height, :] = blocks[j][:, t * chunk:(t + 1) * chunk]
    turned[...] = jnp.swapaxes(stack[...], 0, 1)
    for r in range(pieces):
        wave = waves[:, r * width:(r + 1) * width]
        field = dot(turned[...], wave, NN)
        slope = (0.5 * jnp.tanh(0.5 * field) - 0.5).astype(jnp.bfloat16)
        part = dot(wave, slope, NT)
        if r > 0:
            part += acc[...]
        if r < pieces - 1:
            acc[...] = part
        else:
            for j in range(count):
                outs[j][...] = part[j * height:(j + 1) * height].astype(outs[j].dtype)


def data_kernel(count, info, mine_ref, other_ref, chosen, top_ref, low_ref, coef, *refs):
    grads = refs[:count]
    updated, residual_ref, later, back_a, back_b, buf, sems, out_sems = refs[count:]
    me, side = info[0], info[1]
    half, rays = mine_ref.shape[:2]
    chunk = grads[0].shape[1]
    own_width = residual_ref.shape[2]

    def columns(j, t):
        return aligned((me ^ j) * CHUNKS + t, chunk)

    order = [(t, j) for t in range(CHUNKS) for j in range(count)]
    copies = {}
    for n, (t, j) in enumerate(order):
        spot = buf.at[j] if t == 0 else later.at[(t - 1) * count + j]
        copies[t, j] = pltpu.make_async_copy(coef.at[:, columns(j, t)], spot, sems.at[n])
        copies[t, j].start()
    for back, ref, start in ((back_a, mine_ref, 0), (back_b, other_ref, half)):
        for i in range(half):
            part = dot(chosen[start + i], ref[i].astype(jnp.bfloat16), NT)
            back[:, i * rays:(i + 1) * rays] = part.astype(jnp.bfloat16)
    writes = []
    for t, j in order:
        at = columns(j, t)
        grad = dot(back_a[...], top_ref[:, at], NN) + dot(back_b[...], low_ref[:, at], NN)
        copies[t, j].wait()
        if t == 0:
            buf[j] = buf[j] - 0.5 * grad - 0.5 * grads[j][...].astype(jnp.float32)
            writes.append(pltpu.make_async_copy(buf.at[j], updated.at[:, at], out_sems.at[j]))
            writes[-1].start()
        else:
            later[(t - 1) * count + j] = later[(t - 1) * count + j] - 0.5 * grad
    for q in range(count):
        @pl.when(me == q)
        def _():
            for i in range(half):
                residual_ref[side * half + i] = mine_ref[i, :, q * own_width:(q + 1) * own_width]
                residual_ref[(1 - side) * half + i] = other_ref[i, :, q * own_width:(q + 1) * own_width]
    for w in writes:
        w.wait()


def finish_kernel(count, t, info, later, *refs):
    grads = refs[:count]
    _, updated, buf, sems = refs[count:]
    chunk = grads[0].shape[1]
    writes = []
    for j in range(count):
        buf[j] = later[(t - 1) * count + j] - 0.5 * grads[j][...].astype(jnp.float32)
        at = aligned((info[0] ^ j) * CHUNKS + t, chunk)
        writes.append(pltpu.make_async_copy(buf.at[j], updated.at[:, at], sems.at[j]))
        writes[-1].start()
    for w in writes:
        w.wait()


def step_of(coefficients, measured, ray_voxels, ray_weights, angle_ids, angle_table, harmonics):
    coef_local, cols = coefficients.shape
    projections, _, rays, channels = measured.shape
    rows = projections * rays
    samples = ray_voxels.shape[2]
    count = lax.axis_size("coef")
    me = lax.axis_index("coef")
    half = projections // 2
    block = cols // count
    chunk = block // CHUNKS
    bf16, f32 = jnp.bfloat16, jnp.float32
    shape = jax.ShapeDtypeStruct

    def kernel(body_of, ins, outs, out_shape, scratch=(), grant=12, aliases={}):
        return pl.pallas_call(
            body_of,
            in_specs=ins,
            out_specs=outs,
            out_shape=out_shape,
            scratch_shapes=list(scratch),
            input_output_aliases=aliases,
            compiler_params=pltpu.CompilerParams(vmem_limit_bytes=grant << 20),
        )

    group_bits = 1 if lax.axis_size("groups") % 2 == 0 else 0
    slab_count = lax.axis_size("slab")
    slab_bits = 1 if slab_count % 2 == 0 else 0
    pieces = 1 << (group_bits + slab_bits)
    place = jnp.zeros((), jnp.int32)
    if slab_bits:
        place = place + (lax.axis_index("slab") & 1)
    if group_bits:
        place = place + ((lax.axis_index("groups") & 1) << slab_bits)
    width = harmonics.shape[1] // pieces
    info = jnp.stack([me, me & 1, place]).astype(jnp.int32)
    rows_shape = (rows, samples)
    coef_far, measured_far, vox_far, wgt_far, table_far, harm_far = [
        pltpu.with_memory_space_constraint(v, pltpu.HBM)
        for v in (
            coefficients,
            measured.reshape(projections, rays, channels),
            ray_voxels.reshape(rows_shape),
            ray_weights.reshape(rows_shape),
            angle_table,
            harmonics,
        )
    ]

    *blocks, piece, vox, wgt, chosen = kernel(
        lambda *refs: prepare_kernel(count, *refs),
        [SMEM, SMEM] + [HBM] * 5,
        [VMEM] * (count + 4),
        [shape((coef_local, block), bf16)] * count
        + [
            shape((coef_local, width), bf16),
            shape((rows // 2, samples), jnp.int32),
            shape((rows // 2, samples), jnp.int32),
            shape((projections,) + angle_table.shape[1:], bf16),
        ],
        [pltpu.VMEM((count, coef_local, block), f32), pltpu.SemaphoreType.DMA((count + 3 + projections,))],
    )(info, angle_ids, coef_far, harm_far, vox_far, wgt_far, table_far)

    fetched = {m: [swap(piece, "coef", m)] for m in range(2, count, 2)}
    received = {m: swap(blocks[m], "coef", m) for m in range(2, count)}
    received[0] = blocks[0]
    received[1] = swap(blocks[1], "coef", 1)
    near = swap(harmonics, "coef", 1)
    moves = [(0, 1)] * slab_bits + [(1, 0)] * group_bits + [(1, 1)] * (slab_bits * group_bits)
    for m in fetched:
        for up, along in moves:
            total = lax.axis_size("groups") * slab_count
            pairs = [(i, (((i // slab_count) ^ up) * slab_count) + ((i % slab_count) ^ along)) for i in range(total)]
            fetched[m].append(lax.ppermute(fetched[m][0], ("groups", "slab"), pairs))

    top = kernel(
        build_kernel,
        [VMEM, VMEM],
        VMEM,
        shape((rows // 2, cols), bf16),
        [pltpu.VMEM((GROUP * cols // LANES, LANES), f32)],
    )(vox, wgt)
    low = swap(top, "coef", 1)
    for m in list(fetched):
        fetched[m ^ 1] = [swap(v, "coef", 1) for v in fetched[m]]
    far = [v for m in range(2, count) for v in fetched[m]]

    mine, other = kernel(
        lambda *refs: sums_kernel(count, *refs),
        [SMEM] + [VMEM] * (count + 3) + [HBM],
        [VMEM, VMEM],
        [shape((half, rays, channels), f32)] * 2,
        [pltpu.VMEM((half, rays, channels), f32), pltpu.SemaphoreType.DMA(())],
    )(info, top, low, *blocks, chosen, measured_far)
    total = mine + swap(other, "coef", 1)
    mask = 2
    while mask < count:
        total = total + swap(total, "coef", mask)
        mask *= 2
    waves = kernel(
        lambda *refs: gather_kernel(count, pieces, *refs),
        [SMEM, HBM] + [VMEM] * (1 + len(far)),
        VMEM,
        shape((count * coef_local, harmonics.shape[1]), bf16),
        [pltpu.SemaphoreType.DMA((pieces,))],
    )(info, harm_far, near, *far)

    returned = []
    for t in range(CHUNKS):
        outs = kernel(
            lambda *refs: penalty_kernel(count, pieces, t, *refs),
            [VMEM] * (count + 1),
            [VMEM] * count,
            [shape((coef_local, chunk), bf16)] * count,
            [
                pltpu.VMEM((count * coef_local, chunk), bf16),
                pltpu.VMEM((chunk, count * coef_local), bf16),
                pltpu.VMEM((count * coef_local, chunk), f32),
            ],
        )(waves, *[received[m] for m in range(count)])
        returned.append([outs[0]] + [swap(outs[m], "coef", m) for m in range(1, count)])

    resid_other = swap(total, "coef", 1)
    updated, residual, later = kernel(
        lambda *refs: data_kernel(count, *refs),
        [SMEM] + [VMEM] * 5 + [HBM] + [VMEM] * count,
        [HBM, VMEM, VMEM],
        [
            shape((coef_local, cols), f32),
            shape((projections, rays, channels // count), f32),
            shape(((CHUNKS - 1) * count, coef_local, chunk), f32),
        ],
        [
            pltpu.VMEM((coef_local, rows // 2), bf16),
            pltpu.VMEM((coef_local, rows // 2), bf16),
            pltpu.VMEM((count, coef_local, chunk), f32),
            pltpu.SemaphoreType.DMA((CHUNKS * count,)),
            pltpu.SemaphoreType.DMA((count,)),
        ],
    )(info, total, resid_other, chosen, top, low, coef_far, *returned[0])
    for t in range(1, CHUNKS):
        updated = kernel(
            lambda *refs: finish_kernel(count, t, *refs),
            [SMEM] + [VMEM] * (count + 1) + [HBM],
            HBM,
            shape((coef_local, cols), f32),
            [pltpu.VMEM((count, coef_local, chunk), f32), pltpu.SemaphoreType.DMA((count,))],
            aliases={count + 2: 0},
        )(info, later, *returned[t], updated)
    return (updated, residual[:, None])


def solution(mesh):
    in_specs = (
        P("coef", ("groups", "slab")),
        P("groups", "slab", None, None),
        P(),
        P(),
        P(),
        P(None, "coef", None),
        P("coef", None),
    )
    out_specs = (P("coef", ("groups", "slab")), P("groups", "slab", None, "coef"))
    return jax.shard_map(step_of, mesh=mesh, in_specs=in_specs, out_specs=out_specs, check_vma=False)
```

```python
import jax
import jax.numpy as jnp
from jax import lax
from jax.experimental import pallas as pl
from jax.experimental.pallas import tpu as pltpu
from jax.sharding import PartitionSpec as P


LANES = 128
QUARTERS = (1, 2, 1)
GROUP = 16
NT = (((1,), (1,)), ((), ()))
NN = (((1,), (0,)), ((), ()))
VMEM = pl.BlockSpec(memory_space=pltpu.VMEM)
SMEM = pl.BlockSpec(memory_space=pltpu.SMEM)
HBM = pl.BlockSpec(memory_space=pltpu.HBM)


def dot(a, b, dims):
    return lax.dot_general(a, b, dims, preferred_element_type=jnp.float32)


def swap(value, axis, mask):
    count = lax.axis_size(axis)
    return lax.ppermute(value, axis, [(i, i ^ mask) for i in range(count)])


def aligned(index, width):
    return pl.ds(pl.multiple_of(index * width, width), width)


def cuts_of(block):
    if block % (4 * LANES):
        return [(0, block)]
    unit = block // 4
    starts = [unit * sum(QUARTERS[:t]) for t in range(len(QUARTERS))]
    return [(start, unit * size) for start, size in zip(starts, QUARTERS)]


def columns(index, block, cut):
    return pl.ds(pl.multiple_of(index * block + cut[0], LANES), cut[1])


def prepare_kernel(count, info, ids, coef, vox, wgt, table, *refs):
    blocks, (vox_out, wgt_out, chosen, stage, sems) = refs[:count], refs[count:]
    me, side = info[0], info[1]
    block = blocks[0].shape[1]
    half_rows, projections = vox_out.shape[0], chosen.shape[0]
    half = projections // 2
    order = list(range(2, count)) + [1, 0]
    copies = {}
    for m in order:
        copies[m] = pltpu.make_async_copy(coef.at[:, aligned(me ^ m, block)], stage.at[m], sems.at[m])
    rest = [
        pltpu.make_async_copy(vox.at[aligned(side, half_rows)], vox_out, sems.at[count]),
        pltpu.make_async_copy(wgt.at[aligned(side, half_rows)], wgt_out, sems.at[count + 1]),
    ]
    for i in range(projections):
        a = jnp.where(i < half, side, 1 - side) * half + i % half
        rest.append(pltpu.make_async_copy(table.at[ids[a]], chosen.at[i], sems.at[count + 2 + i]))
    for m in order:
        copies[m].start()
    for c in rest:
        c.start()
    for m in order:
        copies[m].wait()
        blocks[m][...] = stage[m].astype(jnp.bfloat16)
    for c in rest:
        c.wait()


def build_kernel(vox_ref, wgt_ref, matrix_ref, tile_ref):
    rows, samples = vox_ref.shape
    cols = matrix_ref.shape[1]
    high_count = cols // LANES
    low_pos = lax.broadcasted_iota(jnp.int32, (LANES, samples), 0)
    high_pos = lax.broadcasted_iota(jnp.int32, (high_count, samples), 0)

    def build(step, carry):
        first = pl.multiple_of(step * GROUP, GROUP)
        vox = vox_ref[pl.ds(first, GROUP), :]
        wgt = wgt_ref[pl.ds(first, GROUP), :].astype(jnp.float32) * (1.0 / 256.0)
        low = vox & (LANES - 1)
        high = lax.shift_right_logical(vox, LANES.bit_length() - 1)
        for i in range(GROUP):
            low_hot = (low_pos == low[i:i + 1]).astype(jnp.float32).astype(jnp.bfloat16)
            high_hot = jnp.where(high_pos == high[i:i + 1], wgt[i:i + 1], 0.0).astype(jnp.bfloat16)
            tile_ref[i * high_count:(i + 1) * high_count, :] = dot(high_hot, low_hot, NT)
        for h in range(high_count):
            part = tile_ref[pl.ds(h, GROUP, stride=high_count), :]
            matrix_ref[pl.ds(first, GROUP), h * LANES:(h + 1) * LANES] = part.astype(jnp.bfloat16)
        return carry

    lax.fori_loop(0, rows // GROUP, build, 0)


def sums_kernel(count, info, top_ref, low_ref, *refs):
    blocks = refs[:count]
    chosen, measured, mine_ref, other_ref, target, sem = refs[count:]
    half, rays = mine_ref.shape[:2]
    block = blocks[0].shape[1]
    me, side = info[0], info[1]
    fetch = pltpu.make_async_copy(measured.at[pl.ds(side * half, half)], target, sem)
    fetch.start()
    for out_ref, ref, start in ((other_ref, low_ref, half), (mine_ref, top_ref, 0)):
        sums = jnp.zeros((ref.shape[0], blocks[0].shape[0]), jnp.float32)
        for j in range(count):
            sums += dot(ref[:, aligned(me ^ j, block)], blocks[j][...], NT)
        sums = sums.astype(jnp.bfloat16)
        for i in range(half):
            out_ref[i] = dot(sums[i * rays:(i + 1) * rays], chosen[start + i], NN)
    fetch.wait()
    mine_ref[...] = mine_ref[...] - (2.0 / count) * target[...]


def gather_kernel(count, pieces, info, own, near, *refs):
    far, (out, sems) = refs[:-2], refs[-2:]
    place = info[2]
    height = own.shape[0]
    width = own.shape[1] // pieces
    copies = []
    for r in range(pieces):
        spot = out.at[0:height, r * width:(r + 1) * width]
        copies.append(pltpu.make_async_copy(own.at[:, aligned(place ^ r, width)], spot, sems.at[r]))
    for c in copies:
        c.start()
    for r in range(pieces):
        out[height:2 * height, r * width:(r + 1) * width] = near[:, aligned(place ^ r, width)]
        for j in range(count - 2):
            out[(j + 2) * height:(j + 3) * height, r * width:(r + 1) * width] = far[j * pieces + r][...]
    for c in copies:
        c.wait()


def penalty_kernel(count, pieces, cut, waves, *refs):
    blocks, outs = refs[:count], refs[count:2 * count]
    stack, turned, acc = refs[2 * count:]
    height = outs[0].shape[0]
    width = waves.shape[1] // pieces
    for j in range(count):
        stack[j * height:(j + 1) * height, :] = blocks[j][:, cut[0]:cut[0] + cut[1]]
    turned[...] = jnp.swapaxes(stack[...], 0, 1)
    for r in range(pieces):
        wave = waves[:, r * width:(r + 1) * width]
        field = dot(turned[...], wave, NN)
        slope = (0.5 * jnp.tanh(0.5 * field) - 0.5).astype(jnp.bfloat16)
        part = dot(wave, slope, NT)
        if r > 0:
            part += acc[...]
        if r < pieces - 1:
            acc[...] = part
        else:
            for j in range(count):
                outs[j][...] = part[j * height:(j + 1) * height].astype(outs[j].dtype)


def data_kernel(count, cuts, info, mine_ref, other_ref, chosen, top_ref, low_ref, coef, *refs):
    grads, later = refs[:count], refs[count + 2:count + 1 + len(cuts)]
    updated, residual_ref = refs[count:count + 2]
    back_a, back_b, buf, sems, out_sems = refs[count + 1 + len(cuts):]
    me, side = info[0], info[1]
    half, rays = mine_ref.shape[:2]
    block = coef.shape[1] // count
    own_width = residual_ref.shape[2]
    order = [(t, j) for t in range(len(cuts)) for j in range(count)]
    copies = {}
    for n, (t, j) in enumerate(order):
        spot = (buf if t == 0 else later[t - 1]).at[j]
        copies[t, j] = pltpu.make_async_copy(coef.at[:, columns(me ^ j, block, cuts[t])], spot, sems.at[n])
        copies[t, j].start()
    for back, ref, start in ((back_a, mine_ref, 0), (back_b, other_ref, half)):
        for i in range(half):
            part = dot(chosen[start + i], ref[i].astype(jnp.bfloat16), NT)
            back[:, i * rays:(i + 1) * rays] = part.astype(jnp.bfloat16)
    writes = []
    for t, j in order:
        at = columns(me ^ j, block, cuts[t])
        grad = dot(back_a[...], top_ref[:, at], NN) + dot(back_b[...], low_ref[:, at], NN)
        copies[t, j].wait()
        if t == 0:
            buf[j] = buf[j] - 0.5 * grad - 0.5 * grads[j][...].astype(jnp.float32)
            writes.append(pltpu.make_async_copy(buf.at[j], updated.at[:, at], out_sems.at[j]))
            writes[-1].start()
        else:
            later[t - 1][j] = later[t - 1][j] - 0.5 * grad
    for q in range(count):
        @pl.when(me == q)
        def _():
            for i in range(half):
                residual_ref[side * half + i] = mine_ref[i, :, q * own_width:(q + 1) * own_width]
                residual_ref[(1 - side) * half + i] = other_ref[i, :, q * own_width:(q + 1) * own_width]
    for w in writes:
        w.wait()


def finish_kernel(count, cut, info, later, *refs):
    grads = refs[:count]
    _, updated, buf, sems = refs[count:]
    block = updated.shape[1] // count
    writes = []
    for j in range(count):
        buf[j] = later[j] - 0.5 * grads[j][...].astype(jnp.float32)
        at = columns(info[0] ^ j, block, cut)
        writes.append(pltpu.make_async_copy(buf.at[j], updated.at[:, at], sems.at[j]))
        writes[-1].start()
    for w in writes:
        w.wait()


def step_of(coefficients, measured, ray_voxels, ray_weights, angle_ids, angle_table, harmonics):
    coef_local, cols = coefficients.shape
    projections, _, rays, channels = measured.shape
    rows = projections * rays
    samples = ray_voxels.shape[2]
    count = lax.axis_size("coef")
    me = lax.axis_index("coef")
    half = projections // 2
    block = cols // count
    cuts = cuts_of(block)
    bf16, f32 = jnp.bfloat16, jnp.float32
    shape = jax.ShapeDtypeStruct

    def kernel(body_of, ins, outs, out_shape, scratch=(), grant=12, aliases={}):
        return pl.pallas_call(
            body_of,
            in_specs=ins,
            out_specs=outs,
            out_shape=out_shape,
            scratch_shapes=list(scratch),
            input_output_aliases=aliases,
            compiler_params=pltpu.CompilerParams(vmem_limit_bytes=grant << 20),
        )

    group_bits = 1 if lax.axis_size("groups") % 2 == 0 else 0
    slab_count = lax.axis_size("slab")
    slab_bits = 1 if slab_count % 2 == 0 else 0
    pieces = 1 << (group_bits + slab_bits)
    place = jnp.zeros((), jnp.int32)
    if slab_bits:
        place = place + (lax.axis_index("slab") & 1)
    if group_bits:
        place = place + ((lax.axis_index("groups") & 1) << slab_bits)
    width = harmonics.shape[1] // pieces
    info = jnp.stack([me, me & 1, place]).astype(jnp.int32)
    rows_shape = (rows, samples)
    coef_far, measured_far, vox_far, wgt_far, ids_far, table_far, harm_far = [
        pltpu.with_memory_space_constraint(v, pltpu.HBM)
        for v in (
            coefficients,
            measured.reshape(projections, rays, channels),
            ray_voxels.reshape(rows_shape),
            ray_weights.reshape(rows_shape),
            angle_ids,
            angle_table,
            harmonics,
        )
    ]

    piece = lax.dynamic_slice_in_dim(harmonics, place * width, width, 1)
    fetched = {m: [swap(piece, "coef", m)] for m in range(2, count, 2)}
    *blocks, vox, wgt, chosen = kernel(
        lambda *refs: prepare_kernel(count, *refs),
        [SMEM, SMEM] + [HBM] * 4,
        [VMEM] * (count + 3),
        [shape((coef_local, block), bf16)] * count
        + [
            shape((rows // 2, samples), jnp.int32),
            shape((rows // 2, samples), jnp.int32),
            shape((projections,) + angle_table.shape[1:], bf16),
        ],
        [pltpu.VMEM((count, coef_local, block), f32), pltpu.SemaphoreType.DMA((count + 2 + projections,))],
    )(info, ids_far, coef_far, vox_far, wgt_far, table_far)

    received = {m: swap(blocks[m], "coef", m) for m in range(2, count)}
    received[0] = blocks[0]
    received[1] = swap(blocks[1], "coef", 1)
    near = swap(harmonics, "coef", 1)
    moves = [(0, 1)] * slab_bits + [(1, 0)] * group_bits + [(1, 1)] * (slab_bits * group_bits)
    for m in fetched:
        for up, along in moves:
            total = lax.axis_size("groups") * slab_count
            pairs = [(i, (((i // slab_count) ^ up) * slab_count) + ((i % slab_count) ^ along)) for i in range(total)]
            fetched[m].append(lax.ppermute(fetched[m][0], ("groups", "slab"), pairs))

    top = kernel(
        build_kernel,
        [VMEM, VMEM],
        VMEM,
        shape((rows // 2, cols), bf16),
        [pltpu.VMEM((GROUP * cols // LANES, LANES), f32)],
    )(vox, wgt)
    low = swap(top, "coef", 1)
    for m in list(fetched):
        fetched[m ^ 1] = [swap(v, "coef", 1) for v in fetched[m]]
    far = [v for m in range(2, count) for v in fetched[m]]

    mine, other = kernel(
        lambda *refs: sums_kernel(count, *refs),
        [SMEM] + [VMEM] * (count + 3) + [HBM],
        [VMEM, VMEM],
        [shape((half, rays, channels), f32)] * 2,
        [pltpu.VMEM((half, rays, channels), f32), pltpu.SemaphoreType.DMA(())],
    )(info, top, low, *blocks, chosen, measured_far)
    total = mine + swap(other, "coef", 1)
    mask = 2
    while mask < count:
        total = total + swap(total, "coef", mask)
        mask *= 2
    waves = kernel(
        lambda *refs: gather_kernel(count, pieces, *refs),
        [SMEM, HBM] + [VMEM] * (1 + len(far)),
        VMEM,
        shape((count * coef_local, harmonics.shape[1]), bf16),
        [pltpu.SemaphoreType.DMA((pieces,))],
    )(info, harm_far, near, *far)

    returned = []
    for cut in cuts:
        chunk = cut[1]
        outs = kernel(
            lambda *refs: penalty_kernel(count, pieces, cut, *refs),
            [VMEM] * (count + 1),
            [VMEM] * count,
            [shape((coef_local, chunk), bf16)] * count,
            [
                pltpu.VMEM((count * coef_local, chunk), bf16),
                pltpu.VMEM((chunk, count * coef_local), bf16),
                pltpu.VMEM((count * coef_local, chunk), f32),
            ],
        )(waves, *[received[m] for m in range(count)])
        returned.append([outs[0]] + [swap(outs[m], "coef", m) for m in range(1, count)])

    resid_other = swap(total, "coef", 1)
    updated, residual, *later = kernel(
        lambda *refs: data_kernel(count, cuts, *refs),
        [SMEM] + [VMEM] * 5 + [HBM] + [VMEM] * count,
        [HBM] + [VMEM] * len(cuts),
        [shape((coef_local, cols), f32), shape((projections, rays, channels // count), f32)]
        + [shape((count, coef_local, cut[1]), f32) for cut in cuts[1:]],
        [
            pltpu.VMEM((coef_local, rows // 2), bf16),
            pltpu.VMEM((coef_local, rows // 2), bf16),
            pltpu.VMEM((count, coef_local, cuts[0][1]), f32),
            pltpu.SemaphoreType.DMA((len(cuts) * count,)),
            pltpu.SemaphoreType.DMA((count,)),
        ],
    )(info, total, resid_other, chosen, top, low, coef_far, *returned[0])
    for t, cut in list(enumerate(cuts))[1:]:
        updated = kernel(
            lambda *refs: finish_kernel(count, cut, *refs),
            [SMEM] + [VMEM] * (count + 1) + [HBM],
            HBM,
            shape((coef_local, cols), f32),
            [pltpu.VMEM((count, coef_local, cut[1]), f32), pltpu.SemaphoreType.DMA((count,))],
            aliases={count + 2: 0},
        )(info, later[t - 1], *returned[t], updated)
    return (updated, residual[:, None])


def solution(mesh):
    in_specs = (
        P("coef", ("groups", "slab")),
        P("groups", "slab", None, None),
        P(),
        P(),
        P(),
        P(None, "coef", None),
        P("coef", None),
    )
    out_specs = (P("coef", ("groups", "slab")), P("groups", "slab", None, "coef"))
    return jax.shard_map(step_of, mesh=mesh, in_specs=in_specs, out_specs=out_specs, check_vma=False)
```

```python
import jax
import jax.numpy as jnp
from jax import lax
from jax.experimental import pallas as pl
from jax.experimental.pallas import tpu as pltpu
from jax.sharding import PartitionSpec as P


LANES = 128
QUARTERS = (2, 2)
GROUP = 32
NT = (((1,), (1,)), ((), ()))
NN = (((1,), (0,)), ((), ()))
VMEM = pl.BlockSpec(memory_space=pltpu.VMEM)
SMEM = pl.BlockSpec(memory_space=pltpu.SMEM)
HBM = pl.BlockSpec(memory_space=pltpu.HBM)


def dot(a, b, dims):
    return lax.dot_general(a, b, dims, preferred_element_type=jnp.float32)


def swap(value, axis, mask):
    count = lax.axis_size(axis)
    return lax.ppermute(value, axis, [(i, i ^ mask) for i in range(count)])


def aligned(index, width):
    return pl.ds(pl.multiple_of(index * width, width), width)


def cuts_of(block):
    if block % (4 * LANES):
        return [(0, block)]
    unit = block // 4
    starts = [unit * sum(QUARTERS[:t]) for t in range(len(QUARTERS))]
    return [(start, unit * size) for start, size in zip(starts, QUARTERS)]


def columns(index, block, cut):
    return pl.ds(pl.multiple_of(index * block + cut[0], LANES), cut[1])


def prepare_kernel(count, info, ids, coef, vox, wgt, table, *refs):
    blocks, (vox_out, wgt_out, chosen, stage, sems) = refs[:count], refs[count:]
    me, side = info[0], info[1]
    block = blocks[0].shape[1]
    half_rows, projections = vox_out.shape[0], chosen.shape[0]
    half = projections // 2
    order = list(range(2, count)) + [1, 0]
    copies = {}
    for m in order:
        copies[m] = pltpu.make_async_copy(coef.at[:, aligned(me ^ m, block)], stage.at[m], sems.at[m])
    rest = [
        pltpu.make_async_copy(vox.at[aligned(side, half_rows)], vox_out, sems.at[count]),
        pltpu.make_async_copy(wgt.at[aligned(side, half_rows)], wgt_out, sems.at[count + 1]),
    ]
    for i in range(projections):
        a = jnp.where(i < half, side, 1 - side) * half + i % half
        rest.append(pltpu.make_async_copy(table.at[ids[a]], chosen.at[i], sems.at[count + 2 + i]))
    for m in order:
        copies[m].start()
    for c in rest:
        c.start()
    for m in order:
        copies[m].wait()
        blocks[m][...] = stage[m].astype(jnp.bfloat16)
    for c in rest:
        c.wait()


def build_kernel(vox_ref, wgt_ref, matrix_ref, tile_ref):
    rows, samples = vox_ref.shape
    cols = matrix_ref.shape[1]
    high_count = cols // LANES
    low_pos = lax.broadcasted_iota(jnp.int32, (LANES, samples), 0)
    high_pos = lax.broadcasted_iota(jnp.int32, (high_count, samples), 0)
    blank = jnp.zeros((high_count, samples), jnp.bfloat16)

    def build(step, carry):
        first = pl.multiple_of(step * GROUP, GROUP)
        vox = vox_ref[pl.ds(first, GROUP), :]
        wgt = wgt_ref[pl.ds(first, GROUP), :].astype(jnp.float32) * (1.0 / 256.0)
        low = vox & (LANES - 1)
        high = lax.shift_right_logical(vox, LANES.bit_length() - 1)
        hots = []
        for i in range(GROUP):
            low_hot = (low_pos == low[i:i + 1]).astype(jnp.float32).astype(jnp.bfloat16)
            high_hot = jnp.where(high_pos == high[i:i + 1], wgt[i:i + 1], 0.0).astype(jnp.bfloat16)
            hots.append((low_hot, high_hot))
        for i in range(0, GROUP, 2):
            (low_a, high_a), (low_b, high_b) = hots[i:i + 2]
            left = jnp.concatenate([jnp.concatenate([high_a, blank], 1), jnp.concatenate([blank, high_b], 1)], 0)
            right = jnp.concatenate([low_a, low_b], 1)
            tile_ref[i * high_count:(i + 2) * high_count, :] = dot(left, right, NT)
        for h in range(high_count):
            part = tile_ref[pl.ds(h, GROUP, stride=high_count), :]
            matrix_ref[pl.ds(first, GROUP), h * LANES:(h + 1) * LANES] = part.astype(jnp.bfloat16)
        return carry

    lax.fori_loop(0, rows // GROUP, build, 0)


def sums_kernel(count, info, top_ref, low_ref, *refs):
    blocks = refs[:count]
    chosen, measured, mine_ref, other_ref, target, sem = refs[count:]
    half, rays = mine_ref.shape[:2]
    block = blocks[0].shape[1]
    me, side = info[0], info[1]
    fetch = pltpu.make_async_copy(measured.at[pl.ds(side * half, half)], target, sem)
    fetch.start()
    for out_ref, ref, start in ((other_ref, low_ref, half), (mine_ref, top_ref, 0)):
        sums = jnp.zeros((ref.shape[0], blocks[0].shape[0]), jnp.float32)
        for j in range(count):
            sums += dot(ref[:, aligned(me ^ j, block)], blocks[j][...], NT)
        sums = sums.astype(jnp.bfloat16)
        for i in range(half):
            out_ref[i] = dot(sums[i * rays:(i + 1) * rays], chosen[start + i], NN)
    fetch.wait()
    mine_ref[...] = mine_ref[...] - (2.0 / count) * target[...]


def gather_kernel(count, pieces, info, own, near, *refs):
    far, (out, sems) = refs[:-2], refs[-2:]
    place = info[2]
    height = own.shape[0]
    width = own.shape[1] // pieces
    copies = []
    for r in range(pieces):
        spot = out.at[0:height, r * width:(r + 1) * width]
        copies.append(pltpu.make_async_copy(own.at[:, aligned(place ^ r, width)], spot, sems.at[r]))
    for c in copies:
        c.start()
    for r in range(pieces):
        out[height:2 * height, r * width:(r + 1) * width] = near[:, aligned(place ^ r, width)]
        for j in range(count - 2):
            out[(j + 2) * height:(j + 3) * height, r * width:(r + 1) * width] = far[j * pieces + r][...]
    for c in copies:
        c.wait()


def penalty_kernel(count, pieces, cut, waves, *refs):
    blocks, outs = refs[:count], refs[count:2 * count]
    stack, turned, acc = refs[2 * count:]
    height = outs[0].shape[0]
    width = waves.shape[1] // pieces
    for j in range(count):
        stack[j * height:(j + 1) * height, :] = blocks[j][:, cut[0]:cut[0] + cut[1]]
    turned[...] = jnp.swapaxes(stack[...], 0, 1)
    for r in range(pieces):
        wave = waves[:, r * width:(r + 1) * width]
        field = dot(turned[...], wave, NN)
        slope = (0.5 * jnp.tanh(0.5 * field) - 0.5).astype(jnp.bfloat16)
        part = dot(wave, slope, NT)
        if r > 0:
            part += acc[...]
        if r < pieces - 1:
            acc[...] = part
        else:
            for j in range(count):
                outs[j][...] = part[j * height:(j + 1) * height].astype(outs[j].dtype)


def data_kernel(count, cuts, info, mine_ref, other_ref, chosen, top_ref, low_ref, coef, *refs):
    grads, later = refs[:count], refs[count + 2:count + 1 + len(cuts)]
    updated, residual_ref = refs[count:count + 2]
    back_a, back_b, buf, sems, out_sems = refs[count + 1 + len(cuts):]
    me, side = info[0], info[1]
    half, rays = mine_ref.shape[:2]
    block = coef.shape[1] // count
    own_width = residual_ref.shape[2]
    order = [(t, j) for t in range(len(cuts)) for j in range(count)]
    copies = {}
    for n, (t, j) in enumerate(order):
        spot = (buf if t == 0 else later[t - 1]).at[j]
        copies[t, j] = pltpu.make_async_copy(coef.at[:, columns(me ^ j, block, cuts[t])], spot, sems.at[n])
        copies[t, j].start()
    for back, ref, start in ((back_a, mine_ref, 0), (back_b, other_ref, half)):
        for i in range(half):
            part = dot(chosen[start + i], ref[i].astype(jnp.bfloat16), NT)
            back[:, i * rays:(i + 1) * rays] = part.astype(jnp.bfloat16)
    writes = []
    for t, j in order:
        at = columns(me ^ j, block, cuts[t])
        grad = dot(back_a[...], top_ref[:, at], NN) + dot(back_b[...], low_ref[:, at], NN)
        copies[t, j].wait()
        if t == 0:
            buf[j] = buf[j] - 0.5 * grad - 0.5 * grads[j][...].astype(jnp.float32)
            writes.append(pltpu.make_async_copy(buf.at[j], updated.at[:, at], out_sems.at[j]))
            writes[-1].start()
        else:
            later[t - 1][j] = later[t - 1][j] - 0.5 * grad
    for q in range(count):
        @pl.when(me == q)
        def _():
            for i in range(half):
                residual_ref[side * half + i] = mine_ref[i, :, q * own_width:(q + 1) * own_width]
                residual_ref[(1 - side) * half + i] = other_ref[i, :, q * own_width:(q + 1) * own_width]
    for w in writes:
        w.wait()


def finish_kernel(count, cut, info, later, *refs):
    grads = refs[:count]
    _, updated, buf, sems = refs[count:]
    block = updated.shape[1] // count
    writes = []
    for j in range(count):
        buf[j] = later[j] - 0.5 * grads[j][...].astype(jnp.float32)
        at = columns(info[0] ^ j, block, cut)
        writes.append(pltpu.make_async_copy(buf.at[j], updated.at[:, at], sems.at[j]))
        writes[-1].start()
    for w in writes:
        w.wait()


def step_of(coefficients, measured, ray_voxels, ray_weights, angle_ids, angle_table, harmonics):
    coef_local, cols = coefficients.shape
    projections, _, rays, channels = measured.shape
    rows = projections * rays
    samples = ray_voxels.shape[2]
    count = lax.axis_size("coef")
    me = lax.axis_index("coef")
    half = projections // 2
    block = cols // count
    cuts = cuts_of(block)
    bf16, f32 = jnp.bfloat16, jnp.float32
    shape = jax.ShapeDtypeStruct

    def kernel(body_of, ins, outs, out_shape, scratch=(), grant=12, aliases={}):
        return pl.pallas_call(
            body_of,
            in_specs=ins,
            out_specs=outs,
            out_shape=out_shape,
            scratch_shapes=list(scratch),
            input_output_aliases=aliases,
            compiler_params=pltpu.CompilerParams(vmem_limit_bytes=grant << 20),
        )

    group_bits = 1 if lax.axis_size("groups") % 2 == 0 else 0
    slab_count = lax.axis_size("slab")
    slab_bits = 1 if slab_count % 2 == 0 else 0
    pieces = 1 << (group_bits + slab_bits)
    place = jnp.zeros((), jnp.int32)
    if slab_bits:
        place = place + (lax.axis_index("slab") & 1)
    if group_bits:
        place = place + ((lax.axis_index("groups") & 1) << slab_bits)
    width = harmonics.shape[1] // pieces
    info = jnp.stack([me, me & 1, place]).astype(jnp.int32)
    rows_shape = (rows, samples)
    coef_far, measured_far, vox_far, wgt_far, ids_far, table_far, harm_far = [
        pltpu.with_memory_space_constraint(v, pltpu.HBM)
        for v in (
            coefficients,
            measured.reshape(projections, rays, channels),
            ray_voxels.reshape(rows_shape),
            ray_weights.reshape(rows_shape),
            angle_ids,
            angle_table,
            harmonics,
        )
    ]

    piece = lax.dynamic_slice_in_dim(harmonics, place * width, width, 1)
    fetched = {m: [swap(piece, "coef", m)] for m in range(2, count, 2)}
    *blocks, vox, wgt, chosen = kernel(
        lambda *refs: prepare_kernel(count, *refs),
        [SMEM, SMEM] + [HBM] * 4,
        [VMEM] * (count + 3),
        [shape((coef_local, block), bf16)] * count
        + [
            shape((rows // 2, samples), jnp.int32),
            shape((rows // 2, samples), jnp.int32),
            shape((projections,) + angle_table.shape[1:], bf16),
        ],
        [pltpu.VMEM((count, coef_local, block), f32), pltpu.SemaphoreType.DMA((count + 2 + projections,))],
    )(info, ids_far, coef_far, vox_far, wgt_far, table_far)

    received = {m: swap(blocks[m], "coef", m) for m in range(2, count)}
    received[0] = blocks[0]
    received[1] = swap(blocks[1], "coef", 1)
    near = swap(harmonics, "coef", 1)
    moves = [(0, 1)] * slab_bits + [(1, 0)] * group_bits + [(1, 1)] * (slab_bits * group_bits)
    for m in fetched:
        for up, along in moves:
            total = lax.axis_size("groups") * slab_count
            pairs = [(i, (((i // slab_count) ^ up) * slab_count) + ((i % slab_count) ^ along)) for i in range(total)]
            fetched[m].append(lax.ppermute(fetched[m][0], ("groups", "slab"), pairs))

    top = kernel(
        build_kernel,
        [VMEM, VMEM],
        VMEM,
        shape((rows // 2, cols), bf16),
        [pltpu.VMEM((GROUP * cols // LANES, LANES), f32)],
    )(vox, wgt)
    low = swap(top, "coef", 1)
    for m in list(fetched):
        fetched[m ^ 1] = [swap(v, "coef", 1) for v in fetched[m]]
    far = [v for m in range(2, count) for v in fetched[m]]

    mine, other = kernel(
        lambda *refs: sums_kernel(count, *refs),
        [SMEM] + [VMEM] * (count + 3) + [HBM],
        [VMEM, VMEM],
        [shape((half, rays, channels), f32)] * 2,
        [pltpu.VMEM((half, rays, channels), f32), pltpu.SemaphoreType.DMA(())],
    )(info, top, low, *blocks, chosen, measured_far)
    total = mine + swap(other, "coef", 1)
    mask = 2
    while mask < count:
        total = total + swap(total, "coef", mask)
        mask *= 2
    waves = kernel(
        lambda *refs: gather_kernel(count, pieces, *refs),
        [SMEM, HBM] + [VMEM] * (1 + len(far)),
        VMEM,
        shape((count * coef_local, harmonics.shape[1]), bf16),
        [pltpu.SemaphoreType.DMA((pieces,))],
    )(info, harm_far, near, *far)

    returned = []
    for cut in cuts:
        chunk = cut[1]
        outs = kernel(
            lambda *refs: penalty_kernel(count, pieces, cut, *refs),
            [VMEM] * (count + 1),
            [VMEM] * count,
            [shape((coef_local, chunk), bf16)] * count,
            [
                pltpu.VMEM((count * coef_local, chunk), bf16),
                pltpu.VMEM((chunk, count * coef_local), bf16),
                pltpu.VMEM((count * coef_local, chunk), f32),
            ],
        )(waves, *[received[m] for m in range(count)])
        returned.append([outs[0]] + [swap(outs[m], "coef", m) for m in range(1, count)])

    resid_other = swap(total, "coef", 1)
    updated, residual, *later = kernel(
        lambda *refs: data_kernel(count, cuts, *refs),
        [SMEM] + [VMEM] * 5 + [HBM] + [VMEM] * count,
        [HBM] + [VMEM] * len(cuts),
        [shape((coef_local, cols), f32), shape((projections, rays, channels // count), f32)]
        + [shape((count, coef_local, cut[1]), f32) for cut in cuts[1:]],
        [
            pltpu.VMEM((coef_local, rows // 2), bf16),
            pltpu.VMEM((coef_local, rows // 2), bf16),
            pltpu.VMEM((count, coef_local, cuts[0][1]), f32),
            pltpu.SemaphoreType.DMA((len(cuts) * count,)),
            pltpu.SemaphoreType.DMA((count,)),
        ],
    )(info, total, resid_other, chosen, top, low, coef_far, *returned[0])
    for t, cut in list(enumerate(cuts))[1:]:
        updated = kernel(
            lambda *refs: finish_kernel(count, cut, *refs),
            [SMEM] + [VMEM] * (count + 1) + [HBM],
            HBM,
            shape((coef_local, cols), f32),
            [pltpu.VMEM((count, coef_local, cut[1]), f32), pltpu.SemaphoreType.DMA((count,))],
            aliases={count + 2: 0},
        )(info, later[t - 1], *returned[t], updated)
    return (updated, residual[:, None])


def solution(mesh):
    in_specs = (
        P("coef", ("groups", "slab")),
        P("groups", "slab", None, None),
        P(),
        P(),
        P(),
        P(None, "coef", None),
        P("coef", None),
    )
    out_specs = (P("coef", ("groups", "slab")), P("groups", "slab", None, "coef"))
    return jax.shard_map(step_of, mesh=mesh, in_specs=in_specs, out_specs=out_specs, check_vma=False)
```

```python
import jax
import jax.numpy as jnp
from jax import lax
from jax.experimental import pallas as pl
from jax.experimental.pallas import tpu as pltpu
from jax.sharding import PartitionSpec as P


LANES = 128
QUARTERS = (2, 2)
GROUP = 32
NT = (((1,), (1,)), ((), ()))
NN = (((1,), (0,)), ((), ()))
VMEM = pl.BlockSpec(memory_space=pltpu.VMEM)
SMEM = pl.BlockSpec(memory_space=pltpu.SMEM)
HBM = pl.BlockSpec(memory_space=pltpu.HBM)


def dot(a, b, dims):
    return lax.dot_general(a, b, dims, preferred_element_type=jnp.float32)


def swap(value, axis, mask):
    count = lax.axis_size(axis)
    return lax.ppermute(value, axis, [(i, i ^ mask) for i in range(count)])


def aligned(index, width):
    return pl.ds(pl.multiple_of(index * width, width), width)


def cuts_of(block):
    if block % (4 * LANES):
        return [(0, block)]
    unit = block // 4
    starts = [unit * sum(QUARTERS[:t]) for t in range(len(QUARTERS))]
    return [(start, unit * size) for start, size in zip(starts, QUARTERS)]


def columns(index, block, cut):
    return pl.ds(pl.multiple_of(index * block + cut[0], LANES), cut[1])


def prepare_kernel(count, info, ids, coef, vox, wgt, table, *refs):
    blocks, (vox_out, wgt_out, chosen, stage, sems) = refs[:count], refs[count:]
    me, side = info[0], info[1]
    block = blocks[0].shape[1]
    half_rows, projections = vox_out.shape[0], chosen.shape[0]
    half = projections // 2
    order = list(range(2, count)) + [1, 0]
    copies = {}
    for m in order:
        copies[m] = pltpu.make_async_copy(coef.at[:, aligned(me ^ m, block)], stage.at[m], sems.at[m])
    rest = [
        pltpu.make_async_copy(vox.at[aligned(side, half_rows)], vox_out, sems.at[count]),
        pltpu.make_async_copy(wgt.at[aligned(side, half_rows)], wgt_out, sems.at[count + 1]),
    ]
    for i in range(projections):
        a = jnp.where(i < half, side, 1 - side) * half + i % half
        rest.append(pltpu.make_async_copy(table.at[ids[a]], chosen.at[i], sems.at[count + 2 + i]))
    for m in order:
        copies[m].start()
    for c in rest:
        c.start()
    for m in order:
        copies[m].wait()
        blocks[m][...] = stage[m].astype(jnp.bfloat16)
    for c in rest:
        c.wait()


def build_kernel(vox_ref, wgt_ref, matrix_ref, tile_ref):
    rows, samples = vox_ref.shape
    cols = matrix_ref.shape[1]
    high_count = cols // LANES
    low_pos = lax.broadcasted_iota(jnp.int32, (LANES, samples), 0)
    high_pos = lax.broadcasted_iota(jnp.int32, (high_count, samples), 0)
    blank = jnp.zeros((high_count, samples), jnp.bfloat16)

    def build(step, carry):
        first = pl.multiple_of(step * GROUP, GROUP)
        vox = vox_ref[pl.ds(first, GROUP), :]
        wgt = wgt_ref[pl.ds(first, GROUP), :].astype(jnp.float32) * (1.0 / 256.0)
        low = vox & (LANES - 1)
        high = lax.shift_right_logical(vox, LANES.bit_length() - 1)
        hots = []
        for i in range(GROUP):
            low_hot = (low_pos == low[i:i + 1]).astype(jnp.float32).astype(jnp.bfloat16)
            high_hot = jnp.where(high_pos == high[i:i + 1], wgt[i:i + 1], 0.0).astype(jnp.bfloat16)
            hots.append((low_hot, high_hot))
        for i in range(0, GROUP, 2):
            (low_a, high_a), (low_b, high_b) = hots[i:i + 2]
            left = jnp.concatenate([jnp.concatenate([high_a, blank], 1), jnp.concatenate([blank, high_b], 1)], 0)
            right = jnp.concatenate([low_a, low_b], 1)
            tile_ref[i * high_count:(i + 2) * high_count, :] = dot(left, right, NT)
        for h in range(high_count):
            part = tile_ref[pl.ds(h, GROUP, stride=high_count), :]
            matrix_ref[pl.ds(first, GROUP), h * LANES:(h + 1) * LANES] = part.astype(jnp.bfloat16)
        return carry

    lax.fori_loop(0, rows // GROUP, build, 0)


def sums_kernel(count, own, info, matrix_ref, *refs):
    blocks = refs[:count]
    chosen, measured, out_ref, target, sem = refs[count:]
    half, rays = out_ref.shape[:2]
    block = blocks[0].shape[1]
    me, side = info[0], info[1]
    if own:
        fetch = pltpu.make_async_copy(measured.at[pl.ds(side * half, half)], target, sem)
        fetch.start()
    sums = jnp.zeros((matrix_ref.shape[0], blocks[0].shape[0]), jnp.float32)
    for j in range(count):
        sums += dot(matrix_ref[:, aligned(me ^ j, block)], blocks[j][...], NT)
    sums = sums.astype(jnp.bfloat16)
    for i in range(half):
        out_ref[i] = dot(sums[i * rays:(i + 1) * rays], chosen[i + (0 if own else half)], NN)
    if own:
        fetch.wait()
        out_ref[...] = out_ref[...] - (2.0 / count) * target[...]


def gather_kernel(count, pieces, info, own, near, *refs):
    far, (out, sems) = refs[:-2], refs[-2:]
    place = info[2]
    height = own.shape[0]
    width = own.shape[1] // pieces
    copies = []
    for r in range(pieces):
        spot = out.at[0:height, r * width:(r + 1) * width]
        copies.append(pltpu.make_async_copy(own.at[:, aligned(place ^ r, width)], spot, sems.at[r]))
    for c in copies:
        c.start()
    for r in range(pieces):
        out[height:2 * height, r * width:(r + 1) * width] = near[:, aligned(place ^ r, width)]
        for j in range(count - 2):
            out[(j + 2) * height:(j + 3) * height, r * width:(r + 1) * width] = far[j * pieces + r][...]
    for c in copies:
        c.wait()


def penalty_kernel(count, pieces, cut, waves, *refs):
    blocks, outs = refs[:count], refs[count:2 * count]
    stack, turned, acc = refs[2 * count:]
    height = outs[0].shape[0]
    width = waves.shape[1] // pieces
    for j in range(count):
        stack[j * height:(j + 1) * height, :] = blocks[j][:, cut[0]:cut[0] + cut[1]]
    turned[...] = jnp.swapaxes(stack[...], 0, 1)
    for r in range(pieces):
        wave = waves[:, r * width:(r + 1) * width]
        field = dot(turned[...], wave, NN)
        slope = (0.5 * jnp.tanh(0.5 * field) - 0.5).astype(jnp.bfloat16)
        part = dot(wave, slope, NT)
        if r > 0:
            part += acc[...]
        if r < pieces - 1:
            acc[...] = part
        else:
            for j in range(count):
                outs[j][...] = part[j * height:(j + 1) * height].astype(outs[j].dtype)


def data_kernel(count, cuts, info, mine_ref, other_ref, chosen, top_ref, low_ref, coef, *refs):
    grads, later = refs[:count], refs[count + 2:count + 1 + len(cuts)]
    updated, residual_ref = refs[count:count + 2]
    back_a, back_b, buf, sems, out_sems = refs[count + 1 + len(cuts):]
    me, side = info[0], info[1]
    half, rays = mine_ref.shape[:2]
    block = coef.shape[1] // count
    own_width = residual_ref.shape[2]
    order = [(t, j) for t in range(len(cuts)) for j in range(count)]
    copies = {}
    for n, (t, j) in enumerate(order):
        spot = (buf if t == 0 else later[t - 1]).at[j]
        copies[t, j] = pltpu.make_async_copy(coef.at[:, columns(me ^ j, block, cuts[t])], spot, sems.at[n])
        copies[t, j].start()
    for back, ref, start in ((back_a, mine_ref, 0), (back_b, other_ref, half)):
        for i in range(half):
            part = dot(chosen[start + i], ref[i].astype(jnp.bfloat16), NT)
            back[:, i * rays:(i + 1) * rays] = part.astype(jnp.bfloat16)
    writes = []
    for t, j in order:
        at = columns(me ^ j, block, cuts[t])
        grad = dot(back_a[...], top_ref[:, at], NN) + dot(back_b[...], low_ref[:, at], NN)
        copies[t, j].wait()
        if t == 0:
            buf[j] = buf[j] - 0.5 * grad - 0.5 * grads[j][...].astype(jnp.float32)
            writes.append(pltpu.make_async_copy(buf.at[j], updated.at[:, at], out_sems.at[j]))
            writes[-1].start()
        else:
            later[t - 1][j] = later[t - 1][j] - 0.5 * grad
    for q in range(count):
        @pl.when(me == q)
        def _():
            for i in range(half):
                residual_ref[side * half + i] = mine_ref[i, :, q * own_width:(q + 1) * own_width]
                residual_ref[(1 - side) * half + i] = other_ref[i, :, q * own_width:(q + 1) * own_width]
    for w in writes:
        w.wait()


def finish_kernel(count, cut, masks, info, later, *refs):
    grads = refs[:len(masks)]
    _, updated, buf, sems = refs[len(masks):]
    block = updated.shape[1] // count
    writes = []
    for n, j in enumerate(masks):
        buf[n] = later[j] - 0.5 * grads[n][...].astype(jnp.float32)
        at = columns(info[0] ^ j, block, cut)
        writes.append(pltpu.make_async_copy(buf.at[n], updated.at[:, at], sems.at[n]))
        writes[-1].start()
    for w in writes:
        w.wait()


def step_of(coefficients, measured, ray_voxels, ray_weights, angle_ids, angle_table, harmonics):
    coef_local, cols = coefficients.shape
    projections, _, rays, channels = measured.shape
    rows = projections * rays
    samples = ray_voxels.shape[2]
    count = lax.axis_size("coef")
    me = lax.axis_index("coef")
    half = projections // 2
    block = cols // count
    cuts = cuts_of(block)
    bf16, f32 = jnp.bfloat16, jnp.float32
    shape = jax.ShapeDtypeStruct

    def kernel(body_of, ins, outs, out_shape, scratch=(), grant=12, aliases={}):
        return pl.pallas_call(
            body_of,
            in_specs=ins,
            out_specs=outs,
            out_shape=out_shape,
            scratch_shapes=list(scratch),
            input_output_aliases=aliases,
            compiler_params=pltpu.CompilerParams(vmem_limit_bytes=grant << 20),
        )

    group_bits = 1 if lax.axis_size("groups") % 2 == 0 else 0
    slab_count = lax.axis_size("slab")
    slab_bits = 1 if slab_count % 2 == 0 else 0
    pieces = 1 << (group_bits + slab_bits)
    place = jnp.zeros((), jnp.int32)
    if slab_bits:
        place = place + (lax.axis_index("slab") & 1)
    if group_bits:
        place = place + ((lax.axis_index("groups") & 1) << slab_bits)
    width = harmonics.shape[1] // pieces
    info = jnp.stack([me, me & 1, place]).astype(jnp.int32)
    rows_shape = (rows, samples)
    coef_far, measured_far, vox_far, wgt_far, ids_far, table_far, harm_far = [
        pltpu.with_memory_space_constraint(v, pltpu.HBM)
        for v in (
            coefficients,
            measured.reshape(projections, rays, channels),
            ray_voxels.reshape(rows_shape),
            ray_weights.reshape(rows_shape),
            angle_ids,
            angle_table,
            harmonics,
        )
    ]

    piece = lax.dynamic_slice_in_dim(harmonics, place * width, width, 1)
    fetched = {m: [swap(piece, "coef", m)] for m in range(2, count, 2)}
    *blocks, vox, wgt, chosen = kernel(
        lambda *refs: prepare_kernel(count, *refs),
        [SMEM, SMEM] + [HBM] * 4,
        [VMEM] * (count + 3),
        [shape((coef_local, block), bf16)] * count
        + [
            shape((rows // 2, samples), jnp.int32),
            shape((rows // 2, samples), jnp.int32),
            shape((projections,) + angle_table.shape[1:], bf16),
        ],
        [pltpu.VMEM((count, coef_local, block), f32), pltpu.SemaphoreType.DMA((count + 2 + projections,))],
    )(info, ids_far, coef_far, vox_far, wgt_far, table_far)

    received = {m: swap(blocks[m], "coef", m) for m in range(2, count)}
    received[0] = blocks[0]
    received[1] = swap(blocks[1], "coef", 1)
    near = swap(harmonics, "coef", 1)
    moves = [(0, 1)] * slab_bits + [(1, 0)] * group_bits + [(1, 1)] * (slab_bits * group_bits)
    for m in fetched:
        for up, along in moves:
            total = lax.axis_size("groups") * slab_count
            pairs = [(i, (((i // slab_count) ^ up) * slab_count) + ((i % slab_count) ^ along)) for i in range(total)]
            fetched[m].append(lax.ppermute(fetched[m][0], ("groups", "slab"), pairs))

    top = kernel(
        build_kernel,
        [VMEM, VMEM],
        VMEM,
        shape((rows // 2, cols), bf16),
        [pltpu.VMEM((GROUP * cols // LANES, LANES), f32)],
    )(vox, wgt)
    low = swap(top, "coef", 1)
    for m in list(fetched):
        fetched[m ^ 1] = [swap(v, "coef", 1) for v in fetched[m]]
    far = [v for m in range(2, count) for v in fetched[m]]

    def ray_sums(own, matrix):
        return kernel(
            lambda *refs: sums_kernel(count, own, *refs),
            [SMEM] + [VMEM] * (count + 2) + [HBM],
            VMEM,
            shape((half, rays, channels), f32),
            [pltpu.VMEM((half, rays, channels), f32), pltpu.SemaphoreType.DMA(())],
        )(info, matrix, *blocks, chosen, measured_far)

    mine = ray_sums(True, top)
    other = ray_sums(False, low)
    total = mine + swap(other, "coef", 1)
    mask = 2
    while mask < count:
        total = total + swap(total, "coef", mask)
        mask *= 2
    waves = kernel(
        lambda *refs: gather_kernel(count, pieces, *refs),
        [SMEM, HBM] + [VMEM] * (1 + len(far)),
        VMEM,
        shape((count * coef_local, harmonics.shape[1]), bf16),
        [pltpu.SemaphoreType.DMA((pieces,))],
    )(info, harm_far, near, *far)

    returned = []
    for cut in cuts:
        chunk = cut[1]
        outs = kernel(
            lambda *refs: penalty_kernel(count, pieces, cut, *refs),
            [VMEM] * (count + 1),
            [VMEM] * count,
            [shape((coef_local, chunk), bf16)] * count,
            [
                pltpu.VMEM((count * coef_local, chunk), bf16),
                pltpu.VMEM((chunk, count * coef_local), bf16),
                pltpu.VMEM((count * coef_local, chunk), f32),
            ],
        )(waves, *[received[m] for m in range(count)])
        back = [outs[0]]
        for m in range(1, count):
            back.append(swap(outs[m], "coef", m))
        returned.append(back)

    resid_other = swap(total, "coef", 1)
    updated, residual, *later = kernel(
        lambda *refs: data_kernel(count, cuts, *refs),
        [SMEM] + [VMEM] * 5 + [HBM] + [VMEM] * count,
        [HBM] + [VMEM] * len(cuts),
        [shape((coef_local, cols), f32), shape((projections, rays, channels // count), f32)]
        + [shape((count, coef_local, cut[1]), f32) for cut in cuts[1:]],
        [
            pltpu.VMEM((coef_local, rows // 2), bf16),
            pltpu.VMEM((coef_local, rows // 2), bf16),
            pltpu.VMEM((count, coef_local, cuts[0][1]), f32),
            pltpu.SemaphoreType.DMA((len(cuts) * count,)),
            pltpu.SemaphoreType.DMA((count,)),
        ],
    )(info, total, resid_other, chosen, top, low, coef_far, *returned[0])
    remote = list(range(2, count))
    middle = len(remote) // 2
    for t, cut in list(enumerate(cuts))[1:]:
        for masks in ([0, 1], remote[:middle], remote[middle:]):
            if not masks:
                continue
            updated = kernel(
                lambda *refs: finish_kernel(count, cut, masks, *refs),
                [SMEM] + [VMEM] * (len(masks) + 1) + [HBM],
                HBM,
                shape((coef_local, cols), f32),
                [pltpu.VMEM((len(masks), coef_local, cut[1]), f32), pltpu.SemaphoreType.DMA((len(masks),))],
                aliases={len(masks) + 2: 0},
            )(info, later[t - 1], *[returned[t][m] for m in masks], updated)
    return (updated, residual[:, None])


def solution(mesh):
    in_specs = (
        P("coef", ("groups", "slab")),
        P("groups", "slab", None, None),
        P(),
        P(),
        P(),
        P(None, "coef", None),
        P("coef", None),
    )
    out_specs = (P("coef", ("groups", "slab")), P("groups", "slab", None, "coef"))
    return jax.shard_map(step_of, mesh=mesh, in_specs=in_specs, out_specs=out_specs, check_vma=False)
```

```python
import jax
import jax.numpy as jnp
from jax import lax
from jax.experimental import pallas as pl
from jax.experimental.pallas import tpu as pltpu
from jax.sharding import PartitionSpec as P


LANES = 128
QUARTERS = (2, 2)
GROUP = 32
NT = (((1,), (1,)), ((), ()))
NN = (((1,), (0,)), ((), ()))
VMEM = pl.BlockSpec(memory_space=pltpu.VMEM)
SMEM = pl.BlockSpec(memory_space=pltpu.SMEM)
HBM = pl.BlockSpec(memory_space=pltpu.HBM)


def dot(a, b, dims):
    return lax.dot_general(a, b, dims, preferred_element_type=jnp.float32)


def swap(value, axis, mask):
    count = lax.axis_size(axis)
    return lax.ppermute(value, axis, [(i, i ^ mask) for i in range(count)])


def aligned(index, width):
    return pl.ds(pl.multiple_of(index * width, width), width)


def cuts_of(block):
    if block % (4 * LANES):
        return [(0, block)]
    unit = block // 4
    starts = [unit * sum(QUARTERS[:t]) for t in range(len(QUARTERS))]
    return [(start, unit * size) for start, size in zip(starts, QUARTERS)]


def columns(index, block, cut):
    return pl.ds(pl.multiple_of(index * block + cut[0], LANES), cut[1])


def prepare_kernel(count, cuts, info, ids, coef, vox, wgt, table, *refs):
    parts = refs[:(count - 2) * len(cuts)]
    whole, vox_out, wgt_out, table_mine, table_other, stage, sems = refs[len(parts):]
    me, side = info[0], info[1]
    block = coef.shape[1] // count
    half_rows, half = vox_out.shape[0], table_mine.shape[0]
    order = list(range(2, count)) + [1, 0]
    copies = {}
    for m in order:
        copies[m] = pltpu.make_async_copy(coef.at[:, aligned(me ^ m, block)], stage.at[m], sems.at[m])
    rest = [
        pltpu.make_async_copy(vox.at[aligned(side, half_rows)], vox_out, sems.at[count]),
        pltpu.make_async_copy(wgt.at[aligned(side, half_rows)], wgt_out, sems.at[count + 1]),
    ]
    for n, (out, first) in enumerate(((table_other, (1 - side) * half), (table_mine, side * half))):
        for i in range(half):
            rest.append(pltpu.make_async_copy(table.at[ids[first + i]], out.at[i], sems.at[count + 2 + n * half + i]))
    for m in order:
        copies[m].start()
    for c in rest:
        c.start()
    for m in order:
        copies[m].wait()
        values = stage[m].astype(jnp.bfloat16)
        whole[:, aligned(me ^ m, block)] = values
        if m > 1:
            for t, cut in enumerate(cuts):
                parts[(m - 2) * len(cuts) + t][...] = values[:, cut[0]:cut[0] + cut[1]]
    for c in rest:
        c.wait()


def build_kernel(vox_ref, wgt_ref, matrix_ref, tile_ref):
    rows, samples = vox_ref.shape
    cols = matrix_ref.shape[1]
    high_count = cols // LANES
    low_pos = lax.broadcasted_iota(jnp.int32, (LANES, samples), 0)
    high_pos = lax.broadcasted_iota(jnp.int32, (high_count, samples), 0)
    blank = jnp.zeros((high_count, samples), jnp.bfloat16)

    def build(step, carry):
        first = pl.multiple_of(step * GROUP, GROUP)
        vox = vox_ref[pl.ds(first, GROUP), :]
        wgt = wgt_ref[pl.ds(first, GROUP), :].astype(jnp.float32) * (1.0 / 256.0)
        low = vox & (LANES - 1)
        high = lax.shift_right_logical(vox, LANES.bit_length() - 1)
        hots = []
        for i in range(GROUP):
            low_hot = (low_pos == low[i:i + 1]).astype(jnp.float32).astype(jnp.bfloat16)
            high_hot = jnp.where(high_pos == high[i:i + 1], wgt[i:i + 1], 0.0).astype(jnp.bfloat16)
            hots.append((low_hot, high_hot))
        for i in range(0, GROUP, 2):
            (low_a, high_a), (low_b, high_b) = hots[i:i + 2]
            left = jnp.concatenate([jnp.concatenate([high_a, blank], 1), jnp.concatenate([blank, high_b], 1)], 0)
            right = jnp.concatenate([low_a, low_b], 1)
            tile_ref[i * high_count:(i + 2) * high_count, :] = dot(left, right, NT)
        for h in range(high_count):
            part = tile_ref[pl.ds(h, GROUP, stride=high_count), :]
            matrix_ref[pl.ds(first, GROUP), h * LANES:(h + 1) * LANES] = part.astype(jnp.bfloat16)
        return carry

    lax.fori_loop(0, rows // GROUP, build, 0)


def sums_kernel(count, info, matrix_ref, own, partner, table_own, table_partner, measured, keep, send, target, sem):
    half, rays, width = keep.shape
    me, side = info[0], info[1]
    fetch = pltpu.make_async_copy(measured.at[pl.ds(side * half, half)], target, sem)
    fetch.start()
    sums_own = dot(matrix_ref[...], own[...], NT).astype(jnp.bfloat16)
    sums_partner = dot(matrix_ref[...], partner[...], NT).astype(jnp.bfloat16)
    fetch.wait()
    high = (me // (count // 2)) & 1
    for i in range(half):
        rows = slice(i * rays, (i + 1) * rays)
        for out, bit in ((send, 1 - high), (keep, high)):
            at = aligned(bit, width)
            total = dot(sums_own[rows], table_own[i, :, at], NN) + dot(sums_partner[rows], table_partner[i, :, at], NN)
            out[i] = total - (2.0 / count) * target[i, :, at]


def penalty_kernel(count, pieces, cut, first, info, own, partner, *refs):
    blocks, refs = refs[:count - 2], refs[count - 2:]
    if first:
        harm, near, far = refs[0], refs[1], refs[2:2 + (count - 2) * pieces]
        refs = refs[2 + len(far):]
        outs, waves, sems = refs[:count], refs[count], refs[-1]
        refs = refs[count + 1:-1]
    else:
        waves, outs, refs = refs[0], refs[1:count + 1], refs[count + 1:]
    stack, turned, acc = refs
    me, place = info[0], info[2]
    height = outs[0].shape[0]
    width = waves.shape[1] // pieces
    if first:
        copies = []
        for r in range(pieces):
            spot = waves.at[0:height, r * width:(r + 1) * width]
            copies.append(pltpu.make_async_copy(harm.at[:, aligned(place ^ r, width)], spot, sems.at[r]))
            copies[-1].start()
    at = columns(me, own.shape[1] // count, cut)
    stack[0:height, :] = own[:, at]
    stack[height:2 * height, :] = partner[:, at]
    for j in range(2, count):
        stack[j * height:(j + 1) * height, :] = blocks[j - 2][...]
    turned[...] = jnp.swapaxes(stack[...], 0, 1)
    for r in range(pieces):
        span = slice(r * width, (r + 1) * width)
        if first:
            waves[height:2 * height, span] = near[:, aligned(place ^ r, width)]
            for j in range(2, count):
                waves[j * height:(j + 1) * height, span] = far[(j - 2) * pieces + r][...]
            copies[r].wait()
        wave = waves[:, span]
        field = dot(turned[...], wave, NN)
        slope = (0.5 * jnp.tanh(0.5 * field) - 0.5).astype(jnp.bfloat16)
        part = dot(wave, slope, NT)
        if r > 0:
            part += acc[...]
        if r < pieces - 1:
            acc[...] = part
        else:
            for j in range(count):
                outs[j][...] = part[j * height:(j + 1) * height].astype(outs[j].dtype)


def data_kernel(count, cuts, split, info, *refs):
    halves, refs = (refs[:split], refs[split:2 * split]), refs[2 * split:]
    res_mine, res_other, table_mine, table_other, top_ref, low_ref, coef = refs[:7]
    refs = refs[7:]
    order = [(0, j) for j in range(count)] + [(t, j) for t in range(1, len(cuts)) for j in range(count)]
    ready = [key for key in order if key[0] == 0 or key[1] < 2]
    grads, refs = dict(zip(ready, refs)), refs[len(ready):]
    updated, residual_ref, later = refs[0], refs[1], refs[2:1 + len(cuts)]
    back_a, back_b, buf, sems, out_sems = refs[1 + len(cuts):]
    me, side = info[0], info[1]
    half, rays, width = halves[0][0].shape
    block = coef.shape[1] // count
    own_width = residual_ref.shape[2]
    spots, copies = {}, {}
    for n, (t, j) in enumerate(order):
        if (t, j) in grads:
            spots[t, j] = buf.at[ready.index((t, j)), :, 0:cuts[t][1]]
        else:
            spots[t, j] = later[t - 1].at[j - 2]
        copies[t, j] = pltpu.make_async_copy(coef.at[:, columns(me ^ j, block, cuts[t])], spots[t, j], sems.at[n])
        copies[t, j].start()
    for back, parts, table in ((back_a, halves[0], table_mine), (back_b, halves[1], table_other)):
        for i in range(half):
            total = dot(table[i, :, aligned(me // 2 if split > 1 else 0, width)], parts[0][i], NT)
            for p in range(1, split):
                total += dot(table[i, :, aligned((me // 2) ^ p, width)], parts[p][i], NT)
            back[:, i * rays:(i + 1) * rays] = total.astype(jnp.bfloat16)
    writes = []
    for t, j in order:
        at = columns(me ^ j, block, cuts[t])
        grad = dot(back_a[...], top_ref[:, at], NN) + dot(back_b[...], low_ref[:, at], NN)
        copies[t, j].wait()
        spot = spots[t, j]
        if (t, j) in grads:
            spot[...] = spot[...] - 0.5 * grad - 0.5 * grads[t, j][...].astype(jnp.float32)
            writes.append(pltpu.make_async_copy(spot, updated.at[:, at], out_sems.at[len(writes)]))
            writes[-1].start()
        else:
            spot[...] = spot[...] - 0.5 * grad
    for q in range(2):
        @pl.when(side == q)
        def _():
            for i in range(half):
                residual_ref[side * half + i] = res_mine[i, :, q * own_width:(q + 1) * own_width]
                residual_ref[(1 - side) * half + i] = res_other[i, :, q * own_width:(q + 1) * own_width]
    for w in writes:
        w.wait()


def finish_kernel(count, cut, masks, info, later, *refs):
    grads = refs[:len(masks)]
    _, updated, buf, sems = refs[len(masks):]
    block = updated.shape[1] // count
    writes = []
    for n, j in enumerate(masks):
        buf[n] = later[j - 2] - 0.5 * grads[n][...].astype(jnp.float32)
        at = columns(info[0] ^ j, block, cut)
        writes.append(pltpu.make_async_copy(buf.at[n], updated.at[:, at], sems.at[n]))
        writes[-1].start()
    for w in writes:
        w.wait()


def step_of(coefficients, measured, ray_voxels, ray_weights, angle_ids, angle_table, harmonics):
    coef_local, cols = coefficients.shape
    projections, _, rays, channels = measured.shape
    rows = projections * rays
    samples = ray_voxels.shape[2]
    count = lax.axis_size("coef")
    me = lax.axis_index("coef")
    half = projections // 2
    block = cols // count
    cuts = cuts_of(block)
    bf16, f32 = jnp.bfloat16, jnp.float32
    shape = jax.ShapeDtypeStruct

    def kernel(body_of, ins, outs, out_shape, scratch=(), grant=12, aliases={}):
        return pl.pallas_call(
            body_of,
            in_specs=ins,
            out_specs=outs,
            out_shape=out_shape,
            scratch_shapes=list(scratch),
            input_output_aliases=aliases,
            compiler_params=pltpu.CompilerParams(vmem_limit_bytes=grant << 20),
        )

    group_bits = 1 if lax.axis_size("groups") % 2 == 0 else 0
    slab_count = lax.axis_size("slab")
    slab_bits = 1 if slab_count % 2 == 0 else 0
    pieces = 1 << (group_bits + slab_bits)
    place = jnp.zeros((), jnp.int32)
    if slab_bits:
        place = place + (lax.axis_index("slab") & 1)
    if group_bits:
        place = place + ((lax.axis_index("groups") & 1) << slab_bits)
    width = harmonics.shape[1] // pieces
    info = jnp.stack([me, me & 1, place]).astype(jnp.int32)
    rows_shape = (rows, samples)
    coef_far, measured_far, vox_far, wgt_far, ids_far, table_far, harm_far = [
        pltpu.with_memory_space_constraint(v, pltpu.HBM)
        for v in (
            coefficients,
            measured.reshape(projections, rays, channels),
            ray_voxels.reshape(rows_shape),
            ray_weights.reshape(rows_shape),
            angle_ids,
            angle_table,
            harmonics,
        )
    ]

    piece = lax.dynamic_slice_in_dim(harmonics, place * width, width, 1)
    fetched = {m: [swap(piece, "coef", m)] for m in range(2, count, 2)}
    table_shape = shape((half,) + angle_table.shape[1:], bf16)
    *parts, own, vox, wgt, table_mine, table_other = kernel(
        lambda *refs: prepare_kernel(count, cuts, *refs),
        [SMEM, SMEM] + [HBM] * 4,
        [VMEM] * ((count - 2) * len(cuts) + 5),
        [shape((coef_local, cut[1]), bf16) for _ in range(2, count) for cut in cuts]
        + [shape((coef_local, cols), bf16)]
        + [shape((rows // 2, samples), jnp.int32)] * 2
        + [table_shape] * 2,
        [pltpu.VMEM((count, coef_local, block), f32), pltpu.SemaphoreType.DMA((count + 2 + projections,))],
    )(info, ids_far, coef_far, vox_far, wgt_far, table_far)
    received = []
    for t in range(len(cuts)):
        received.append([swap(parts[(m - 2) * len(cuts) + t], "coef", m) for m in range(2, count)])
    partner = swap(own, "coef", 1)
    table_partner = swap(table_other, "coef", 1)
    near = swap(harmonics, "coef", 1)
    moves = [(0, 1)] * slab_bits + [(1, 0)] * group_bits + [(1, 1)] * (slab_bits * group_bits)
    for m in fetched:
        for up, along in moves:
            total = lax.axis_size("groups") * slab_count
            pairs = [(i, (((i // slab_count) ^ up) * slab_count) + ((i % slab_count) ^ along)) for i in range(total)]
            fetched[m].append(lax.ppermute(fetched[m][0], ("groups", "slab"), pairs))

    top = kernel(
        build_kernel,
        [VMEM, VMEM],
        VMEM,
        shape((rows // 2, cols), bf16),
        [pltpu.VMEM((GROUP * cols // LANES, LANES), f32)],
    )(vox, wgt)
    low = swap(top, "coef", 1)
    for m in list(fetched):
        fetched[m ^ 1] = [swap(v, "coef", 1) for v in fetched[m]]
    far = [v for m in range(2, count) for v in fetched[m]]

    total, send = kernel(
        lambda *refs: sums_kernel(count, *refs),
        [SMEM] + [VMEM] * 5 + [HBM],
        [VMEM, VMEM],
        [shape((half, rays, channels // 2), f32)] * 2,
        [pltpu.VMEM((half, rays, channels), f32), pltpu.SemaphoreType.DMA(())],
    )(info, top, own, partner, table_mine, table_partner, measured_far)

    masks = [1 << n for n in range(1, count.bit_length() - 1)]
    for mask in masks[::-1]:
        if mask < count // 2:
            width = total.shape[2] // 2
            bit = jnp.where((me & mask) == 0, 0, 1)
            send = lax.dynamic_slice_in_dim(total, (1 - bit) * width, width, 2)
            total = lax.dynamic_slice_in_dim(total, bit * width, width, 2)
        total = total + swap(send, "coef", mask)

    returned = []
    waves = None
    for t, cut in enumerate(cuts):
        first = t == 0
        extra = [harm_far, near] + far if first else [waves]
        wide = [shape((count * coef_local, harmonics.shape[1]), bf16)] if first else []
        outs = kernel(
            lambda *refs: penalty_kernel(count, pieces, cut, first, *refs),
            [SMEM] + [VMEM] * count + ([HBM] + [VMEM] * (1 + len(far)) if first else [VMEM]),
            [VMEM] * (count + len(wide)),
            [shape((coef_local, cut[1]), bf16)] * count + wide,
            [
                pltpu.VMEM((count * coef_local, cut[1]), bf16),
                pltpu.VMEM((cut[1], count * coef_local), bf16),
                pltpu.VMEM((count * coef_local, cut[1]), f32),
            ]
            + ([pltpu.SemaphoreType.DMA((pieces,))] if first else []),
        )(info, own, partner, *received[t], *extra)
        if first:
            waves = outs[-1]
        back = [outs[0]]
        for m in range(1, count):
            back.append(swap(outs[m], "coef", m))
        returned.append(back)
        if first:
            half_mine = [total.astype(bf16)]
            for mask in masks:
                other = [swap(v, "coef", mask) for v in half_mine]
                if total.shape[2] % LANES == 0:
                    half_mine = half_mine + other
                    continue
                low_bit, pair = (me & mask) == 0, (half_mine[0], other[0])
                ordered = [jnp.where(low_bit, *pair), jnp.where(low_bit, *pair[::-1])]
                half_mine = [jnp.concatenate(ordered, 2)]
    res_other = swap(total, "coef", 1)
    half_other = [swap(v, "coef", 1) for v in half_mine]

    ready = [(t, j) for t in range(len(cuts)) for j in range(count) if t == 0 or j < 2]
    updated, residual, *later = kernel(
        lambda *refs: data_kernel(count, cuts, len(half_mine), *refs),
        [SMEM] + [VMEM] * (2 * len(half_mine) + 6) + [HBM] + [VMEM] * len(ready),
        [HBM] + [VMEM] * len(cuts),
        [shape((coef_local, cols), f32), shape((projections, rays, channels // count), f32)]
        + [shape((count - 2, coef_local, cut[1]), f32) for cut in cuts[1:]],
        [
            pltpu.VMEM((coef_local, rows // 2), bf16),
            pltpu.VMEM((coef_local, rows // 2), bf16),
            pltpu.VMEM((len(ready), coef_local, max(cut[1] for cut in cuts)), f32),
            pltpu.SemaphoreType.DMA((len(cuts) * count,)),
            pltpu.SemaphoreType.DMA((len(ready),)),
        ],
    )(
        info,
        *half_mine,
        *half_other,
        total,
        res_other,
        table_mine,
        table_other,
        top,
        low,
        coef_far,
        *[returned[t][j] for t, j in ready],
    )
    remote = list(range(2, count))
    middle = len(remote) // 2
    for t, cut in list(enumerate(cuts))[1:]:
        for masks in (remote[:middle], remote[middle:]):
            if not masks:
                continue
            updated = kernel(
                lambda *refs: finish_kernel(count, cut, masks, *refs),
                [SMEM] + [VMEM] * (len(masks) + 1) + [HBM],
                HBM,
                shape((coef_local, cols), f32),
                [pltpu.VMEM((len(masks), coef_local, cut[1]), f32), pltpu.SemaphoreType.DMA((len(masks),))],
                aliases={len(masks) + 2: 0},
            )(info, later[t - 1], *[returned[t][m] for m in masks], updated)
    return (updated, residual[:, None])


def solution(mesh):
    in_specs = (
        P("coef", ("groups", "slab")),
        P("groups", "slab", None, None),
        P(),
        P(),
        P(),
        P(None, "coef", None),
        P("coef", None),
    )
    out_specs = (P("coef", ("groups", "slab")), P("groups", "slab", None, "coef"))
    return jax.shard_map(step_of, mesh=mesh, in_specs=in_specs, out_specs=out_specs, check_vma=False)
```

```python
import jax
import jax.numpy as jnp
from jax import lax
from jax.experimental import pallas as pl
from jax.experimental.pallas import tpu as pltpu
from jax.sharding import PartitionSpec as P


LANES = 128
QUARTERS = (2, 2)
GROUP = 32
NT = (((1,), (1,)), ((), ()))
NN = (((1,), (0,)), ((), ()))
VMEM = pl.BlockSpec(memory_space=pltpu.VMEM)
SMEM = pl.BlockSpec(memory_space=pltpu.SMEM)
HBM = pl.BlockSpec(memory_space=pltpu.HBM)


def dot(a, b, dims):
    return lax.dot_general(a, b, dims, preferred_element_type=jnp.float32)


def swap(value, axis, mask):
    count = lax.axis_size(axis)
    return lax.ppermute(value, axis, [(i, i ^ mask) for i in range(count)])


def aligned(index, width):
    return pl.ds(pl.multiple_of(index * width, width), width)


def cuts_of(block):
    if block % (4 * LANES):
        return [(0, block)]
    unit = block // 4
    starts = [unit * sum(QUARTERS[:t]) for t in range(len(QUARTERS))]
    return [(start, unit * size) for start, size in zip(starts, QUARTERS)]


def columns(index, block, cut):
    return pl.ds(pl.multiple_of(index * block + cut[0], LANES), cut[1])


def prepare_kernel(count, cuts, info, ids, coef, vox, wgt, table, *refs):
    parts = refs[:(count - 2) * len(cuts)]
    whole, vox_out, wgt_out, table_mine, table_other, stage, sems = refs[len(parts):]
    me, side = info[0], info[1]
    block = coef.shape[1] // count
    half_rows, half = vox_out.shape[0], table_mine.shape[0]
    order = list(range(2, count)) + [1, 0]
    copies = {}
    for m in order:
        copies[m] = pltpu.make_async_copy(coef.at[:, aligned(me ^ m, block)], stage.at[m], sems.at[m])
    rest = [
        pltpu.make_async_copy(vox.at[aligned(side, half_rows)], vox_out, sems.at[count]),
        pltpu.make_async_copy(wgt.at[aligned(side, half_rows)], wgt_out, sems.at[count + 1]),
    ]
    for n, (out, first) in enumerate(((table_other, (1 - side) * half), (table_mine, side * half))):
        for i in range(half):
            rest.append(pltpu.make_async_copy(table.at[ids[first + i]], out.at[i], sems.at[count + 2 + n * half + i]))
    for m in order:
        copies[m].start()
    for c in rest:
        c.start()
    for m in order:
        copies[m].wait()
        values = stage[m].astype(jnp.bfloat16)
        whole[:, aligned(me ^ m, block)] = values
        if m > 1:
            for t, cut in enumerate(cuts):
                parts[(m - 2) * len(cuts) + t][...] = values[:, cut[0]:cut[0] + cut[1]]
    for c in rest:
        c.wait()


def build_kernel(vox_ref, wgt_ref, matrix_ref, tile_ref):
    rows, samples = vox_ref.shape
    cols = matrix_ref.shape[1]
    high_count = cols // LANES
    low_pos = lax.broadcasted_iota(jnp.int32, (LANES, samples), 0)
    high_pos = lax.broadcasted_iota(jnp.int32, (high_count, samples), 0)
    blank = jnp.zeros((high_count, samples), jnp.bfloat16)

    def build(step, carry):
        first = pl.multiple_of(step * GROUP, GROUP)
        vox = vox_ref[pl.ds(first, GROUP), :]
        wgt = wgt_ref[pl.ds(first, GROUP), :].astype(jnp.float32) * (1.0 / 256.0)
        low = vox & (LANES - 1)
        high = lax.shift_right_logical(vox, LANES.bit_length() - 1)
        hots = []
        for i in range(GROUP):
            low_hot = (low_pos == low[i:i + 1]).astype(jnp.float32).astype(jnp.bfloat16)
            high_hot = jnp.where(high_pos == high[i:i + 1], wgt[i:i + 1], 0.0).astype(jnp.bfloat16)
            hots.append((low_hot, high_hot))
        for i in range(0, GROUP, 2):
            (low_a, high_a), (low_b, high_b) = hots[i:i + 2]
            left = jnp.concatenate([jnp.concatenate([high_a, blank], 1), jnp.concatenate([blank, high_b], 1)], 0)
            right = jnp.concatenate([low_a, low_b], 1)
            tile_ref[i * high_count:(i + 2) * high_count, :] = dot(left, right, NT)
        for h in range(high_count):
            part = tile_ref[pl.ds(h, GROUP, stride=high_count), :]
            matrix_ref[pl.ds(first, GROUP), h * LANES:(h + 1) * LANES] = part.astype(jnp.bfloat16)
        return carry

    lax.fori_loop(0, rows // GROUP, build, 0)


def sums_kernel(count, info, matrix_ref, own, partner, table_own, table_partner, measured, keep, send, target, sem):
    half, rays, width = keep.shape
    me, side = info[0], info[1]
    fetch = pltpu.make_async_copy(measured.at[pl.ds(side * half, half)], target, sem)
    fetch.start()
    sums_own = dot(matrix_ref[...], own[...], NT).astype(jnp.bfloat16)
    sums_partner = dot(matrix_ref[...], partner[...], NT).astype(jnp.bfloat16)
    fetch.wait()
    high = (me // (count // 2)) & 1
    for i in range(half):
        rows = slice(i * rays, (i + 1) * rays)
        for out, bit in ((send, 1 - high), (keep, high)):
            at = aligned(bit, width)
            total = dot(sums_own[rows], table_own[i, :, at], NN) + dot(sums_partner[rows], table_partner[i, :, at], NN)
            out[i] = total - (2.0 / count) * target[i, :, at]


def stack_near_kernel(pieces, info, harm, near, waves, sems):
    place = info[2]
    height = near.shape[0]
    width = waves.shape[1] // pieces
    copies = []
    for r in range(pieces):
        spot = waves.at[0:height, r * width:(r + 1) * width]
        copies.append(pltpu.make_async_copy(harm.at[:, aligned(place ^ r, width)], spot, sems.at[r]))
        copies[-1].start()
    for r in range(pieces):
        waves[height:2 * height, r * width:(r + 1) * width] = near[:, aligned(place ^ r, width)]
    for c in copies:
        c.wait()


def stack_far_kernel(pieces, _, *refs):
    far, waves = refs[:-1], refs[-1]
    height, width = far[0].shape
    for n, ref in enumerate(far):
        j, r = divmod(n, pieces)
        waves[(j + 2) * height:(j + 3) * height, r * width:(r + 1) * width] = ref[...]


def penalty_kernel(count, pieces, cut, info, waves, own, partner, *refs):
    blocks, outs = refs[:count - 2], refs[count - 2:2 * count - 2]
    stack, turned, acc = refs[2 * count - 2:]
    height = outs[0].shape[0]
    width = waves.shape[1] // pieces
    at = columns(info[0], own.shape[1] // count, cut)
    stack[0:height, :] = own[:, at]
    stack[height:2 * height, :] = partner[:, at]
    for j in range(2, count):
        stack[j * height:(j + 1) * height, :] = blocks[j - 2][...]
    turned[...] = jnp.swapaxes(stack[...], 0, 1)
    for r in range(pieces):
        wave = waves[:, r * width:(r + 1) * width]
        field = dot(turned[...], wave, NN)
        slope = (0.5 * jnp.tanh(0.5 * field) - 0.5).astype(jnp.bfloat16)
        part = dot(wave, slope, NT)
        if r > 0:
            part += acc[...]
        if r < pieces - 1:
            acc[...] = part
        else:
            for j in range(count):
                outs[j][...] = part[j * height:(j + 1) * height].astype(outs[j].dtype)


def data_kernel(count, cuts, split, info, *refs):
    halves, refs = (refs[:split], refs[split:2 * split]), refs[2 * split:]
    res_mine, res_other, table_mine, table_other, top_ref, low_ref, coef = refs[:7]
    refs = refs[7:]
    order = [(0, j) for j in range(count)] + [(t, j) for t in range(1, len(cuts)) for j in range(count)]
    ready = [key for key in order if key[0] == 0 or key[1] < 2]
    grads, refs = dict(zip(ready, refs)), refs[len(ready):]
    updated, residual_ref, later = refs[0], refs[1], refs[2:1 + len(cuts)]
    back_a, back_b, buf, sems, out_sems = refs[1 + len(cuts):]
    me, side = info[0], info[1]
    half, rays, width = halves[0][0].shape
    block = coef.shape[1] // count
    own_width = residual_ref.shape[2]
    spots, copies = {}, {}
    for n, (t, j) in enumerate(order):
        if (t, j) in grads:
            spots[t, j] = buf.at[ready.index((t, j)), :, 0:cuts[t][1]]
        else:
            spots[t, j] = later[t - 1].at[j - 2]
        copies[t, j] = pltpu.make_async_copy(coef.at[:, columns(me ^ j, block, cuts[t])], spots[t, j], sems.at[n])
        copies[t, j].start()
    for back, parts, table in ((back_a, halves[0], table_mine), (back_b, halves[1], table_other)):
        for i in range(half):
            total = dot(table[i, :, aligned(me // 2 if split > 1 else 0, width)], parts[0][i], NT)
            for p in range(1, split):
                total += dot(table[i, :, aligned((me // 2) ^ p, width)], parts[p][i], NT)
            back[:, i * rays:(i + 1) * rays] = total.astype(jnp.bfloat16)
    writes = []
    for t, j in order:
        at = columns(me ^ j, block, cuts[t])
        grad = dot(back_a[...], top_ref[:, at], NN) + dot(back_b[...], low_ref[:, at], NN)
        copies[t, j].wait()
        spot = spots[t, j]
        if (t, j) in grads:
            spot[...] = spot[...] - 0.5 * grad - 0.5 * grads[t, j][...].astype(jnp.float32)
            writes.append(pltpu.make_async_copy(spot, updated.at[:, at], out_sems.at[len(writes)]))
            writes[-1].start()
        else:
            spot[...] = spot[...] - 0.5 * grad
    for q in range(2):
        @pl.when(side == q)
        def _():
            for i in range(half):
                residual_ref[side * half + i] = res_mine[i, :, q * own_width:(q + 1) * own_width]
                residual_ref[(1 - side) * half + i] = res_other[i, :, q * own_width:(q + 1) * own_width]
    for w in writes:
        w.wait()


def finish_kernel(count, cut, masks, info, later, *refs):
    grads = refs[:len(masks)]
    _, updated, buf, sems = refs[len(masks):]
    block = updated.shape[1] // count
    writes = []
    for n, j in enumerate(masks):
        buf[n] = later[j - 2] - 0.5 * grads[n][...].astype(jnp.float32)
        at = columns(info[0] ^ j, block, cut)
        writes.append(pltpu.make_async_copy(buf.at[n], updated.at[:, at], sems.at[n]))
        writes[-1].start()
    for w in writes:
        w.wait()


def step_of(coefficients, measured, ray_voxels, ray_weights, angle_ids, angle_table, harmonics):
    coef_local, cols = coefficients.shape
    projections, _, rays, channels = measured.shape
    rows = projections * rays
    samples = ray_voxels.shape[2]
    count = lax.axis_size("coef")
    me = lax.axis_index("coef")
    half = projections // 2
    block = cols // count
    cuts = cuts_of(block)
    bf16, f32 = jnp.bfloat16, jnp.float32
    shape = jax.ShapeDtypeStruct

    def kernel(body_of, ins, outs, out_shape, scratch=(), grant=12, aliases={}):
        return pl.pallas_call(
            body_of,
            in_specs=ins,
            out_specs=outs,
            out_shape=out_shape,
            scratch_shapes=list(scratch),
            input_output_aliases=aliases,
            compiler_params=pltpu.CompilerParams(vmem_limit_bytes=grant << 20),
        )

    group_bits = 1 if lax.axis_size("groups") % 2 == 0 else 0
    slab_count = lax.axis_size("slab")
    slab_bits = 1 if slab_count % 2 == 0 else 0
    pieces = 1 << (group_bits + slab_bits)
    place = jnp.zeros((), jnp.int32)
    if slab_bits:
        place = place + (lax.axis_index("slab") & 1)
    if group_bits:
        place = place + ((lax.axis_index("groups") & 1) << slab_bits)
    width = harmonics.shape[1] // pieces
    info = jnp.stack([me, me & 1, place]).astype(jnp.int32)
    rows_shape = (rows, samples)
    coef_far, measured_far, vox_far, wgt_far, ids_far, table_far, harm_far = [
        pltpu.with_memory_space_constraint(v, pltpu.HBM)
        for v in (
            coefficients,
            measured.reshape(projections, rays, channels),
            ray_voxels.reshape(rows_shape),
            ray_weights.reshape(rows_shape),
            angle_ids,
            angle_table,
            harmonics,
        )
    ]

    piece = lax.dynamic_slice_in_dim(harmonics, place * width, width, 1)
    fetched = {m: [swap(piece, "coef", m)] for m in range(2, count, 2)}
    table_shape = shape((half,) + angle_table.shape[1:], bf16)
    *parts, own, vox, wgt, table_mine, table_other = kernel(
        lambda *refs: prepare_kernel(count, cuts, *refs),
        [SMEM, SMEM] + [HBM] * 4,
        [VMEM] * ((count - 2) * len(cuts) + 5),
        [shape((coef_local, cut[1]), bf16) for _ in range(2, count) for cut in cuts]
        + [shape((coef_local, cols), bf16)]
        + [shape((rows // 2, samples), jnp.int32)] * 2
        + [table_shape] * 2,
        [pltpu.VMEM((count, coef_local, block), f32), pltpu.SemaphoreType.DMA((count + 2 + projections,))],
    )(info, ids_far, coef_far, vox_far, wgt_far, table_far)
    received = []
    for t in range(len(cuts)):
        received.append([swap(parts[(m - 2) * len(cuts) + t], "coef", m) for m in range(2, count)])
    partner = swap(own, "coef", 1)
    near = swap(harmonics, "coef", 1)
    table_partner = swap(table_other, "coef", 1)
    moves = [(0, 1)] * slab_bits + [(1, 0)] * group_bits + [(1, 1)] * (slab_bits * group_bits)
    for m in fetched:
        for up, along in moves:
            total = lax.axis_size("groups") * slab_count
            pairs = [(i, (((i // slab_count) ^ up) * slab_count) + ((i % slab_count) ^ along)) for i in range(total)]
            fetched[m].append(lax.ppermute(fetched[m][0], ("groups", "slab"), pairs))

    top = kernel(
        build_kernel,
        [VMEM, VMEM],
        VMEM,
        shape((rows // 2, cols), bf16),
        [pltpu.VMEM((GROUP * cols // LANES, LANES), f32)],
    )(vox, wgt)
    low = swap(top, "coef", 1)
    for m in list(fetched):
        fetched[m ^ 1] = [swap(v, "coef", 1) for v in fetched[m]]
    far = [v for m in range(2, count) for v in fetched[m]]

    total, send = kernel(
        lambda *refs: sums_kernel(count, *refs),
        [SMEM] + [VMEM] * 5 + [HBM],
        [VMEM, VMEM],
        [shape((half, rays, channels // 2), f32)] * 2,
        [pltpu.VMEM((half, rays, channels), f32), pltpu.SemaphoreType.DMA(())],
    )(info, top, own, partner, table_mine, table_partner, measured_far)

    masks = [1 << n for n in range(1, count.bit_length() - 1)]
    for mask in masks[::-1]:
        if mask < count // 2:
            width = total.shape[2] // 2
            bit = jnp.where((me & mask) == 0, 0, 1)
            send = lax.dynamic_slice_in_dim(total, (1 - bit) * width, width, 2)
            total = lax.dynamic_slice_in_dim(total, bit * width, width, 2)
        total = total + swap(send, "coef", mask)

    wide = shape((count * coef_local, harmonics.shape[1]), bf16)
    waves = kernel(
        lambda *refs: stack_near_kernel(pieces, *refs),
        [SMEM, HBM, VMEM],
        VMEM,
        wide,
        [pltpu.SemaphoreType.DMA((pieces,))],
    )(info, harm_far, near)
    waves = kernel(
        lambda *refs: stack_far_kernel(pieces, *refs), [VMEM] * (1 + len(far)), VMEM, wide, aliases={0: 0}
    )(waves, *far)

    returned = []
    for t, cut in enumerate(cuts):
        first = t == 0
        outs = kernel(
            lambda *refs: penalty_kernel(count, pieces, cut, *refs),
            [SMEM] + [VMEM] * (count + 1),
            [VMEM] * count,
            [shape((coef_local, cut[1]), bf16)] * count,
            [
                pltpu.VMEM((count * coef_local, cut[1]), bf16),
                pltpu.VMEM((cut[1], count * coef_local), bf16),
                pltpu.VMEM((count * coef_local, cut[1]), f32),
            ],
        )(info, waves, own, partner, *received[t])
        back = [outs[0]]
        for m in range(1, count):
            back.append(swap(outs[m], "coef", m))
        returned.append(back)
        if first:
            half_mine = [total.astype(bf16)]
            for mask in masks:
                other = [swap(v, "coef", mask) for v in half_mine]
                if total.shape[2] % LANES == 0:
                    half_mine = half_mine + other
                    continue
                low_bit, pair = (me & mask) == 0, (half_mine[0], other[0])
                ordered = [jnp.where(low_bit, *pair), jnp.where(low_bit, *pair[::-1])]
                half_mine = [jnp.concatenate(ordered, 2)]
    res_other = swap(total, "coef", 1)
    half_other = [swap(v, "coef", 1) for v in half_mine]

    ready = [(t, j) for t in range(len(cuts)) for j in range(count) if t == 0 or j < 2]
    updated, residual, *later = kernel(
        lambda *refs: data_kernel(count, cuts, len(half_mine), *refs),
        [SMEM] + [VMEM] * (2 * len(half_mine) + 6) + [HBM] + [VMEM] * len(ready),
        [HBM] + [VMEM] * len(cuts),
        [shape((coef_local, cols), f32), shape((projections, rays, channels // count), f32)]
        + [shape((count - 2, coef_local, cut[1]), f32) for cut in cuts[1:]],
        [
            pltpu.VMEM((coef_local, rows // 2), bf16),
            pltpu.VMEM((coef_local, rows // 2), bf16),
            pltpu.VMEM((len(ready), coef_local, max(cut[1] for cut in cuts)), f32),
            pltpu.SemaphoreType.DMA((len(cuts) * count,)),
            pltpu.SemaphoreType.DMA((len(ready),)),
        ],
    )(
        info,
        *half_mine,
        *half_other,
        total,
        res_other,
        table_mine,
        table_other,
        top,
        low,
        coef_far,
        *[returned[t][j] for t, j in ready],
    )
    remote = list(range(2, count))
    middle = len(remote) // 2
    for t, cut in list(enumerate(cuts))[1:]:
        for masks in (remote[:middle], remote[middle:]):
            if not masks:
                continue
            updated = kernel(
                lambda *refs: finish_kernel(count, cut, masks, *refs),
                [SMEM] + [VMEM] * (len(masks) + 1) + [HBM],
                HBM,
                shape((coef_local, cols), f32),
                [pltpu.VMEM((len(masks), coef_local, cut[1]), f32), pltpu.SemaphoreType.DMA((len(masks),))],
                aliases={len(masks) + 2: 0},
            )(info, later[t - 1], *[returned[t][m] for m in masks], updated)
    return (updated, residual[:, None])


def solution(mesh):
    in_specs = (
        P("coef", ("groups", "slab")),
        P("groups", "slab", None, None),
        P(),
        P(),
        P(),
        P(None, "coef", None),
        P("coef", None),
    )
    out_specs = (P("coef", ("groups", "slab")), P("groups", "slab", None, "coef"))
    return jax.shard_map(step_of, mesh=mesh, in_specs=in_specs, out_specs=out_specs, check_vma=False)
```

```python
import jax
import jax.numpy as jnp
from jax import lax
from jax.experimental import pallas as pl
from jax.experimental.pallas import tpu as pltpu
from jax.sharding import PartitionSpec as P


LANES = 128
QUARTERS = (2, 2)
GROUP = 32
NT = (((1,), (1,)), ((), ()))
NN = (((1,), (0,)), ((), ()))
VMEM = pl.BlockSpec(memory_space=pltpu.VMEM)
HBM = pl.BlockSpec(memory_space=pltpu.HBM)


def dot(a, b, dims):
    return lax.dot_general(a, b, dims, preferred_element_type=jnp.float32)


def swap(value, axis, mask):
    count = lax.axis_size(axis)
    return lax.ppermute(value, axis, [(i, i ^ mask) for i in range(count)])


def aligned(index, width):
    return pl.ds(pl.multiple_of(index * width, width), width)


def cuts_of(block):
    if block % (4 * LANES):
        return [(0, block)]
    unit = block // 4
    starts = [unit * sum(QUARTERS[:t]) for t in range(len(QUARTERS))]
    return [(start, unit * size) for start, size in zip(starts, QUARTERS)]


def position():
    me = lax.axis_index("coef")
    place = jnp.zeros((), jnp.int32)
    for axis in ("groups", "slab"):
        if lax.axis_size(axis) % 2 == 0:
            place = place * 2 + (lax.axis_index(axis) & 1)
    return me, me & 1, place


def columns(index, block, cut):
    return pl.ds(pl.multiple_of(index * block + cut[0], LANES), cut[1])


def prepare_kernel(count, cuts, ids_far, coef, vox, wgt, table, *refs):
    full, parts = refs[:count - 3], refs[count - 3:count - 3 + len(cuts)]
    whole, vox_out, wgt_out, table_mine, table_other, stage, ids, sems = refs[count - 3 + len(cuts):]
    me, side, _ = position()
    block = coef.shape[1] // count
    half_rows, half = vox_out.shape[0], table_mine.shape[0]
    order = list(range(2, count)) + [1, 0]
    copies = {}
    for m in order:
        copies[m] = pltpu.make_async_copy(coef.at[:, aligned(me ^ m, block)], stage.at[m], sems.at[m])
    rest = [
        pltpu.make_async_copy(vox.at[aligned(side, half_rows)], vox_out, sems.at[count]),
        pltpu.make_async_copy(wgt.at[aligned(side, half_rows)], wgt_out, sems.at[count + 1]),
    ]
    numbers = pltpu.make_async_copy(ids_far, ids, sems.at[count + 2 + 2 * half])
    numbers.start()
    for m in order:
        copies[m].start()
    numbers.wait()
    for n, (out, first) in enumerate(((table_other, (1 - side) * half), (table_mine, side * half))):
        for i in range(half):
            rest.append(pltpu.make_async_copy(table.at[ids[first + i]], out.at[i], sems.at[count + 2 + n * half + i]))
    for c in rest:
        c.start()
    for m in order:
        copies[m].wait()
        values = stage[m].astype(jnp.bfloat16)
        whole[:, aligned(me ^ m, block)] = values
        if 1 < m < count - 1:
            full[m - 2][...] = values
        if m == count - 1:
            for t, cut in enumerate(cuts):
                parts[t][...] = values[:, cut[0]:cut[0] + cut[1]]
    for c in rest:
        c.wait()


def build_kernel(vox_ref, wgt_ref, matrix_ref, tile_ref):
    rows, samples = vox_ref.shape
    cols = matrix_ref.shape[1]
    high_count = cols // LANES
    low_pos = lax.broadcasted_iota(jnp.int32, (LANES, samples), 0)
    high_pos = lax.broadcasted_iota(jnp.int32, (high_count, samples), 0)
    blank = jnp.zeros((high_count, samples), jnp.bfloat16)

    def build(step, carry):
        first = pl.multiple_of(step * GROUP, GROUP)
        vox = vox_ref[pl.ds(first, GROUP), :]
        wgt = wgt_ref[pl.ds(first, GROUP), :].astype(jnp.float32) * (1.0 / 256.0)
        low = vox & (LANES - 1)
        high = lax.shift_right_logical(vox, LANES.bit_length() - 1)
        hots = []
        for i in range(GROUP):
            low_hot = (low_pos == low[i:i + 1]).astype(jnp.float32).astype(jnp.bfloat16)
            high_hot = jnp.where(high_pos == high[i:i + 1], wgt[i:i + 1], 0.0).astype(jnp.bfloat16)
            hots.append((low_hot, high_hot))
        for i in range(0, GROUP, 2):
            (low_a, high_a), (low_b, high_b) = hots[i:i + 2]
            left = jnp.concatenate([jnp.concatenate([high_a, blank], 1), jnp.concatenate([blank, high_b], 1)], 0)
            right = jnp.concatenate([low_a, low_b], 1)
            tile_ref[i * high_count:(i + 2) * high_count, :] = dot(left, right, NT)
        for h in range(high_count):
            part = tile_ref[pl.ds(h, GROUP, stride=high_count), :]
            matrix_ref[pl.ds(first, GROUP), h * LANES:(h + 1) * LANES] = part.astype(jnp.bfloat16)
        return carry

    lax.fori_loop(0, rows // GROUP, build, 0)


def sums_kernel(count, matrix_ref, own, partner, table_own, table_partner, measured, keep, send, target, sem):
    half, rays, width = keep.shape
    me, side, _ = position()
    fetch = pltpu.make_async_copy(measured.at[pl.ds(side * half, half)], target, sem)
    fetch.start()
    sums_own = dot(matrix_ref[...], own[...], NT).astype(jnp.bfloat16)
    sums_partner = dot(matrix_ref[...], partner[...], NT).astype(jnp.bfloat16)
    fetch.wait()
    high = (me // (count // 2)) & 1
    for i in range(half):
        rows = slice(i * rays, (i + 1) * rays)
        for out, bit in ((send, 1 - high), (keep, high)):
            at = aligned(bit, width)
            total = dot(sums_own[rows], table_own[i, :, at], NN) + dot(sums_partner[rows], table_partner[i, :, at], NN)
            out[i] = total - (2.0 / count) * target[i, :, at]


def stack_kernel(pieces, own, near, *refs):
    far, waves = refs[:-1], refs[-1]
    place = position()[2]
    height = near.shape[0]
    width = waves.shape[1] // pieces
    for r in range(pieces):
        span = slice(r * width, (r + 1) * width)
        waves[0:height, span] = own[:, aligned(place ^ r, width)]
        waves[height:2 * height, span] = near[:, aligned(place ^ r, width)]
        for j in range(len(far) // pieces):
            waves[(j + 2) * height:(j + 3) * height, span] = far[j * pieces + r][...]


def penalty_kernel(count, pieces, cut, waves, own, partner, *refs):
    blocks, outs = refs[:count - 2], refs[count - 2:2 * count - 2]
    stack, turned, acc = refs[2 * count - 2:]
    height = outs[0].shape[0]
    width = waves.shape[1] // pieces
    at = columns(position()[0], own.shape[1] // count, cut)
    stack[0:height, :] = own[:, at]
    stack[height:2 * height, :] = partner[:, at]
    for j in range(2, count):
        start = 0 if j == count - 1 else cut[0]
        stack[j * height:(j + 1) * height, :] = blocks[j - 2][:, start:start + cut[1]]
    turned[...] = jnp.swapaxes(stack[...], 0, 1)
    for r in range(pieces):
        wave = waves[:, r * width:(r + 1) * width]
        field = dot(turned[...], wave, NN)
        slope = (0.5 * jnp.tanh(0.5 * field) - 0.5).astype(jnp.bfloat16)
        part = dot(wave, slope, NT)
        if r > 0:
            part += acc[...]
        if r < pieces - 1:
            acc[...] = part
        else:
            for j in range(count):
                outs[j][...] = part[j * height:(j + 1) * height].astype(outs[j].dtype)


def data_kernel(count, cuts, split, *refs):
    halves, refs = (refs[:split], refs[split:2 * split]), refs[2 * split:]
    res_mine, res_other, table_mine, table_other, top_ref, low_ref, coef = refs[:7]
    refs = refs[7:]
    order = [(0, j) for j in range(count)] + [(t, j) for t in range(1, len(cuts)) for j in range(count)]
    ready = [key for key in order if key[0] == 0 or key[1] < 2]
    grads, refs = dict(zip(ready, refs)), refs[len(ready):]
    updated, residual_ref, later = refs[0], refs[1], refs[2:1 + len(cuts)]
    back_a, back_b, buf, sems, out_sems = refs[1 + len(cuts):]
    me, side, _ = position()
    half, rays, width = halves[0][0].shape
    block = coef.shape[1] // count
    own_width = residual_ref.shape[2]
    spots, copies = {}, {}
    for n, (t, j) in enumerate(order):
        if (t, j) in grads:
            spots[t, j] = buf.at[ready.index((t, j)), :, 0:cuts[t][1]]
        else:
            spots[t, j] = later[t - 1].at[j - 2]
        copies[t, j] = pltpu.make_async_copy(coef.at[:, columns(me ^ j, block, cuts[t])], spots[t, j], sems.at[n])
        copies[t, j].start()
    for back, parts, table in ((back_a, halves[0], table_mine), (back_b, halves[1], table_other)):
        for i in range(half):
            total = dot(table[i, :, aligned(me // 2 if split > 1 else 0, width)], parts[0][i], NT)
            for p in range(1, split):
                total += dot(table[i, :, aligned((me // 2) ^ p, width)], parts[p][i], NT)
            back[:, i * rays:(i + 1) * rays] = total.astype(jnp.bfloat16)
    writes = []
    for t, j in order:
        at = columns(me ^ j, block, cuts[t])
        grad = dot(back_a[...], top_ref[:, at], NN) + dot(back_b[...], low_ref[:, at], NN)
        copies[t, j].wait()
        spot = spots[t, j]
        if (t, j) in grads:
            spot[...] = spot[...] - 0.5 * grad - 0.5 * grads[t, j][...].astype(jnp.float32)
            writes.append(pltpu.make_async_copy(spot, updated.at[:, at], out_sems.at[len(writes)]))
            writes[-1].start()
        else:
            spot[...] = spot[...] - 0.5 * grad
    for q in range(2):
        @pl.when(side == q)
        def _():
            for i in range(half):
                residual_ref[side * half + i] = res_mine[i, :, q * own_width:(q + 1) * own_width]
                residual_ref[(1 - side) * half + i] = res_other[i, :, q * own_width:(q + 1) * own_width]
    for w in writes:
        w.wait()


def finish_kernel(count, cut, masks, later, *refs):
    grads = refs[:len(masks)]
    _, updated, buf, sems = refs[len(masks):]
    block = updated.shape[1] // count
    writes = []
    for n, j in enumerate(masks):
        buf[n] = later[j - 2] - 0.5 * grads[n][...].astype(jnp.float32)
        at = columns(position()[0] ^ j, block, cut)
        writes.append(pltpu.make_async_copy(buf.at[n], updated.at[:, at], sems.at[n]))
        writes[-1].start()
    for w in writes:
        w.wait()


def step_of(coefficients, measured, ray_voxels, ray_weights, angle_ids, angle_table, harmonics):
    coef_local, cols = coefficients.shape
    projections, _, rays, channels = measured.shape
    rows = projections * rays
    samples = ray_voxels.shape[2]
    count = lax.axis_size("coef")
    me = lax.axis_index("coef")
    half = projections // 2
    block = cols // count
    cuts = cuts_of(block)
    bf16, f32 = jnp.bfloat16, jnp.float32
    shape = jax.ShapeDtypeStruct

    def kernel(body_of, ins, outs, out_shape, scratch=(), grant=12, aliases={}):
        return pl.pallas_call(
            body_of,
            in_specs=ins,
            out_specs=outs,
            out_shape=out_shape,
            scratch_shapes=list(scratch),
            input_output_aliases=aliases,
            compiler_params=pltpu.CompilerParams(vmem_limit_bytes=grant << 20),
        )

    group_bits = 1 if lax.axis_size("groups") % 2 == 0 else 0
    slab_count = lax.axis_size("slab")
    slab_bits = 1 if slab_count % 2 == 0 else 0
    pieces = 1 << (group_bits + slab_bits)
    place = position()[2]
    width = harmonics.shape[1] // pieces
    rows_shape = (rows, samples)
    coef_far, measured_far, vox_far, wgt_far, ids_far, table_far = [
        pltpu.with_memory_space_constraint(v, pltpu.HBM)
        for v in (
            coefficients,
            measured.reshape(projections, rays, channels),
            ray_voxels.reshape(rows_shape),
            ray_weights.reshape(rows_shape),
            angle_ids,
            angle_table,
        )
    ]

    piece = lax.dynamic_slice_in_dim(harmonics, place * width, width, 1)
    fetched = {m: [swap(piece, "coef", m)] for m in range(2, count, 2)}
    table_shape = shape((half,) + angle_table.shape[1:], bf16)
    *parts, own, vox, wgt, table_mine, table_other = kernel(
        lambda *refs: prepare_kernel(count, cuts, *refs),
        [HBM] * 5,
        [VMEM] * (count + len(cuts) + 2),
        [shape((coef_local, block), bf16)] * (count - 3)
        + [shape((coef_local, cut[1]), bf16) for cut in cuts]
        + [shape((coef_local, cols), bf16)]
        + [shape((rows // 2, samples), jnp.int32)] * 2
        + [table_shape] * 2,
        [
            pltpu.VMEM((count, coef_local, block), f32),
            pltpu.SMEM(angle_ids.shape, jnp.int32),
            pltpu.SemaphoreType.DMA((count + 3 + projections,)),
        ],
    )(ids_far, coef_far, vox_far, wgt_far, table_far)
    received = []
    for t in range(len(cuts)):
        if t == 0:
            early = [swap(parts[m - 2], "coef", m) for m in range(2, count - 1)]
        received.append(early + [swap(parts[count - 3 + t], "coef", count - 1)])
    partner = swap(own, "coef", 1)
    near = swap(harmonics, "coef", 1)
    table_partner = swap(table_other, "coef", 1)
    moves = [(0, 1)] * slab_bits + [(1, 0)] * group_bits + [(1, 1)] * (slab_bits * group_bits)
    for m in fetched:
        for up, along in moves:
            total = lax.axis_size("groups") * slab_count
            pairs = [(i, (((i // slab_count) ^ up) * slab_count) + ((i % slab_count) ^ along)) for i in range(total)]
            fetched[m].append(lax.ppermute(fetched[m][0], ("groups", "slab"), pairs))

    top = kernel(
        build_kernel,
        [VMEM, VMEM],
        VMEM,
        shape((rows // 2, cols), bf16),
        [pltpu.VMEM((GROUP * cols // LANES, LANES), f32)],
    )(vox, wgt)
    low = swap(top, "coef", 1)
    for m in list(fetched):
        fetched[m ^ 1] = []
        for value in fetched[m]:
            fetched[m ^ 1].append(swap(value, "coef", 1))
    far = [v for m in range(2, count) for v in fetched[m]]

    total, send = kernel(
        lambda *refs: sums_kernel(count, *refs),
        [VMEM] * 5 + [HBM],
        [VMEM, VMEM],
        [shape((half, rays, channels // 2), f32)] * 2,
        [pltpu.VMEM((half, rays, channels), f32), pltpu.SemaphoreType.DMA(())],
    )(top, own, partner, table_mine, table_partner, measured_far)

    masks = [1 << n for n in range(1, count.bit_length() - 1)]
    for mask in masks[::-1]:
        if mask < count // 2:
            width = total.shape[2] // 2
            bit = jnp.where((me & mask) == 0, 0, 1)
            send = lax.dynamic_slice_in_dim(total, (1 - bit) * width, width, 2)
            total = lax.dynamic_slice_in_dim(total, bit * width, width, 2)
        total = total + swap(send, "coef", mask)

    wide = shape((count * coef_local, harmonics.shape[1]), bf16)
    waves = kernel(
        lambda *refs: stack_kernel(pieces, *refs), [VMEM] * (2 + len(far)), VMEM, wide
    )(harmonics, near, *far)

    returned = []
    for t, cut in enumerate(cuts):
        first = t == 0
        outs = kernel(
            lambda *refs: penalty_kernel(count, pieces, cut, *refs),
            [VMEM] * (count + 1),
            [VMEM] * count,
            [shape((coef_local, cut[1]), bf16)] * count,
            [
                pltpu.VMEM((count * coef_local, cut[1]), bf16),
                pltpu.VMEM((cut[1], count * coef_local), bf16),
                pltpu.VMEM((count * coef_local, cut[1]), f32),
            ],
        )(waves, own, partner, *received[t])
        back = [outs[0]]
        for m in range(1, count):
            back.append(swap(outs[m], "coef", m))
        returned.append(back)
        if first:
            half_mine = [total.astype(bf16)]
            for mask in masks:
                other = [swap(v, "coef", mask) for v in half_mine]
                if total.shape[2] % LANES == 0:
                    half_mine = half_mine + other
                    continue
                low_bit, pair = (me & mask) == 0, (half_mine[0], other[0])
                ordered = [jnp.where(low_bit, *pair), jnp.where(low_bit, *pair[::-1])]
                half_mine = [jnp.concatenate(ordered, 2)]
    res_other = swap(total, "coef", 1)
    half_other = [swap(v, "coef", 1) for v in half_mine]

    ready = [(t, j) for t in range(len(cuts)) for j in range(count) if t == 0 or j < 2]
    updated, residual, *later = kernel(
        lambda *refs: data_kernel(count, cuts, len(half_mine), *refs),
        [VMEM] * (2 * len(half_mine) + 6) + [HBM] + [VMEM] * len(ready),
        [HBM] + [VMEM] * len(cuts),
        [shape((coef_local, cols), f32), shape((projections, rays, channels // count), f32)]
        + [shape((count - 2, coef_local, cut[1]), f32) for cut in cuts[1:]],
        [
            pltpu.VMEM((coef_local, rows // 2), bf16),
            pltpu.VMEM((coef_local, rows // 2), bf16),
            pltpu.VMEM((len(ready), coef_local, max(cut[1] for cut in cuts)), f32),
            pltpu.SemaphoreType.DMA((len(cuts) * count,)),
            pltpu.SemaphoreType.DMA((len(ready),)),
        ],
    )(
        *half_mine,
        *half_other,
        total,
        res_other,
        table_mine,
        table_other,
        top,
        low,
        coef_far,
        *[returned[t][j] for t, j in ready],
    )
    remote = list(range(2, count))
    middle = len(remote) // 2
    for t, cut in list(enumerate(cuts))[1:]:
        for masks in (remote[:middle], remote[middle:]):
            if not masks:
                continue
            updated = kernel(
                lambda *refs: finish_kernel(count, cut, masks, *refs),
                [VMEM] * (len(masks) + 1) + [HBM],
                HBM,
                shape((coef_local, cols), f32),
                [pltpu.VMEM((len(masks), coef_local, cut[1]), f32), pltpu.SemaphoreType.DMA((len(masks),))],
                aliases={len(masks) + 1: 0},
            )(later[t - 1], *[returned[t][m] for m in masks], updated)
    return (updated, residual[:, None])


def solution(mesh):
    in_specs = (
        P("coef", ("groups", "slab")),
        P("groups", "slab", None, None),
        P(),
        P(),
        P(),
        P(None, "coef", None),
        P("coef", None),
    )
    out_specs = (P("coef", ("groups", "slab")), P("groups", "slab", None, "coef"))
    return jax.shard_map(step_of, mesh=mesh, in_specs=in_specs, out_specs=out_specs, check_vma=False)
```

```python
import jax
import jax.numpy as jnp
from jax import lax
from jax.experimental import pallas as pl
from jax.experimental.pallas import tpu as pltpu
from jax.sharding import PartitionSpec as P


LANES = 128
EIGHTHS = (3, 3, 2)
GROUP = 32
NT = (((1,), (1,)), ((), ()))
NN = (((1,), (0,)), ((), ()))
VMEM = pl.BlockSpec(memory_space=pltpu.VMEM)
HBM = pl.BlockSpec(memory_space=pltpu.HBM)


def dot(a, b, dims):
    return lax.dot_general(a, b, dims, preferred_element_type=jnp.float32)


def swap(value, axis, mask):
    count = lax.axis_size(axis)
    return lax.ppermute(value, axis, [(i, i ^ mask) for i in range(count)])


def aligned(index, width):
    return pl.ds(pl.multiple_of(index * width, width), width)


def cuts_of(block):
    if block % (8 * LANES):
        return [(0, block)]
    unit = block // 8
    starts = [unit * sum(EIGHTHS[:t]) for t in range(len(EIGHTHS))]
    return [(start, unit * size) for start, size in zip(starts, EIGHTHS)]


def sides_of(cuts):
    total = cuts[-1][0] + cuts[-1][1]
    return [cuts[0]] + [(cuts[0][1], total - cuts[0][1])] * (len(cuts) > 1)


def position():
    me = lax.axis_index("coef")
    place = jnp.zeros((), jnp.int32)
    for axis in ("groups", "slab"):
        if lax.axis_size(axis) % 2 == 0:
            place = place * 2 + (lax.axis_index(axis) & 1)
    return me, me & 1, place


def columns(index, block, cut):
    return pl.ds(pl.multiple_of(index * block + cut[0], LANES), cut[1])


def prepare_kernel(count, cuts, ids_far, coef, vox, wgt, table, *refs):
    full, parts = refs[:count - 3], refs[count - 3:count - 3 + len(cuts)]
    whole, vox_out, wgt_out, table_mine, table_other, stage, ids, sems = refs[count - 3 + len(cuts):]
    me, side, _ = position()
    block = coef.shape[1] // count
    half_rows, half = vox_out.shape[0], table_mine.shape[0]
    order = list(range(2, count)) + [1, 0]
    copies = {}
    for m in order:
        copies[m] = pltpu.make_async_copy(coef.at[:, aligned(me ^ m, block)], stage.at[m], sems.at[m])
    rest = [
        pltpu.make_async_copy(vox.at[aligned(side, half_rows)], vox_out, sems.at[count]),
        pltpu.make_async_copy(wgt.at[aligned(side, half_rows)], wgt_out, sems.at[count + 1]),
    ]
    numbers = pltpu.make_async_copy(ids_far, ids, sems.at[count + 2 + 2 * half])
    numbers.start()
    for m in order:
        copies[m].start()
    numbers.wait()
    for n, (out, first) in enumerate(((table_other, (1 - side) * half), (table_mine, side * half))):
        for i in range(half):
            rest.append(pltpu.make_async_copy(table.at[ids[first + i]], out.at[i], sems.at[count + 2 + n * half + i]))
    for c in rest:
        c.start()
    for m in order:
        copies[m].wait()
        values = stage[m].astype(jnp.bfloat16)
        whole[:, aligned(me ^ m, block)] = values
        if 1 < m < count - 1:
            full[m - 2][...] = values
        if m == count - 1:
            for t, cut in enumerate(cuts):
                parts[t][...] = values[:, cut[0]:cut[0] + cut[1]]
    for c in rest:
        c.wait()


def build_kernel(vox_ref, wgt_ref, matrix_ref, tile_ref):
    rows, samples = vox_ref.shape
    cols = matrix_ref.shape[1]
    high_count = cols // LANES
    low_pos = lax.broadcasted_iota(jnp.int32, (LANES, samples), 0)
    high_pos = lax.broadcasted_iota(jnp.int32, (high_count, samples), 0)
    blank = jnp.zeros((high_count, samples), jnp.bfloat16)

    def build(step, carry):
        first = pl.multiple_of(step * GROUP, GROUP)
        vox = vox_ref[pl.ds(first, GROUP), :]
        wgt = wgt_ref[pl.ds(first, GROUP), :].astype(jnp.float32) * (1.0 / 256.0)
        low = vox & (LANES - 1)
        high = lax.shift_right_logical(vox, LANES.bit_length() - 1)
        hots = []
        for i in range(GROUP):
            low_hot = (low_pos == low[i:i + 1]).astype(jnp.float32).astype(jnp.bfloat16)
            high_hot = jnp.where(high_pos == high[i:i + 1], wgt[i:i + 1], 0.0).astype(jnp.bfloat16)
            hots.append((low_hot, high_hot))
        for i in range(0, GROUP, 2):
            (low_a, high_a), (low_b, high_b) = hots[i:i + 2]
            left = jnp.concatenate([jnp.concatenate([high_a, blank], 1), jnp.concatenate([blank, high_b], 1)], 0)
            right = jnp.concatenate([low_a, low_b], 1)
            tile_ref[i * high_count:(i + 2) * high_count, :] = dot(left, right, NT)
        for h in range(high_count):
            part = tile_ref[pl.ds(h, GROUP, stride=high_count), :]
            matrix_ref[pl.ds(first, GROUP), h * LANES:(h + 1) * LANES] = part.astype(jnp.bfloat16)
        return carry

    lax.fori_loop(0, rows // GROUP, build, 0)


def sums_kernel(count, matrix_ref, own, partner, table_own, table_partner, measured, keep, send, target, sem):
    half, rays, width = keep.shape
    me, side, _ = position()
    fetch = pltpu.make_async_copy(measured.at[pl.ds(side * half, half)], target, sem)
    fetch.start()
    sums_own = dot(matrix_ref[...], own[...], NT).astype(jnp.bfloat16)
    sums_partner = dot(matrix_ref[...], partner[...], NT).astype(jnp.bfloat16)
    fetch.wait()
    high = (me // (count // 2)) & 1
    for i in range(half):
        rows = slice(i * rays, (i + 1) * rays)
        for out, bit in ((send, 1 - high), (keep, high)):
            at = aligned(bit, width)
            total = dot(sums_own[rows], table_own[i, :, at], NN) + dot(sums_partner[rows], table_partner[i, :, at], NN)
            out[i] = total - (2.0 / count) * target[i, :, at]


def stack_kernel(pieces, own, near, *refs):
    far, waves = refs[:-1], refs[-1]
    place = position()[2]
    height = near.shape[0]
    width = waves.shape[1] // pieces
    for r in range(pieces):
        span = slice(r * width, (r + 1) * width)
        waves[0:height, span] = own[:, aligned(place ^ r, width)]
        waves[height:2 * height, span] = near[:, aligned(place ^ r, width)]
        for j in range(len(far) // pieces):
            waves[(j + 2) * height:(j + 3) * height, span] = far[j * pieces + r][...]


def penalty_kernel(count, pieces, cut, skip, waves, own, partner, *refs):
    blocks, outs = refs[:count - 2], refs[count - 2:2 * count - 2]
    stack, turned, acc = refs[2 * count - 2:]
    height = outs[0].shape[0]
    width = waves.shape[1] // pieces
    at = columns(position()[0], own.shape[1] // count, cut)
    stack[0:height, :] = own[:, at]
    stack[height:2 * height, :] = partner[:, at]
    for j in range(2, count):
        start = cut[0] - (skip if j == count - 1 else 0)
        stack[j * height:(j + 1) * height, :] = blocks[j - 2][:, start:start + cut[1]]
    turned[...] = jnp.swapaxes(stack[...], 0, 1)
    for r in range(pieces):
        wave = waves[:, r * width:(r + 1) * width]
        field = dot(turned[...], wave, NN)
        slope = (0.5 * jnp.tanh(0.5 * field) - 0.5).astype(jnp.bfloat16)
        part = dot(wave, slope, NT)
        if r > 0:
            part += acc[...]
        if r < pieces - 1:
            acc[...] = part
        else:
            for j in range(count):
                outs[j][...] = part[j * height:(j + 1) * height].astype(outs[j].dtype)


def data_kernel(count, cuts, split, *refs):
    halves, refs = (refs[:split], refs[split:2 * split]), refs[2 * split:]
    res_mine, res_other, table_mine, table_other, top_ref, low_ref, coef = refs[:7]
    refs = refs[7:]
    order = [(0, j) for j in range(count)] + [(t, j) for t in range(1, len(cuts)) for j in range(count)]
    ready = [key for key in order if key[0] == 0 or key[1] < 2]
    grads, refs = dict(zip(ready, refs)), refs[len(ready):]
    updated, residual_ref, later = refs[0], refs[1], refs[2:1 + len(cuts)]
    back_a, back_b, buf, sems, out_sems = refs[1 + len(cuts):]
    me, side, _ = position()
    half, rays, width = halves[0][0].shape
    block = coef.shape[1] // count
    own_width = residual_ref.shape[2]
    spots, copies = {}, {}
    for n, (t, j) in enumerate(order):
        if (t, j) in grads:
            spots[t, j] = buf.at[ready.index((t, j)), :, 0:cuts[t][1]]
        else:
            spots[t, j] = later[t - 1].at[j - 2]
        copies[t, j] = pltpu.make_async_copy(coef.at[:, columns(me ^ j, block, cuts[t])], spots[t, j], sems.at[n])
        copies[t, j].start()
    for back, parts, table in ((back_a, halves[0], table_mine), (back_b, halves[1], table_other)):
        for i in range(half):
            total = dot(table[i, :, aligned(me // 2 if split > 1 else 0, width)], parts[0][i], NT)
            for p in range(1, split):
                total += dot(table[i, :, aligned((me // 2) ^ p, width)], parts[p][i], NT)
            back[:, i * rays:(i + 1) * rays] = total.astype(jnp.bfloat16)
    writes = []
    for t, j in order:
        at = columns(me ^ j, block, cuts[t])
        grad = dot(back_a[...], top_ref[:, at], NN) + dot(back_b[...], low_ref[:, at], NN)
        copies[t, j].wait()
        spot = spots[t, j]
        if (t, j) in grads:
            spot[...] = spot[...] - 0.5 * grad - 0.5 * grads[t, j][...].astype(jnp.float32)
            writes.append(pltpu.make_async_copy(spot, updated.at[:, at], out_sems.at[len(writes)]))
            writes[-1].start()
        else:
            spot[...] = spot[...] - 0.5 * grad
    for q in range(2):
        @pl.when(side == q)
        def _():
            for i in range(half):
                residual_ref[side * half + i] = res_mine[i, :, q * own_width:(q + 1) * own_width]
                residual_ref[(1 - side) * half + i] = res_other[i, :, q * own_width:(q + 1) * own_width]
    for w in writes:
        w.wait()


def finish_kernel(count, cut, masks, later, *refs):
    grads = refs[:len(masks)]
    _, updated, buf, sems = refs[len(masks):]
    block = updated.shape[1] // count
    writes = []
    for n, j in enumerate(masks):
        buf[n] = later[j - 2] - 0.5 * grads[n][...].astype(jnp.float32)
        at = columns(position()[0] ^ j, block, cut)
        writes.append(pltpu.make_async_copy(buf.at[n], updated.at[:, at], sems.at[n]))
        writes[-1].start()
    for w in writes:
        w.wait()


def step_of(coefficients, measured, ray_voxels, ray_weights, angle_ids, angle_table, harmonics):
    coef_local, cols = coefficients.shape
    projections, _, rays, channels = measured.shape
    rows = projections * rays
    samples = ray_voxels.shape[2]
    count = lax.axis_size("coef")
    me = lax.axis_index("coef")
    half = projections // 2
    block = cols // count
    cuts = cuts_of(block)
    sides = sides_of(cuts)
    bf16, f32 = jnp.bfloat16, jnp.float32
    shape = jax.ShapeDtypeStruct

    def kernel(body_of, ins, outs, out_shape, scratch=(), grant=12, aliases={}):
        return pl.pallas_call(
            body_of,
            in_specs=ins,
            out_specs=outs,
            out_shape=out_shape,
            scratch_shapes=list(scratch),
            input_output_aliases=aliases,
            compiler_params=pltpu.CompilerParams(vmem_limit_bytes=grant << 20),
        )

    group_bits = 1 if lax.axis_size("groups") % 2 == 0 else 0
    slab_count = lax.axis_size("slab")
    slab_bits = 1 if slab_count % 2 == 0 else 0
    pieces = 1 << (group_bits + slab_bits)
    place = position()[2]
    width = harmonics.shape[1] // pieces
    rows_shape = (rows, samples)
    coef_far, measured_far, vox_far, wgt_far, ids_far, table_far = [
        pltpu.with_memory_space_constraint(v, pltpu.HBM)
        for v in (
            coefficients,
            measured.reshape(projections, rays, channels),
            ray_voxels.reshape(rows_shape),
            ray_weights.reshape(rows_shape),
            angle_ids,
            angle_table,
        )
    ]

    piece = lax.dynamic_slice_in_dim(harmonics, place * width, width, 1)
    fetched = {m: [swap(piece, "coef", m)] for m in range(2, count, 2)}
    table_shape = shape((half,) + angle_table.shape[1:], bf16)
    *parts, own, vox, wgt, table_mine, table_other = kernel(
        lambda *refs: prepare_kernel(count, sides, *refs),
        [HBM] * 5,
        [VMEM] * (count + len(sides) + 2),
        [shape((coef_local, block), bf16)] * (count - 3)
        + [shape((coef_local, cut[1]), bf16) for cut in sides]
        + [shape((coef_local, cols), bf16)]
        + [shape((rows // 2, samples), jnp.int32)] * 2
        + [table_shape] * 2,
        [
            pltpu.VMEM((count, coef_local, block), f32),
            pltpu.SMEM(angle_ids.shape, jnp.int32),
            pltpu.SemaphoreType.DMA((count + 3 + projections,)),
        ],
    )(ids_far, coef_far, vox_far, wgt_far, table_far)
    received = []
    for t in range(len(sides)):
        if t == 0:
            early = [swap(parts[m - 2], "coef", m) for m in range(2, count - 1)]
        received.append(early + [swap(parts[count - 3 + t], "coef", count - 1)])
    partner = swap(own, "coef", 1)
    near = swap(harmonics, "coef", 1)
    table_partner = swap(table_other, "coef", 1)
    moves = [(0, 1)] * slab_bits + [(1, 0)] * group_bits + [(1, 1)] * (slab_bits * group_bits)
    for m in fetched:
        for up, along in moves:
            total = lax.axis_size("groups") * slab_count
            pairs = [(i, (((i // slab_count) ^ up) * slab_count) + ((i % slab_count) ^ along)) for i in range(total)]
            fetched[m].append(lax.ppermute(fetched[m][0], ("groups", "slab"), pairs))

    top = kernel(
        build_kernel,
        [VMEM, VMEM],
        VMEM,
        shape((rows // 2, cols), bf16),
        [pltpu.VMEM((GROUP * cols // LANES, LANES), f32)],
    )(vox, wgt)
    low = swap(top, "coef", 1)
    for m in list(fetched):
        fetched[m ^ 1] = [swap(v, "coef", 1) for v in fetched[m]]
    far = [v for m in range(2, count) for v in fetched[m]]

    total, send = kernel(
        lambda *refs: sums_kernel(count, *refs),
        [VMEM] * 5 + [HBM],
        [VMEM, VMEM],
        [shape((half, rays, channels // 2), f32)] * 2,
        [pltpu.VMEM((half, rays, channels), f32), pltpu.SemaphoreType.DMA(())],
    )(top, own, partner, table_mine, table_partner, measured_far)

    masks = [1 << n for n in range(1, count.bit_length() - 1)]
    for mask in masks[::-1]:
        if mask < count // 2:
            width = total.shape[2] // 2
            bit = jnp.where((me & mask) == 0, 0, 1)
            send = lax.dynamic_slice_in_dim(total, (1 - bit) * width, width, 2)
            total = lax.dynamic_slice_in_dim(total, bit * width, width, 2)
        total = total + swap(send, "coef", mask)

    wide = shape((count * coef_local, harmonics.shape[1]), bf16)
    waves = kernel(
        lambda *refs: stack_kernel(pieces, *refs), [VMEM] * (2 + len(far)), VMEM, wide
    )(harmonics, near, *far)

    returned = []
    for t, cut in enumerate(cuts):
        first = t == 0
        outs = kernel(
            lambda *refs: penalty_kernel(count, pieces, cut, sides[min(t, 1)][0], *refs),
            [VMEM] * (count + 1),
            [VMEM] * count,
            [shape((coef_local, cut[1]), bf16)] * count,
            [
                pltpu.VMEM((count * coef_local, cut[1]), bf16),
                pltpu.VMEM((cut[1], count * coef_local), bf16),
                pltpu.VMEM((count * coef_local, cut[1]), f32),
            ],
        )(waves, own, partner, *received[min(t, 1)])
        back = [outs[0]]
        for m in range(1, count):
            back.append(swap(outs[m], "coef", m))
        returned.append(back)
        if first:
            half_mine = [total.astype(bf16)]
            for mask in masks:
                other = [swap(v, "coef", mask) for v in half_mine]
                if total.shape[2] % LANES == 0:
                    half_mine = half_mine + other
                    continue
                low_bit, pair = (me & mask) == 0, (half_mine[0], other[0])
                ordered = [jnp.where(low_bit, *pair), jnp.where(low_bit, *pair[::-1])]
                half_mine = [jnp.concatenate(ordered, 2)]
    res_other = swap(total, "coef", 1)
    half_other = [swap(v, "coef", 1) for v in half_mine]

    ready = [(t, j) for t in range(len(cuts)) for j in range(count) if t == 0 or j < 2]
    updated, residual, *later = kernel(
        lambda *refs: data_kernel(count, cuts, len(half_mine), *refs),
        [VMEM] * (2 * len(half_mine) + 6) + [HBM] + [VMEM] * len(ready),
        [HBM] + [VMEM] * len(cuts),
        [shape((coef_local, cols), f32), shape((projections, rays, channels // count), f32)]
        + [shape((count - 2, coef_local, cut[1]), f32) for cut in cuts[1:]],
        [
            pltpu.VMEM((coef_local, rows // 2), bf16),
            pltpu.VMEM((coef_local, rows // 2), bf16),
            pltpu.VMEM((len(ready), coef_local, max(cut[1] for cut in cuts)), f32),
            pltpu.SemaphoreType.DMA((len(cuts) * count,)),
            pltpu.SemaphoreType.DMA((len(ready),)),
        ],
    )(
        *half_mine,
        *half_other,
        total,
        res_other,
        table_mine,
        table_other,
        top,
        low,
        coef_far,
        *[returned[t][j] for t, j in ready],
    )
    remote = list(range(2, count))
    middle = len(remote) // 2
    for t, cut in list(enumerate(cuts))[1:]:
        for masks in (remote[:middle], remote[middle:]):
            if not masks:
                continue
            updated = kernel(
                lambda *refs: finish_kernel(count, cut, masks, *refs),
                [VMEM] * (len(masks) + 1) + [HBM],
                HBM,
                shape((coef_local, cols), f32),
                [pltpu.VMEM((len(masks), coef_local, cut[1]), f32), pltpu.SemaphoreType.DMA((len(masks),))],
                aliases={len(masks) + 1: 0},
            )(later[t - 1], *[returned[t][m] for m in masks], updated)
    return (updated, residual[:, None])


def solution(mesh):
    in_specs = (
        P("coef", ("groups", "slab")),
        P("groups", "slab", None, None),
        P(),
        P(),
        P(),
        P(None, "coef", None),
        P("coef", None),
    )
    out_specs = (P("coef", ("groups", "slab")), P("groups", "slab", None, "coef"))
    return jax.shard_map(step_of, mesh=mesh, in_specs=in_specs, out_specs=out_specs, check_vma=False)
```

```python
import jax
import jax.numpy as jnp
from jax import lax
from jax.experimental import pallas as pl
from jax.experimental.pallas import tpu as pltpu
from jax.sharding import PartitionSpec as P


LANES = 128
QUARTERS = (2, 2)
GROUP = 64
NT = (((1,), (1,)), ((), ()))
NN = (((1,), (0,)), ((), ()))
VMEM = pl.BlockSpec(memory_space=pltpu.VMEM)
HBM = pl.BlockSpec(memory_space=pltpu.HBM)


def dot(a, b, dims):
    return lax.dot_general(a, b, dims, preferred_element_type=jnp.float32)


def swap(value, axis, mask):
    count = lax.axis_size(axis)
    return lax.ppermute(value, axis, [(i, i ^ mask) for i in range(count)])


def aligned(index, width):
    return pl.ds(pl.multiple_of(index * width, width), width)


def cuts_of(block):
    if block % (4 * LANES):
        return [(0, block)]
    unit = block // 4
    starts = [unit * sum(QUARTERS[:t]) for t in range(len(QUARTERS))]
    return [(start, unit * size) for start, size in zip(starts, QUARTERS)]


def position():
    me = lax.axis_index("coef")
    place = jnp.zeros((), jnp.int32)
    for axis in ("groups", "slab"):
        if lax.axis_size(axis) % 2 == 0:
            place = place * 2 + (lax.axis_index(axis) & 1)
    return me, me & 1, place


def columns(index, block, cut):
    return pl.ds(pl.multiple_of(index * block + cut[0], LANES), cut[1])


def prepare_kernel(count, cuts, ids_far, coef, vox, wgt, table, *refs):
    full, parts = refs[:count - 3], refs[count - 3:count - 3 + len(cuts)]
    whole, vox_out, wgt_out, table_mine, table_other, stage, ids, sems = refs[count - 3 + len(cuts):]
    me, side, _ = position()
    block = coef.shape[1] // count
    half_rows, half = vox_out.shape[0], table_mine.shape[0]
    order = list(range(2, count)) + [1, 0]
    copies = {}
    for m in order:
        copies[m] = pltpu.make_async_copy(coef.at[:, aligned(me ^ m, block)], stage.at[m], sems.at[m])
    rest = [
        pltpu.make_async_copy(vox.at[aligned(side, half_rows)], vox_out, sems.at[count]),
        pltpu.make_async_copy(wgt.at[aligned(side, half_rows)], wgt_out, sems.at[count + 1]),
    ]
    numbers = pltpu.make_async_copy(ids_far, ids, sems.at[count + 2 + 2 * half])
    numbers.start()
    for m in order:
        copies[m].start()
    numbers.wait()
    for n, (out, first) in enumerate(((table_other, (1 - side) * half), (table_mine, side * half))):
        for i in range(half):
            rest.append(pltpu.make_async_copy(table.at[ids[first + i]], out.at[i], sems.at[count + 2 + n * half + i]))
    for c in rest:
        c.start()
    for m in order:
        copies[m].wait()
        values = stage[m].astype(jnp.bfloat16)
        whole[:, aligned(me ^ m, block)] = values
        if 1 < m < count - 1:
            full[m - 2][...] = values
        if m == count - 1:
            for t, cut in enumerate(cuts):
                parts[t][...] = values[:, cut[0]:cut[0] + cut[1]]
    for c in rest:
        c.wait()


def build_kernel(vox_ref, wgt_ref, matrix_ref, tile_ref):
    rows, samples = vox_ref.shape
    cols = matrix_ref.shape[1]
    high_count = cols // LANES
    low_pos = lax.broadcasted_iota(jnp.int32, (LANES, samples), 0)
    high_pos = lax.broadcasted_iota(jnp.int32, (high_count, samples), 0)
    blank = jnp.zeros((high_count, samples), jnp.bfloat16)

    def build(step, carry):
        first = pl.multiple_of(step * GROUP, GROUP)
        vox = vox_ref[pl.ds(first, GROUP), :]
        wgt = wgt_ref[pl.ds(first, GROUP), :].astype(jnp.float32) * (1.0 / 256.0)
        low = vox & (LANES - 1)
        high = lax.shift_right_logical(vox, LANES.bit_length() - 1)
        hots = []
        for i in range(GROUP):
            low_hot = (low_pos == low[i:i + 1]).astype(jnp.float32).astype(jnp.bfloat16)
            high_hot = jnp.where(high_pos == high[i:i + 1], wgt[i:i + 1], 0.0).astype(jnp.bfloat16)
            hots.append((low_hot, high_hot))
        for i in range(0, GROUP, 2):
            (low_a, high_a), (low_b, high_b) = hots[i:i + 2]
            left = jnp.concatenate([jnp.concatenate([high_a, blank], 1), jnp.concatenate([blank, high_b], 1)], 0)
            right = jnp.concatenate([low_a, low_b], 1)
            tile_ref[i * high_count:(i + 2) * high_count, :] = dot(left, right, NT)
        for h in range(high_count):
            part = tile_ref[pl.ds(h, GROUP, stride=high_count), :]
            matrix_ref[pl.ds(first, GROUP), h * LANES:(h + 1) * LANES] = part.astype(jnp.bfloat16)
        return carry

    lax.fori_loop(0, rows // GROUP, build, 0)


def sums_kernel(count, matrix_ref, own, partner, table_own, table_partner, measured, keep, send, target, sem):
    half, rays, width = keep.shape
    me, side, _ = position()
    fetch = pltpu.make_async_copy(measured.at[pl.ds(side * half, half)], target, sem)
    fetch.start()
    sums_own = dot(matrix_ref[...], own[...], NT).astype(jnp.bfloat16)
    sums_partner = dot(matrix_ref[...], partner[...], NT).astype(jnp.bfloat16)
    fetch.wait()
    high = (me // (count // 2)) & 1
    for i in range(half):
        rows = slice(i * rays, (i + 1) * rays)
        for out, bit in ((send, 1 - high), (keep, high)):
            at = aligned(bit, width)
            total = dot(sums_own[rows], table_own[i, :, at], NN) + dot(sums_partner[rows], table_partner[i, :, at], NN)
            out[i] = total - (2.0 / count) * target[i, :, at]


def penalty_kernel(count, pieces, cut, first, own, partner, *refs):
    blocks, refs = refs[:count - 2], refs[count - 2:]
    if first:
        harm, near, far = refs[0], refs[1], refs[2:2 + (count - 2) * pieces]
        outs, waves, refs = refs[2 + len(far):][:count], refs[2 + len(far) + count], refs[3 + len(far) + count:]
    else:
        waves, outs, refs = refs[0], refs[1:count + 1], refs[count + 1:]
    stack, turned, acc = refs
    me, _, place = position()
    height = outs[0].shape[0]
    width = waves.shape[1] // pieces
    at = columns(me, own.shape[1] // count, cut)
    stack[0:height, :] = own[:, at]
    stack[height:2 * height, :] = partner[:, at]
    for j in range(2, count):
        start = 0 if j == count - 1 else cut[0]
        stack[j * height:(j + 1) * height, :] = blocks[j - 2][:, start:start + cut[1]]
    turned[...] = jnp.swapaxes(stack[...], 0, 1)
    for r in range(pieces):
        span = slice(r * width, (r + 1) * width)
        if first:
            waves[0:height, span] = harm[:, aligned(place ^ r, width)]
            waves[height:2 * height, span] = near[:, aligned(place ^ r, width)]
            for j in range(2, count):
                waves[j * height:(j + 1) * height, span] = far[(j - 2) * pieces + r][...]
        wave = waves[:, span]
        field = dot(turned[...], wave, NN)
        slope = (0.5 * jnp.tanh(0.5 * field) - 0.5).astype(jnp.bfloat16)
        part = dot(wave, slope, NT)
        if r > 0:
            part += acc[...]
        if r < pieces - 1:
            acc[...] = part
        else:
            for j in range(count):
                outs[j][...] = part[j * height:(j + 1) * height].astype(outs[j].dtype)


def data_kernel(count, cuts, split, *refs):
    halves, refs = (refs[:split], refs[split:2 * split]), refs[2 * split:]
    res_mine, res_other, table_mine, table_other, top_ref, low_ref, coef = refs[:7]
    refs = refs[7:]
    order = [(0, j) for j in range(count)] + [(t, j) for t in range(1, len(cuts)) for j in range(count)]
    ready = [key for key in order if key[0] == 0 or key[1] < 2]
    grads, refs = dict(zip(ready, refs)), refs[len(ready):]
    updated, residual_ref, later = refs[0], refs[1], refs[2:1 + len(cuts)]
    back_a, back_b, buf, sems, out_sems = refs[1 + len(cuts):]
    me, side, _ = position()
    half, rays, width = halves[0][0].shape
    block = coef.shape[1] // count
    own_width = residual_ref.shape[2]
    spots, copies = {}, {}
    for n, (t, j) in enumerate(order):
        if (t, j) in grads:
            spots[t, j] = buf.at[ready.index((t, j)), :, 0:cuts[t][1]]
        else:
            spots[t, j] = later[t - 1].at[j - 2]
        copies[t, j] = pltpu.make_async_copy(coef.at[:, columns(me ^ j, block, cuts[t])], spots[t, j], sems.at[n])
        copies[t, j].start()
    for back, parts, table in ((back_a, halves[0], table_mine), (back_b, halves[1], table_other)):
        for i in range(half):
            total = dot(table[i, :, aligned(me // 2 if split > 1 else 0, width)], parts[0][i], NT)
            for p in range(1, split):
                total += dot(table[i, :, aligned((me // 2) ^ p, width)], parts[p][i], NT)
            back[:, i * rays:(i + 1) * rays] = total.astype(jnp.bfloat16)
    writes = []
    for t, j in order:
        at = columns(me ^ j, block, cuts[t])
        grad = dot(back_a[...], top_ref[:, at], NN) + dot(back_b[...], low_ref[:, at], NN)
        copies[t, j].wait()
        spot = spots[t, j]
        if (t, j) in grads:
            spot[...] = spot[...] - 0.5 * grad - 0.5 * grads[t, j][...].astype(jnp.float32)
            writes.append(pltpu.make_async_copy(spot, updated.at[:, at], out_sems.at[len(writes)]))
            writes[-1].start()
        else:
            spot[...] = spot[...] - 0.5 * grad
    for q in range(2):
        @pl.when(side == q)
        def _():
            for i in range(half):
                residual_ref[side * half + i] = res_mine[i, :, q * own_width:(q + 1) * own_width]
                residual_ref[(1 - side) * half + i] = res_other[i, :, q * own_width:(q + 1) * own_width]
    for w in writes:
        w.wait()


def finish_kernel(count, cut, masks, later, *refs):
    grads = refs[:len(masks)]
    _, updated, buf, sems = refs[len(masks):]
    block = updated.shape[1] // count
    writes = []
    for n, j in enumerate(masks):
        buf[n] = later[j - 2] - 0.5 * grads[n][...].astype(jnp.float32)
        at = columns(position()[0] ^ j, block, cut)
        writes.append(pltpu.make_async_copy(buf.at[n], updated.at[:, at], sems.at[n]))
        writes[-1].start()
    for w in writes:
        w.wait()


def step_of(coefficients, measured, ray_voxels, ray_weights, angle_ids, angle_table, harmonics):
    coef_local, cols = coefficients.shape
    projections, _, rays, channels = measured.shape
    rows = projections * rays
    samples = ray_voxels.shape[2]
    count = lax.axis_size("coef")
    me = lax.axis_index("coef")
    half = projections // 2
    block = cols // count
    cuts = cuts_of(block)
    bf16, f32 = jnp.bfloat16, jnp.float32
    shape = jax.ShapeDtypeStruct

    def kernel(body_of, ins, outs, out_shape, scratch=(), grant=12, aliases={}):
        return pl.pallas_call(
            body_of,
            in_specs=ins,
            out_specs=outs,
            out_shape=out_shape,
            scratch_shapes=list(scratch),
            input_output_aliases=aliases,
            compiler_params=pltpu.CompilerParams(vmem_limit_bytes=grant << 20),
        )

    group_bits = 1 if lax.axis_size("groups") % 2 == 0 else 0
    slab_count = lax.axis_size("slab")
    slab_bits = 1 if slab_count % 2 == 0 else 0
    pieces = 1 << (group_bits + slab_bits)
    place = position()[2]
    width = harmonics.shape[1] // pieces
    rows_shape = (rows, samples)
    coef_far, measured_far, vox_far, wgt_far, ids_far, table_far = [
        pltpu.with_memory_space_constraint(v, pltpu.HBM)
        for v in (
            coefficients,
            measured.reshape(projections, rays, channels),
            ray_voxels.reshape(rows_shape),
            ray_weights.reshape(rows_shape),
            angle_ids,
            angle_table,
        )
    ]

    piece = lax.dynamic_slice_in_dim(harmonics, place * width, width, 1)
    fetched = {m: [swap(piece, "coef", m)] for m in range(2, count, 2)}
    table_shape = shape((half,) + angle_table.shape[1:], bf16)
    *parts, own, vox, wgt, table_mine, table_other = kernel(
        lambda *refs: prepare_kernel(count, cuts, *refs),
        [HBM] * 5,
        [VMEM] * (count + len(cuts) + 2),
        [shape((coef_local, block), bf16)] * (count - 3)
        + [shape((coef_local, cut[1]), bf16) for cut in cuts]
        + [shape((coef_local, cols), bf16)]
        + [shape((rows // 2, samples), jnp.int32)] * 2
        + [table_shape] * 2,
        [
            pltpu.VMEM((count, coef_local, block), f32),
            pltpu.SMEM(angle_ids.shape, jnp.int32),
            pltpu.SemaphoreType.DMA((count + 3 + projections,)),
        ],
    )(ids_far, coef_far, vox_far, wgt_far, table_far)
    received = []
    for t in range(len(cuts)):
        if t == 0:
            early = [swap(parts[m - 2], "coef", m) for m in range(2, count - 1)]
        received.append(early + [swap(parts[count - 3 + t], "coef", count - 1)])
    partner = swap(own, "coef", 1)
    near = swap(harmonics, "coef", 1)
    table_partner = swap(table_other, "coef", 1)
    moves = [(0, 1)] * slab_bits + [(1, 0)] * group_bits + [(1, 1)] * (slab_bits * group_bits)
    for m in fetched:
        for up, along in moves:
            total = lax.axis_size("groups") * slab_count
            pairs = [(i, (((i // slab_count) ^ up) * slab_count) + ((i % slab_count) ^ along)) for i in range(total)]
            fetched[m].append(lax.ppermute(fetched[m][0], ("groups", "slab"), pairs))

    top = kernel(
        build_kernel,
        [VMEM, VMEM],
        VMEM,
        shape((rows // 2, cols), bf16),
        [pltpu.VMEM((GROUP * cols // LANES, LANES), f32)],
    )(vox, wgt)
    low = swap(top, "coef", 1)
    for m in list(fetched):
        fetched[m ^ 1] = [swap(v, "coef", 1) for v in fetched[m]]
    far = [v for m in range(2, count) for v in fetched[m]]

    total, send = kernel(
        lambda *refs: sums_kernel(count, *refs),
        [VMEM] * 5 + [HBM],
        [VMEM, VMEM],
        [shape((half, rays, channels // 2), f32)] * 2,
        [pltpu.VMEM((half, rays, channels), f32), pltpu.SemaphoreType.DMA(())],
    )(top, own, partner, table_mine, table_partner, measured_far)

    masks = [1 << n for n in range(1, count.bit_length() - 1)]
    for mask in masks[::-1]:
        if mask < count // 2:
            width = total.shape[2] // 2
            bit = jnp.where((me & mask) == 0, 0, 1)
            send = lax.dynamic_slice_in_dim(total, (1 - bit) * width, width, 2)
            total = lax.dynamic_slice_in_dim(total, bit * width, width, 2)
        total = total + swap(send, "coef", mask)

    wide = shape((count * coef_local, harmonics.shape[1]), bf16)
    returned = []
    for t, cut in enumerate(cuts):
        first = t == 0
        extra = [harmonics, near, *far] if first else [waves]
        outs = kernel(
            lambda *refs: penalty_kernel(count, pieces, cut, first, *refs),
            [VMEM] * (count + len(extra)),
            [VMEM] * (count + first),
            [shape((coef_local, cut[1]), bf16)] * count + [wide] * first,
            [
                pltpu.VMEM((count * coef_local, cut[1]), bf16),
                pltpu.VMEM((cut[1], count * coef_local), bf16),
                pltpu.VMEM((count * coef_local, cut[1]), f32),
            ],
        )(own, partner, *received[t], *extra)
        if first:
            waves = outs[-1]
        back = [outs[0]]
        for m in range(1, count):
            back.append(swap(outs[m], "coef", m))
        returned.append(back)
        if first:
            half_mine = [total.astype(bf16)]
            for mask in masks:
                other = [swap(v, "coef", mask) for v in half_mine]
                if total.shape[2] % LANES == 0:
                    half_mine = half_mine + other
                    continue
                low_bit, pair = (me & mask) == 0, (half_mine[0], other[0])
                ordered = [jnp.where(low_bit, *pair), jnp.where(low_bit, *pair[::-1])]
                half_mine = [jnp.concatenate(ordered, 2)]
    res_other = swap(total, "coef", 1)
    half_other = [swap(v, "coef", 1) for v in half_mine]

    ready = [(t, j) for t in range(len(cuts)) for j in range(count) if t == 0 or j < 2]
    updated, residual, *later = kernel(
        lambda *refs: data_kernel(count, cuts, len(half_mine), *refs),
        [VMEM] * (2 * len(half_mine) + 6) + [HBM] + [VMEM] * len(ready),
        [HBM] + [VMEM] * len(cuts),
        [shape((coef_local, cols), f32), shape((projections, rays, channels // count), f32)]
        + [shape((count - 2, coef_local, cut[1]), f32) for cut in cuts[1:]],
        [
            pltpu.VMEM((coef_local, rows // 2), bf16),
            pltpu.VMEM((coef_local, rows // 2), bf16),
            pltpu.VMEM((len(ready), coef_local, max(cut[1] for cut in cuts)), f32),
            pltpu.SemaphoreType.DMA((len(cuts) * count,)),
            pltpu.SemaphoreType.DMA((len(ready),)),
        ],
    )(
        *half_mine,
        *half_other,
        total,
        res_other,
        table_mine,
        table_other,
        top,
        low,
        coef_far,
        *[returned[t][j] for t, j in ready],
    )
    remote = list(range(2, count))
    middle = len(remote) // 2
    for t, cut in list(enumerate(cuts))[1:]:
        for masks in (remote[:middle], remote[middle:]):
            if not masks:
                continue
            updated = kernel(
                lambda *refs: finish_kernel(count, cut, masks, *refs),
                [VMEM] * (len(masks) + 1) + [HBM],
                HBM,
                shape((coef_local, cols), f32),
                [pltpu.VMEM((len(masks), coef_local, cut[1]), f32), pltpu.SemaphoreType.DMA((len(masks),))],
                aliases={len(masks) + 1: 0},
            )(later[t - 1], *[returned[t][m] for m in masks], updated)
    return (updated, residual[:, None])


def solution(mesh):
    in_specs = (
        P("coef", ("groups", "slab")),
        P("groups", "slab", None, None),
        P(),
        P(),
        P(),
        P(None, "coef", None),
        P("coef", None),
    )
    out_specs = (P("coef", ("groups", "slab")), P("groups", "slab", None, "coef"))
    return jax.shard_map(step_of, mesh=mesh, in_specs=in_specs, out_specs=out_specs, check_vma=False)
```

```python
import jax
import jax.numpy as jnp
from jax import lax
from jax.experimental import pallas as pl
from jax.experimental.pallas import tpu as pltpu
from jax.sharding import PartitionSpec as P


LANES = 128
QUARTERS = (2, 2)
GROUP = 64
NT = (((1,), (1,)), ((), ()))
NN = (((1,), (0,)), ((), ()))
VMEM = pl.BlockSpec(memory_space=pltpu.VMEM)
HBM = pl.BlockSpec(memory_space=pltpu.HBM)


def dot(a, b, dims):
    return lax.dot_general(a, b, dims, preferred_element_type=jnp.float32)


def swap(value, axis, mask):
    count = lax.axis_size(axis)
    return lax.ppermute(value, axis, [(i, i ^ mask) for i in range(count)])


def aligned(index, width):
    return pl.ds(pl.multiple_of(index * width, width), width)


def cuts_of(block):
    if block % (4 * LANES):
        return [(0, block)]
    unit = block // 4
    starts = [unit * sum(QUARTERS[:t]) for t in range(len(QUARTERS))]
    return [(start, unit * size) for start, size in zip(starts, QUARTERS)]


def position():
    me = lax.axis_index("coef")
    place = jnp.zeros((), jnp.int32)
    for axis in ("groups", "slab"):
        if lax.axis_size(axis) % 2 == 0:
            place = place * 2 + (lax.axis_index(axis) & 1)
    return me, me & 1, place


def columns(index, block, cut):
    return pl.ds(pl.multiple_of(index * block + cut[0], LANES), cut[1])


def prepare_kernel(count, cuts, ids_far, coef, vox, wgt, table, *refs):
    full, parts = refs[:count - 3], refs[count - 3:count - 3 + len(cuts)]
    whole, vox_out, wgt_out, table_mine, table_other, stage, ids, sems = refs[count - 3 + len(cuts):]
    me, side, _ = position()
    block = coef.shape[1] // count
    half_rows, half = vox_out.shape[0], table_mine.shape[0]
    order = list(range(2, count)) + [1, 0]
    copies = {}
    for m in order:
        copies[m] = pltpu.make_async_copy(coef.at[:, aligned(me ^ m, block)], stage.at[m], sems.at[m])
    rest = [
        pltpu.make_async_copy(vox.at[aligned(side, half_rows)], vox_out, sems.at[count]),
        pltpu.make_async_copy(wgt.at[aligned(side, half_rows)], wgt_out, sems.at[count + 1]),
    ]
    numbers = pltpu.make_async_copy(ids_far, ids, sems.at[count + 2 + 2 * half])
    numbers.start()
    for m in order:
        copies[m].start()
    numbers.wait()
    for n, (out, first) in enumerate(((table_other, (1 - side) * half), (table_mine, side * half))):
        for i in range(half):
            rest.append(pltpu.make_async_copy(table.at[ids[first + i]], out.at[i], sems.at[count + 2 + n * half + i]))
    for c in rest:
        c.start()
    for m in order:
        copies[m].wait()
        values = stage[m].astype(jnp.bfloat16)
        whole[:, aligned(me ^ m, block)] = values
        if 1 < m < count - 1:
            full[m - 2][...] = values
        if m == count - 1:
            for t, cut in enumerate(cuts):
                parts[t][...] = values[:, cut[0]:cut[0] + cut[1]]
    for c in rest:
        c.wait()


def piece_kernel(harm, out, sem):
    copy = pltpu.make_async_copy(harm.at[:, aligned(position()[2], out.shape[1])], out, sem)
    copy.start()
    copy.wait()


def build_kernel(vox_ref, wgt_ref, matrix_ref, tile_ref):
    rows, samples = vox_ref.shape
    cols = matrix_ref.shape[1]
    high_count = cols // LANES
    low_pos = lax.broadcasted_iota(jnp.int32, (LANES, samples), 0)
    high_pos = lax.broadcasted_iota(jnp.int32, (high_count, samples), 0)
    blank = jnp.zeros((high_count, samples), jnp.bfloat16)

    def build(step, carry):
        first = pl.multiple_of(step * GROUP, GROUP)
        vox = vox_ref[pl.ds(first, GROUP), :]
        wgt = wgt_ref[pl.ds(first, GROUP), :].astype(jnp.float32) * (1.0 / 256.0)
        low = vox & (LANES - 1)
        high = lax.shift_right_logical(vox, LANES.bit_length() - 1)
        hots = []
        for i in range(GROUP):
            low_hot = (low_pos == low[i:i + 1]).astype(jnp.float32).astype(jnp.bfloat16)
            high_hot = jnp.where(high_pos == high[i:i + 1], wgt[i:i + 1], 0.0).astype(jnp.bfloat16)
            hots.append((low_hot, high_hot))
        for i in range(0, GROUP, 2):
            (low_a, high_a), (low_b, high_b) = hots[i:i + 2]
            left = jnp.concatenate([jnp.concatenate([high_a, blank], 1), jnp.concatenate([blank, high_b], 1)], 0)
            right = jnp.concatenate([low_a, low_b], 1)
            tile_ref[i * high_count:(i + 2) * high_count, :] = dot(left, right, NT)
        for h in range(high_count):
            part = tile_ref[pl.ds(h, GROUP, stride=high_count), :]
            matrix_ref[pl.ds(first, GROUP), h * LANES:(h + 1) * LANES] = part.astype(jnp.bfloat16)
        return carry

    lax.fori_loop(0, rows // GROUP, build, 0)


def sums_kernel(count, matrix_ref, own, partner, table_own, table_partner, measured, keep, send, target, sem):
    half, rays, width = keep.shape
    me, side, _ = position()
    fetch = pltpu.make_async_copy(measured.at[pl.ds(side * half, half)], target, sem)
    fetch.start()
    sums_own = dot(matrix_ref[...], own[...], NT).astype(jnp.bfloat16)
    sums_partner = dot(matrix_ref[...], partner[...], NT).astype(jnp.bfloat16)
    fetch.wait()
    high = (me // (count // 2)) & 1
    for i in range(half):
        rows = slice(i * rays, (i + 1) * rays)
        for out, bit in ((send, 1 - high), (keep, high)):
            at = aligned(bit, width)
            total = dot(sums_own[rows], table_own[i, :, at], NN) + dot(sums_partner[rows], table_partner[i, :, at], NN)
            out[i] = total - (2.0 / count) * target[i, :, at]


def penalty_kernel(count, pieces, cut, first, own, partner, *refs):
    blocks, refs = refs[:count - 2], refs[count - 2:]
    if first:
        harm, near, far = refs[0], refs[1], refs[2:2 + (count - 2) * pieces]
        outs, waves, refs = refs[2 + len(far):][:count], refs[2 + len(far) + count], refs[3 + len(far) + count:]
    else:
        waves, outs, refs = refs[0], refs[1:count + 1], refs[count + 1:]
    stack, turned, acc = refs
    me, _, place = position()
    height = outs[0].shape[0]
    width = waves.shape[1] // pieces
    at = columns(me, own.shape[1] // count, cut)
    stack[0:height, :] = own[:, at]
    stack[height:2 * height, :] = partner[:, at]
    for j in range(2, count):
        start = 0 if j == count - 1 else cut[0]
        stack[j * height:(j + 1) * height, :] = blocks[j - 2][:, start:start + cut[1]]
    turned[...] = jnp.swapaxes(stack[...], 0, 1)
    for r in range(pieces):
        span = slice(r * width, (r + 1) * width)
        if first:
            waves[0:height, span] = harm[:, aligned(place ^ r, width)]
            waves[height:2 * height, span] = near[:, aligned(place ^ r, width)]
            for j in range(2, count):
                waves[j * height:(j + 1) * height, span] = far[(j - 2) * pieces + r][...]
        wave = waves[:, span]
        field = dot(turned[...], wave, NN)
        slope = (0.5 * jnp.tanh(0.5 * field) - 0.5).astype(jnp.bfloat16)
        part = dot(wave, slope, NT)
        if r > 0:
            part += acc[...]
        if r < pieces - 1:
            acc[...] = part
        else:
            for j in range(count):
                outs[j][...] = part[j * height:(j + 1) * height].astype(outs[j].dtype)


def data_kernel(count, cuts, split, *refs):
    halves, refs = (refs[:split], refs[split:2 * split]), refs[2 * split:]
    res_mine, res_other, table_mine, table_other, top_ref, low_ref, coef = refs[:7]
    refs = refs[7:]
    order = [(0, j) for j in range(count)] + [(t, j) for t in range(1, len(cuts)) for j in range(count)]
    ready = [key for key in order if key[0] == 0 or key[1] < 2]
    grads, refs = dict(zip(ready, refs)), refs[len(ready):]
    updated, residual_ref, later = refs[0], refs[1], refs[2:1 + len(cuts)]
    back_a, back_b, buf, sems, out_sems = refs[1 + len(cuts):]
    me, side, _ = position()
    half, rays, width = halves[0][0].shape
    block = coef.shape[1] // count
    own_width = residual_ref.shape[2]
    spots, copies = {}, {}
    for n, (t, j) in enumerate(order):
        if (t, j) in grads:
            spots[t, j] = buf.at[ready.index((t, j)), :, 0:cuts[t][1]]
        else:
            spots[t, j] = later[t - 1].at[j - 2]
        copies[t, j] = pltpu.make_async_copy(coef.at[:, columns(me ^ j, block, cuts[t])], spots[t, j], sems.at[n])
        copies[t, j].start()
    for back, parts, table in ((back_a, halves[0], table_mine), (back_b, halves[1], table_other)):
        for i in range(half):
            total = dot(table[i, :, aligned(me // 2 if split > 1 else 0, width)], parts[0][i], NT)
            for p in range(1, split):
                total += dot(table[i, :, aligned((me // 2) ^ p, width)], parts[p][i], NT)
            back[:, i * rays:(i + 1) * rays] = total.astype(jnp.bfloat16)
    writes = []
    for t, j in order:
        at = columns(me ^ j, block, cuts[t])
        grad = dot(back_a[...], top_ref[:, at], NN) + dot(back_b[...], low_ref[:, at], NN)
        copies[t, j].wait()
        spot = spots[t, j]
        if (t, j) in grads:
            spot[...] = spot[...] - 0.5 * grad - 0.5 * grads[t, j][...].astype(jnp.float32)
            writes.append(pltpu.make_async_copy(spot, updated.at[:, at], out_sems.at[len(writes)]))
            writes[-1].start()
        else:
            spot[...] = spot[...] - 0.5 * grad
    for q in range(2):
        @pl.when(side == q)
        def _():
            for i in range(half):
                residual_ref[side * half + i] = res_mine[i, :, q * own_width:(q + 1) * own_width]
                residual_ref[(1 - side) * half + i] = res_other[i, :, q * own_width:(q + 1) * own_width]
    for w in writes:
        w.wait()


def finish_kernel(count, cut, masks, later, *refs):
    grads = refs[:len(masks)]
    _, updated, buf, sems = refs[len(masks):]
    block = updated.shape[1] // count
    writes = []
    for n, j in enumerate(masks):
        buf[n] = later[j - 2] - 0.5 * grads[n][...].astype(jnp.float32)
        at = columns(position()[0] ^ j, block, cut)
        writes.append(pltpu.make_async_copy(buf.at[n], updated.at[:, at], sems.at[n]))
        writes[-1].start()
    for w in writes:
        w.wait()


def step_of(coefficients, measured, ray_voxels, ray_weights, angle_ids, angle_table, harmonics):
    coef_local, cols = coefficients.shape
    projections, _, rays, channels = measured.shape
    rows = projections * rays
    samples = ray_voxels.shape[2]
    count = lax.axis_size("coef")
    me = lax.axis_index("coef")
    half = projections // 2
    block = cols // count
    cuts = cuts_of(block)
    bf16, f32 = jnp.bfloat16, jnp.float32
    shape = jax.ShapeDtypeStruct

    def kernel(body_of, ins, outs, out_shape, scratch=(), grant=12, aliases={}):
        return pl.pallas_call(
            body_of,
            in_specs=ins,
            out_specs=outs,
            out_shape=out_shape,
            scratch_shapes=list(scratch),
            input_output_aliases=aliases,
            compiler_params=pltpu.CompilerParams(vmem_limit_bytes=grant << 20),
        )

    group_bits = 1 if lax.axis_size("groups") % 2 == 0 else 0
    slab_count = lax.axis_size("slab")
    slab_bits = 1 if slab_count % 2 == 0 else 0
    pieces = 1 << (group_bits + slab_bits)
    width = harmonics.shape[1] // pieces
    rows_shape = (rows, samples)
    coef_far, measured_far, vox_far, wgt_far, ids_far, table_far, harm_far = [
        pltpu.with_memory_space_constraint(v, pltpu.HBM)
        for v in (
            coefficients,
            measured.reshape(projections, rays, channels),
            ray_voxels.reshape(rows_shape),
            ray_weights.reshape(rows_shape),
            angle_ids,
            angle_table,
            harmonics,
        )
    ]

    piece = kernel(
        piece_kernel, [HBM], VMEM, shape((coef_local, width), bf16), [pltpu.SemaphoreType.DMA(())], grant=4
    )(harm_far)
    fetched = {m: [swap(piece, "coef", m)] for m in range(2, count, 2)}
    table_shape = shape((half,) + angle_table.shape[1:], bf16)
    *parts, own, vox, wgt, table_mine, table_other = kernel(
        lambda *refs: prepare_kernel(count, cuts, *refs),
        [HBM] * 5,
        [VMEM] * (count + len(cuts) + 2),
        [shape((coef_local, block), bf16)] * (count - 3)
        + [shape((coef_local, cut[1]), bf16) for cut in cuts]
        + [shape((coef_local, cols), bf16)]
        + [shape((rows // 2, samples), jnp.int32)] * 2
        + [table_shape] * 2,
        [
            pltpu.VMEM((count, coef_local, block), f32),
            pltpu.SMEM(angle_ids.shape, jnp.int32),
            pltpu.SemaphoreType.DMA((count + 3 + projections,)),
        ],
    )(ids_far, coef_far, vox_far, wgt_far, table_far)
    received = []
    for t in range(len(cuts)):
        if t == 0:
            early = [swap(parts[m - 2], "coef", m) for m in range(2, count - 1)]
        received.append(early + [swap(parts[count - 3 + t], "coef", count - 1)])
    partner = swap(own, "coef", 1)
    near = swap(harmonics, "coef", 1)
    table_partner = swap(table_other, "coef", 1)
    moves = [(0, 1)] * slab_bits + [(1, 0)] * group_bits + [(1, 1)] * (slab_bits * group_bits)
    for m in fetched:
        for up, along in moves:
            total = lax.axis_size("groups") * slab_count
            pairs = [(i, (((i // slab_count) ^ up) * slab_count) + ((i % slab_count) ^ along)) for i in range(total)]
            fetched[m].append(lax.ppermute(fetched[m][0], ("groups", "slab"), pairs))

    top = kernel(
        build_kernel,
        [VMEM, VMEM],
        VMEM,
        shape((rows // 2, cols), bf16),
        [pltpu.VMEM((GROUP * cols // LANES, LANES), f32)],
    )(vox, wgt)
    low = swap(top, "coef", 1)
    for m in list(fetched):
        fetched[m ^ 1] = [swap(v, "coef", 1) for v in fetched[m]]
    far = [v for m in range(2, count) for v in fetched[m]]

    total, send = kernel(
        lambda *refs: sums_kernel(count, *refs),
        [VMEM] * 5 + [HBM],
        [VMEM, VMEM],
        [shape((half, rays, channels // 2), f32)] * 2,
        [pltpu.VMEM((half, rays, channels), f32), pltpu.SemaphoreType.DMA(())],
    )(top, own, partner, table_mine, table_partner, measured_far)

    masks = [1 << n for n in range(1, count.bit_length() - 1)]
    for mask in masks[::-1]:
        if mask < count // 2:
            width = total.shape[2] // 2
            bit = jnp.where((me & mask) == 0, 0, 1)
            send = lax.dynamic_slice_in_dim(total, (1 - bit) * width, width, 2)
            total = lax.dynamic_slice_in_dim(total, bit * width, width, 2)
        total = total + swap(send, "coef", mask)

    wide = shape((count * coef_local, harmonics.shape[1]), bf16)
    returned = []
    for t, cut in enumerate(cuts):
        first = t == 0
        extra = [harmonics, near, *far] if first else [waves]
        outs = kernel(
            lambda *refs: penalty_kernel(count, pieces, cut, first, *refs),
            [VMEM] * (count + len(extra)),
            [VMEM] * (count + first),
            [shape((coef_local, cut[1]), bf16)] * count + [wide] * first,
            [
                pltpu.VMEM((count * coef_local, cut[1]), bf16),
                pltpu.VMEM((cut[1], count * coef_local), bf16),
                pltpu.VMEM((count * coef_local, cut[1]), f32),
            ],
        )(own, partner, *received[t], *extra)
        if first:
            waves = outs[-1]
        back = [outs[0]]
        for m in range(1, count):
            back.append(swap(outs[m], "coef", m))
        returned.append(back)
        if first:
            half_mine = [total.astype(bf16)]
            for mask in masks:
                other = [swap(v, "coef", mask) for v in half_mine]
                if total.shape[2] % LANES == 0:
                    half_mine = half_mine + other
                    continue
                low_bit, pair = (me & mask) == 0, (half_mine[0], other[0])
                ordered = [jnp.where(low_bit, *pair), jnp.where(low_bit, *pair[::-1])]
                half_mine = [jnp.concatenate(ordered, 2)]
    res_other = swap(total, "coef", 1)
    half_other = [swap(v, "coef", 1) for v in half_mine]

    ready = [(t, j) for t in range(len(cuts)) for j in range(count) if t == 0 or j < 2]
    updated, residual, *later = kernel(
        lambda *refs: data_kernel(count, cuts, len(half_mine), *refs),
        [VMEM] * (2 * len(half_mine) + 6) + [HBM] + [VMEM] * len(ready),
        [HBM] + [VMEM] * len(cuts),
        [shape((coef_local, cols), f32), shape((projections, rays, channels // count), f32)]
        + [shape((count - 2, coef_local, cut[1]), f32) for cut in cuts[1:]],
        [
            pltpu.VMEM((coef_local, rows // 2), bf16),
            pltpu.VMEM((coef_local, rows // 2), bf16),
            pltpu.VMEM((len(ready), coef_local, max(cut[1] for cut in cuts)), f32),
            pltpu.SemaphoreType.DMA((len(cuts) * count,)),
            pltpu.SemaphoreType.DMA((len(ready),)),
        ],
    )(
        *half_mine,
        *half_other,
        total,
        res_other,
        table_mine,
        table_other,
        top,
        low,
        coef_far,
        *[returned[t][j] for t, j in ready],
    )
    remote = list(range(2, count))
    middle = len(remote) // 2
    for t, cut in list(enumerate(cuts))[1:]:
        for masks in (remote[:middle], remote[middle:]):
            if not masks:
                continue
            updated = kernel(
                lambda *refs: finish_kernel(count, cut, masks, *refs),
                [VMEM] * (len(masks) + 1) + [HBM],
                HBM,
                shape((coef_local, cols), f32),
                [pltpu.VMEM((len(masks), coef_local, cut[1]), f32), pltpu.SemaphoreType.DMA((len(masks),))],
                aliases={len(masks) + 1: 0},
            )(later[t - 1], *[returned[t][m] for m in masks], updated)
    return (updated, residual[:, None])


def solution(mesh):
    in_specs = (
        P("coef", ("groups", "slab")),
        P("groups", "slab", None, None),
        P(),
        P(),
        P(),
        P(None, "coef", None),
        P("coef", None),
    )
    out_specs = (P("coef", ("groups", "slab")), P("groups", "slab", None, "coef"))
    return jax.shard_map(step_of, mesh=mesh, in_specs=in_specs, out_specs=out_specs, check_vma=False)
```

```python
import jax
import jax.numpy as jnp
from jax import lax
from jax.experimental import pallas as pl
from jax.experimental.pallas import tpu as pltpu
from jax.sharding import PartitionSpec as P


LANES = 128
QUARTERS = (2, 2)
GROUP = 64
NT = (((1,), (1,)), ((), ()))
NN = (((1,), (0,)), ((), ()))
VMEM = pl.BlockSpec(memory_space=pltpu.VMEM)
HBM = pl.BlockSpec(memory_space=pltpu.HBM)


def dot(a, b, dims):
    return lax.dot_general(a, b, dims, preferred_element_type=jnp.float32)


def swap(value, axis, mask):
    count = lax.axis_size(axis)
    return lax.ppermute(value, axis, [(i, i ^ mask) for i in range(count)])


def aligned(index, width):
    return pl.ds(pl.multiple_of(index * width, width), width)


def cuts_of(block):
    if block % (4 * LANES):
        return [(0, block)]
    unit = block // 4
    starts = [unit * sum(QUARTERS[:t]) for t in range(len(QUARTERS))]
    return [(start, unit * size) for start, size in zip(starts, QUARTERS)]


def position():
    me = lax.axis_index("coef")
    place = jnp.zeros((), jnp.int32)
    for axis in ("groups", "slab"):
        if lax.axis_size(axis) % 2 == 0:
            place = place * 2 + (lax.axis_index(axis) & 1)
    return me, me & 1, place


def columns(index, block, cut):
    return pl.ds(pl.multiple_of(index * block + cut[0], LANES), cut[1])


def prepare_kernel(count, cuts, ids_far, coef, vox, wgt, table, harm, *refs):
    full, parts = refs[:count - 3], refs[count - 3:count - 3 + len(cuts)]
    whole, vox_out, wgt_out, table_mine, table_other, harm_out, stage, ids, sems = refs[count - 3 + len(cuts):]
    me, side, _ = position()
    block = coef.shape[1] // count
    half_rows, half = vox_out.shape[0], table_mine.shape[0]
    order = list(range(2, count)) + [1, 0]
    copies = {}
    for m in order:
        copies[m] = pltpu.make_async_copy(coef.at[:, aligned(me ^ m, block)], stage.at[m], sems.at[m])
    rest = [
        pltpu.make_async_copy(vox.at[aligned(side, half_rows)], vox_out, sems.at[count]),
        pltpu.make_async_copy(wgt.at[aligned(side, half_rows)], wgt_out, sems.at[count + 1]),
        pltpu.make_async_copy(harm, harm_out, sems.at[count + 3 + 2 * half]),
    ]
    numbers = pltpu.make_async_copy(ids_far, ids, sems.at[count + 2 + 2 * half])
    numbers.start()
    for m in order:
        copies[m].start()
    numbers.wait()
    for n, (out, first) in enumerate(((table_other, (1 - side) * half), (table_mine, side * half))):
        for i in range(half):
            rest.append(pltpu.make_async_copy(table.at[ids[first + i]], out.at[i], sems.at[count + 2 + n * half + i]))
    for c in rest:
        c.start()
    for m in order:
        copies[m].wait()
        values = stage[m].astype(jnp.bfloat16)
        whole[:, aligned(me ^ m, block)] = values
        if 1 < m < count - 1:
            full[m - 2][...] = values
        if m == count - 1:
            for t, cut in enumerate(cuts):
                parts[t][...] = values[:, cut[0]:cut[0] + cut[1]]
    for c in rest:
        c.wait()


def build_kernel(vox_ref, wgt_ref, matrix_ref, tile_ref):
    rows, samples = vox_ref.shape
    cols = matrix_ref.shape[1]
    high_count = cols // LANES
    low_pos = lax.broadcasted_iota(jnp.int32, (LANES, samples), 0)
    high_pos = lax.broadcasted_iota(jnp.int32, (high_count, samples), 0)
    blank = jnp.zeros((high_count, samples), jnp.bfloat16)

    def build(step, carry):
        first = pl.multiple_of(step * GROUP, GROUP)
        vox = vox_ref[pl.ds(first, GROUP), :]
        wgt = wgt_ref[pl.ds(first, GROUP), :].astype(jnp.float32) * (1.0 / 256.0)
        low = vox & (LANES - 1)
        high = lax.shift_right_logical(vox, LANES.bit_length() - 1)
        hots = []
        for i in range(GROUP):
            low_hot = (low_pos == low[i:i + 1]).astype(jnp.float32).astype(jnp.bfloat16)
            high_hot = jnp.where(high_pos == high[i:i + 1], wgt[i:i + 1], 0.0).astype(jnp.bfloat16)
            hots.append((low_hot, high_hot))
        for i in range(0, GROUP, 2):
            (low_a, high_a), (low_b, high_b) = hots[i:i + 2]
            left = jnp.concatenate([jnp.concatenate([high_a, blank], 1), jnp.concatenate([blank, high_b], 1)], 0)
            right = jnp.concatenate([low_a, low_b], 1)
            tile_ref[i * high_count:(i + 2) * high_count, :] = dot(left, right, NT)
        for h in range(high_count):
            part = tile_ref[pl.ds(h, GROUP, stride=high_count), :]
            matrix_ref[pl.ds(first, GROUP), h * LANES:(h + 1) * LANES] = part.astype(jnp.bfloat16)
        return carry

    lax.fori_loop(0, rows // GROUP, build, 0)


def sums_kernel(count, matrix_ref, own, partner, table_own, table_partner, measured, keep, send, target, sem):
    half, rays, width = keep.shape
    me, side, _ = position()
    fetch = pltpu.make_async_copy(measured.at[pl.ds(side * half, half)], target, sem)
    fetch.start()
    sums_own = dot(matrix_ref[...], own[...], NT).astype(jnp.bfloat16)
    sums_partner = dot(matrix_ref[...], partner[...], NT).astype(jnp.bfloat16)
    fetch.wait()
    high = (me // (count // 2)) & 1
    for i in range(half):
        rows = slice(i * rays, (i + 1) * rays)
        for out, bit in ((send, 1 - high), (keep, high)):
            at = aligned(bit, width)
            total = dot(sums_own[rows], table_own[i, :, at], NN) + dot(sums_partner[rows], table_partner[i, :, at], NN)
            out[i] = total - (2.0 / count) * target[i, :, at]


def penalty_kernel(count, pieces, cut, first, own, partner, *refs):
    blocks, refs = refs[:count - 2], refs[count - 2:]
    if first:
        harm, near, far = refs[0], refs[1], refs[2:2 + (count - 2) * pieces]
        outs, waves, refs = refs[2 + len(far):][:count], refs[2 + len(far) + count], refs[3 + len(far) + count:]
    else:
        waves, outs, refs = refs[0], refs[1:count + 1], refs[count + 1:]
    stack, turned, acc = refs
    me, _, place = position()
    height = outs[0].shape[0]
    width = waves.shape[1] // pieces
    at = columns(me, own.shape[1] // count, cut)
    stack[0:height, :] = own[:, at]
    stack[height:2 * height, :] = partner[:, at]
    for j in range(2, count):
        start = 0 if j == count - 1 else cut[0]
        stack[j * height:(j + 1) * height, :] = blocks[j - 2][:, start:start + cut[1]]
    turned[...] = jnp.swapaxes(stack[...], 0, 1)
    for r in range(pieces):
        span = slice(r * width, (r + 1) * width)
        if first:
            waves[0:height, span] = harm[:, aligned(place ^ r, width)]
            waves[height:2 * height, span] = near[:, aligned(place ^ r, width)]
            for j in range(2, count):
                waves[j * height:(j + 1) * height, span] = far[(j - 2) * pieces + r][...]
        wave = waves[:, span]
        field = dot(turned[...], wave, NN)
        slope = (0.5 * jnp.tanh(0.5 * field) - 0.5).astype(jnp.bfloat16)
        part = dot(wave, slope, NT)
        if r > 0:
            part += acc[...]
        if r < pieces - 1:
            acc[...] = part
        else:
            for j in range(count):
                outs[j][...] = part[j * height:(j + 1) * height].astype(outs[j].dtype)


def data_kernel(count, cuts, split, *refs):
    halves, refs = (refs[:split], refs[split:2 * split]), refs[2 * split:]
    res_mine, res_other, table_mine, table_other, top_ref, low_ref, coef = refs[:7]
    refs = refs[7:]
    order = [(0, j) for j in range(count)] + [(t, j) for t in range(1, len(cuts)) for j in range(count)]
    ready = [key for key in order if key[0] == 0 or key[1] < 2]
    grads, refs = dict(zip(ready, refs)), refs[len(ready):]
    updated, residual_ref, later = refs[0], refs[1], refs[2:1 + len(cuts)]
    back_a, back_b, buf, sems, out_sems = refs[1 + len(cuts):]
    me, side, _ = position()
    half, rays, width = halves[0][0].shape
    block = coef.shape[1] // count
    own_width = residual_ref.shape[2]
    spots, copies = {}, {}
    for n, (t, j) in enumerate(order):
        if (t, j) in grads:
            spots[t, j] = buf.at[ready.index((t, j)), :, 0:cuts[t][1]]
        else:
            spots[t, j] = later[t - 1].at[j - 2]
        copies[t, j] = pltpu.make_async_copy(coef.at[:, columns(me ^ j, block, cuts[t])], spots[t, j], sems.at[n])
        copies[t, j].start()
    for back, parts, table in ((back_a, halves[0], table_mine), (back_b, halves[1], table_other)):
        for i in range(half):
            total = dot(table[i, :, aligned(me // 2 if split > 1 else 0, width)], parts[0][i], NT)
            for p in range(1, split):
                total += dot(table[i, :, aligned((me // 2) ^ p, width)], parts[p][i], NT)
            back[:, i * rays:(i + 1) * rays] = total.astype(jnp.bfloat16)
    writes = []
    for t, j in order:
        at = columns(me ^ j, block, cuts[t])
        grad = dot(back_a[...], top_ref[:, at], NN) + dot(back_b[...], low_ref[:, at], NN)
        copies[t, j].wait()
        spot = spots[t, j]
        if (t, j) in grads:
            spot[...] = spot[...] - 0.5 * grad - 0.5 * grads[t, j][...].astype(jnp.float32)
            writes.append(pltpu.make_async_copy(spot, updated.at[:, at], out_sems.at[len(writes)]))
            writes[-1].start()
        else:
            spot[...] = spot[...] - 0.5 * grad
    for q in range(2):
        @pl.when(side == q)
        def _():
            for i in range(half):
                residual_ref[side * half + i] = res_mine[i, :, q * own_width:(q + 1) * own_width]
                residual_ref[(1 - side) * half + i] = res_other[i, :, q * own_width:(q + 1) * own_width]
    for w in writes:
        w.wait()


def finish_kernel(count, cut, masks, later, *refs):
    grads = refs[:len(masks)]
    _, updated, buf, sems = refs[len(masks):]
    block = updated.shape[1] // count
    writes = []
    for n, j in enumerate(masks):
        buf[n] = later[j - 2] - 0.5 * grads[n][...].astype(jnp.float32)
        at = columns(position()[0] ^ j, block, cut)
        writes.append(pltpu.make_async_copy(buf.at[n], updated.at[:, at], sems.at[n]))
        writes[-1].start()
    for w in writes:
        w.wait()


def step_of(coefficients, measured, ray_voxels, ray_weights, angle_ids, angle_table, harmonics):
    coef_local, cols = coefficients.shape
    projections, _, rays, channels = measured.shape
    rows = projections * rays
    samples = ray_voxels.shape[2]
    count = lax.axis_size("coef")
    me = lax.axis_index("coef")
    half = projections // 2
    block = cols // count
    cuts = cuts_of(block)
    bf16, f32 = jnp.bfloat16, jnp.float32
    shape = jax.ShapeDtypeStruct

    def kernel(body_of, ins, outs, out_shape, scratch=(), grant=12, aliases={}):
        return pl.pallas_call(
            body_of,
            in_specs=ins,
            out_specs=outs,
            out_shape=out_shape,
            scratch_shapes=list(scratch),
            input_output_aliases=aliases,
            compiler_params=pltpu.CompilerParams(vmem_limit_bytes=grant << 20),
        )

    group_bits = 1 if lax.axis_size("groups") % 2 == 0 else 0
    slab_count = lax.axis_size("slab")
    slab_bits = 1 if slab_count % 2 == 0 else 0
    pieces = 1 << (group_bits + slab_bits)
    place = position()[2]
    width = harmonics.shape[1] // pieces
    rows_shape = (rows, samples)
    coef_far, measured_far, vox_far, wgt_far, ids_far, table_far, harm_far = [
        pltpu.with_memory_space_constraint(v, pltpu.HBM)
        for v in (
            coefficients,
            measured.reshape(projections, rays, channels),
            ray_voxels.reshape(rows_shape),
            ray_weights.reshape(rows_shape),
            angle_ids,
            angle_table,
            harmonics,
        )
    ]

    piece = lax.dynamic_slice_in_dim(harmonics, place * width, width, 1)
    fetched = {m: [swap(piece, "coef", m)] for m in range(2, count, 2)}
    table_shape = shape((half,) + angle_table.shape[1:], bf16)
    *parts, own, vox, wgt, table_mine, table_other, harm_own = kernel(
        lambda *refs: prepare_kernel(count, cuts, *refs),
        [HBM] * 6,
        [VMEM] * (count + len(cuts) + 3),
        [shape((coef_local, block), bf16)] * (count - 3)
        + [shape((coef_local, cut[1]), bf16) for cut in cuts]
        + [shape((coef_local, cols), bf16)]
        + [shape((rows // 2, samples), jnp.int32)] * 2
        + [table_shape] * 2
        + [shape(harmonics.shape, bf16)],
        [
            pltpu.VMEM((count, coef_local, block), f32),
            pltpu.SMEM(angle_ids.shape, jnp.int32),
            pltpu.SemaphoreType.DMA((count + 4 + projections,)),
        ],
    )(ids_far, coef_far, vox_far, wgt_far, table_far, harm_far)
    received = []
    for t in range(len(cuts)):
        if t == 0:
            early = [swap(parts[m - 2], "coef", m) for m in range(2, count - 1)]
        received.append(early + [swap(parts[count - 3 + t], "coef", count - 1)])
    partner = swap(own, "coef", 1)
    near = swap(harm_own, "coef", 1)
    table_partner = swap(table_other, "coef", 1)
    moves = [(0, 1)] * slab_bits + [(1, 0)] * group_bits + [(1, 1)] * (slab_bits * group_bits)
    for m in fetched:
        for up, along in moves:
            total = lax.axis_size("groups") * slab_count
            pairs = [(i, (((i // slab_count) ^ up) * slab_count) + ((i % slab_count) ^ along)) for i in range(total)]
            fetched[m].append(lax.ppermute(fetched[m][0], ("groups", "slab"), pairs))

    top = kernel(
        build_kernel,
        [VMEM, VMEM],
        VMEM,
        shape((rows // 2, cols), bf16),
        [pltpu.VMEM((GROUP * cols // LANES, LANES), f32)],
    )(vox, wgt)
    low = swap(top, "coef", 1)
    for m in list(fetched):
        fetched[m ^ 1] = [swap(v, "coef", 1) for v in fetched[m]]
    far = [v for m in range(2, count) for v in fetched[m]]

    total, send = kernel(
        lambda *refs: sums_kernel(count, *refs),
        [VMEM] * 5 + [HBM],
        [VMEM, VMEM],
        [shape((half, rays, channels // 2), f32)] * 2,
        [pltpu.VMEM((half, rays, channels), f32), pltpu.SemaphoreType.DMA(())],
    )(top, own, partner, table_mine, table_partner, measured_far)

    masks = [1 << n for n in range(1, count.bit_length() - 1)]
    for mask in masks[::-1]:
        if mask < count // 2:
            width = total.shape[2] // 2
            bit = jnp.where((me & mask) == 0, 0, 1)
            send = lax.dynamic_slice_in_dim(total, (1 - bit) * width, width, 2)
            total = lax.dynamic_slice_in_dim(total, bit * width, width, 2)
        total = total + swap(send, "coef", mask)

    wide = shape((count * coef_local, harmonics.shape[1]), bf16)
    returned = []
    for t, cut in enumerate(cuts):
        first = t == 0
        extra = [harm_own, near, *far] if first else [waves]
        outs = kernel(
            lambda *refs: penalty_kernel(count, pieces, cut, first, *refs),
            [VMEM] * (count + len(extra)),
            [VMEM] * (count + first),
            [shape((coef_local, cut[1]), bf16)] * count + [wide] * first,
            [
                pltpu.VMEM((count * coef_local, cut[1]), bf16),
                pltpu.VMEM((cut[1], count * coef_local), bf16),
                pltpu.VMEM((count * coef_local, cut[1]), f32),
            ],
        )(own, partner, *received[t], *extra)
        if first:
            waves = outs[-1]
        back = [outs[0]]
        for m in range(1, count):
            back.append(swap(outs[m], "coef", m))
        returned.append(back)
        if first:
            half_mine = [total.astype(bf16)]
            for mask in masks:
                other = [swap(v, "coef", mask) for v in half_mine]
                if total.shape[2] % LANES == 0:
                    half_mine = half_mine + other
                    continue
                low_bit, pair = (me & mask) == 0, (half_mine[0], other[0])
                ordered = [jnp.where(low_bit, *pair), jnp.where(low_bit, *pair[::-1])]
                half_mine = [jnp.concatenate(ordered, 2)]
    res_other = swap(total, "coef", 1)
    half_other = [swap(v, "coef", 1) for v in half_mine]

    ready = [(t, j) for t in range(len(cuts)) for j in range(count) if t == 0 or j < 2]
    updated, residual, *later = kernel(
        lambda *refs: data_kernel(count, cuts, len(half_mine), *refs),
        [VMEM] * (2 * len(half_mine) + 6) + [HBM] + [VMEM] * len(ready),
        [HBM] + [VMEM] * len(cuts),
        [shape((coef_local, cols), f32), shape((projections, rays, channels // count), f32)]
        + [shape((count - 2, coef_local, cut[1]), f32) for cut in cuts[1:]],
        [
            pltpu.VMEM((coef_local, rows // 2), bf16),
            pltpu.VMEM((coef_local, rows // 2), bf16),
            pltpu.VMEM((len(ready), coef_local, max(cut[1] for cut in cuts)), f32),
            pltpu.SemaphoreType.DMA((len(cuts) * count,)),
            pltpu.SemaphoreType.DMA((len(ready),)),
        ],
    )(
        *half_mine,
        *half_other,
        total,
        res_other,
        table_mine,
        table_other,
        top,
        low,
        coef_far,
        *[returned[t][j] for t, j in ready],
    )
    remote = list(range(2, count))
    middle = len(remote) // 2
    for t, cut in list(enumerate(cuts))[1:]:
        for masks in (remote[:middle], remote[middle:]):
            if not masks:
                continue
            updated = kernel(
                lambda *refs: finish_kernel(count, cut, masks, *refs),
                [VMEM] * (len(masks) + 1) + [HBM],
                HBM,
                shape((coef_local, cols), f32),
                [pltpu.VMEM((len(masks), coef_local, cut[1]), f32), pltpu.SemaphoreType.DMA((len(masks),))],
                aliases={len(masks) + 1: 0},
            )(later[t - 1], *[returned[t][m] for m in masks], updated)
    return (updated, residual[:, None])


def solution(mesh):
    in_specs = (
        P("coef", ("groups", "slab")),
        P("groups", "slab", None, None),
        P(),
        P(),
        P(),
        P(None, "coef", None),
        P("coef", None),
    )
    out_specs = (P("coef", ("groups", "slab")), P("groups", "slab", None, "coef"))
    return jax.shard_map(step_of, mesh=mesh, in_specs=in_specs, out_specs=out_specs, check_vma=False)
```

```python
import jax
import jax.numpy as jnp
from jax import lax
from jax.experimental import pallas as pl
from jax.experimental.pallas import tpu as pltpu
from jax.sharding import PartitionSpec as P


LANES = 128
QUARTERS = (2, 2)
GROUP = 128
NT = (((1,), (1,)), ((), ()))
NN = (((1,), (0,)), ((), ()))
VMEM = pl.BlockSpec(memory_space=pltpu.VMEM)
HBM = pl.BlockSpec(memory_space=pltpu.HBM)


def dot(a, b, dims):
    return lax.dot_general(a, b, dims, preferred_element_type=jnp.float32)


def swap(value, axis, mask):
    count = lax.axis_size(axis)
    return lax.ppermute(value, axis, [(i, i ^ mask) for i in range(count)])


def aligned(index, width):
    return pl.ds(pl.multiple_of(index * width, width), width)


def cuts_of(block):
    if block % (4 * LANES):
        return [(0, block)]
    unit = block // 4
    starts = [unit * sum(QUARTERS[:t]) for t in range(len(QUARTERS))]
    return [(start, unit * size) for start, size in zip(starts, QUARTERS)]


def position():
    me = lax.axis_index("coef")
    place = jnp.zeros((), jnp.int32)
    for axis in ("groups", "slab"):
        if lax.axis_size(axis) % 2 == 0:
            place = place * 2 + (lax.axis_index(axis) & 1)
    return me, me & 1, place


def columns(index, block, cut):
    return pl.ds(pl.multiple_of(index * block + cut[0], LANES), cut[1])


def prepare_kernel(count, cuts, ids_far, coef, vox, wgt, table, harm, *refs):
    full, parts = refs[:count - 3], refs[count - 3:count - 3 + len(cuts)]
    whole, vox_out, wgt_out, table_mine, table_other, harm_out, stage, ids, sems = refs[count - 3 + len(cuts):]
    me, side, _ = position()
    block = coef.shape[1] // count
    half_rows, half = vox_out.shape[0], table_mine.shape[0]
    order = list(range(2, count)) + [1, 0]
    copies = {}
    for m in order:
        copies[m] = pltpu.make_async_copy(coef.at[:, aligned(me ^ m, block)], stage.at[m], sems.at[m])
    rest = [
        pltpu.make_async_copy(vox.at[aligned(side, half_rows)], vox_out, sems.at[count]),
        pltpu.make_async_copy(wgt.at[aligned(side, half_rows)], wgt_out, sems.at[count + 1]),
        pltpu.make_async_copy(harm, harm_out, sems.at[count + 3 + 2 * half]),
    ]
    numbers = pltpu.make_async_copy(ids_far, ids, sems.at[count + 2 + 2 * half])
    numbers.start()
    for m in order:
        copies[m].start()
    numbers.wait()
    for n, (out, first) in enumerate(((table_other, (1 - side) * half), (table_mine, side * half))):
        for i in range(half):
            rest.append(pltpu.make_async_copy(table.at[ids[first + i]], out.at[i], sems.at[count + 2 + n * half + i]))
    for c in rest:
        c.start()
    for m in order:
        copies[m].wait()
        values = stage[m].astype(jnp.bfloat16)
        whole[:, aligned(me ^ m, block)] = values
        if 1 < m < count - 1:
            full[m - 2][...] = values
        if m == count - 1:
            for t, cut in enumerate(cuts):
                parts[t][...] = values[:, cut[0]:cut[0] + cut[1]]
    for c in rest:
        c.wait()


def piece_kernel(harm, out, sem):
    copy = pltpu.make_async_copy(harm.at[:, aligned(position()[2], out.shape[1])], out, sem)
    copy.start()
    copy.wait()


def build_kernel(vox_ref, wgt_ref, matrix_ref, tile_ref):
    rows, samples = vox_ref.shape
    cols = matrix_ref.shape[1]
    high_count = cols // LANES
    low_pos = lax.broadcasted_iota(jnp.int32, (LANES, samples), 0)
    high_pos = lax.broadcasted_iota(jnp.int32, (high_count, samples), 0)
    blank = jnp.zeros((high_count, samples), jnp.bfloat16)

    def build(step, carry):
        first = pl.multiple_of(step * GROUP, GROUP)
        vox = vox_ref[pl.ds(first, GROUP), :]
        wgt = wgt_ref[pl.ds(first, GROUP), :].astype(jnp.float32) * (1.0 / 256.0)
        low = vox & (LANES - 1)
        high = lax.shift_right_logical(vox, LANES.bit_length() - 1)
        hots = []
        for i in range(GROUP):
            low_hot = (low_pos == low[i:i + 1]).astype(jnp.float32).astype(jnp.bfloat16)
            high_hot = jnp.where(high_pos == high[i:i + 1], wgt[i:i + 1], 0.0).astype(jnp.bfloat16)
            hots.append((low_hot, high_hot))
        for i in range(0, GROUP, 2):
            (low_a, high_a), (low_b, high_b) = hots[i:i + 2]
            left = jnp.concatenate([jnp.concatenate([high_a, blank], 1), jnp.concatenate([blank, high_b], 1)], 0)
            right = jnp.concatenate([low_a, low_b], 1)
            tile_ref[i * high_count:(i + 2) * high_count, :] = dot(left, right, NT)
        for h in range(high_count):
            part = tile_ref[pl.ds(h, GROUP, stride=high_count), :]
            matrix_ref[pl.ds(first, GROUP), h * LANES:(h + 1) * LANES] = part.astype(jnp.bfloat16)
        return carry

    lax.fori_loop(0, rows // GROUP, build, 0)


def sums_kernel(count, matrix_ref, own, partner, table_own, table_partner, measured, keep, send, target, sem):
    half, rays, width = keep.shape
    me, side, _ = position()
    fetch = pltpu.make_async_copy(measured.at[pl.ds(side * half, half)], target, sem)
    fetch.start()
    sums_own = dot(matrix_ref[...], own[...], NT).astype(jnp.bfloat16)
    sums_partner = dot(matrix_ref[...], partner[...], NT).astype(jnp.bfloat16)
    fetch.wait()
    high = (me // (count // 2)) & 1
    for i in range(half):
        rows = slice(i * rays, (i + 1) * rays)
        for out, bit in ((send, 1 - high), (keep, high)):
            at = aligned(bit, width)
            total = dot(sums_own[rows], table_own[i, :, at], NN) + dot(sums_partner[rows], table_partner[i, :, at], NN)
            out[i] = total - (2.0 / count) * target[i, :, at]


def penalty_kernel(count, pieces, cut, first, own, partner, *refs):
    blocks, refs = refs[:count - 2], refs[count - 2:]
    if first:
        harm, near, far = refs[0], refs[1], refs[2:2 + (count - 2) * pieces]
        outs, waves, refs = refs[2 + len(far):][:count], refs[2 + len(far) + count], refs[3 + len(far) + count:]
    else:
        waves, outs, refs = refs[0], refs[1:count + 1], refs[count + 1:]
    stack, turned, acc = refs
    me, _, place = position()
    height = outs[0].shape[0]
    width = waves.shape[1] // pieces
    at = columns(me, own.shape[1] // count, cut)
    stack[0:height, :] = own[:, at]
    stack[height:2 * height, :] = partner[:, at]
    for j in range(2, count):
        start = 0 if j == count - 1 else cut[0]
        stack[j * height:(j + 1) * height, :] = blocks[j - 2][:, start:start + cut[1]]
    turned[...] = jnp.swapaxes(stack[...], 0, 1)
    for r in range(pieces):
        span = slice(r * width, (r + 1) * width)
        if first:
            waves[0:height, span] = harm[:, aligned(place ^ r, width)]
            waves[height:2 * height, span] = near[:, aligned(place ^ r, width)]
            for j in range(2, count):
                waves[j * height:(j + 1) * height, span] = far[(j - 2) * pieces + r][...]
        wave = waves[:, span]
        field = dot(turned[...], wave, NN)
        slope = (0.5 * jnp.tanh(0.5 * field) - 0.5).astype(jnp.bfloat16)
        part = dot(wave, slope, NT)
        if r > 0:
            part += acc[...]
        if r < pieces - 1:
            acc[...] = part
        else:
            for j in range(count):
                outs[j][...] = part[j * height:(j + 1) * height].astype(outs[j].dtype)


def data_kernel(count, cuts, split, *refs):
    halves, refs = (refs[:split], refs[split:2 * split]), refs[2 * split:]
    res_mine, res_other, table_mine, table_other, top_ref, low_ref, coef = refs[:7]
    refs = refs[7:]
    order = [(0, j) for j in range(count)] + [(t, j) for t in range(1, len(cuts)) for j in range(count)]
    ready = [key for key in order if key[0] == 0 or key[1] < 2]
    grads, refs = dict(zip(ready, refs)), refs[len(ready):]
    updated, residual_ref, later = refs[0], refs[1], refs[2:1 + len(cuts)]
    back_a, back_b, buf, sems, out_sems = refs[1 + len(cuts):]
    me, side, _ = position()
    half, rays, width = halves[0][0].shape
    block = coef.shape[1] // count
    own_width = residual_ref.shape[2]
    spots, copies = {}, {}
    for n, (t, j) in enumerate(order):
        if (t, j) in grads:
            spots[t, j] = buf.at[ready.index((t, j)), :, 0:cuts[t][1]]
        else:
            spots[t, j] = later[t - 1].at[j - 2]
        copies[t, j] = pltpu.make_async_copy(coef.at[:, columns(me ^ j, block, cuts[t])], spots[t, j], sems.at[n])
        copies[t, j].start()
    for back, parts, table in ((back_a, halves[0], table_mine), (back_b, halves[1], table_other)):
        for i in range(half):
            total = dot(table[i, :, aligned(me // 2 if split > 1 else 0, width)], parts[0][i], NT)
            for p in range(1, split):
                total += dot(table[i, :, aligned((me // 2) ^ p, width)], parts[p][i], NT)
            back[:, i * rays:(i + 1) * rays] = total.astype(jnp.bfloat16)
    writes = []
    for t, j in order:
        at = columns(me ^ j, block, cuts[t])
        grad = dot(back_a[...], top_ref[:, at], NN) + dot(back_b[...], low_ref[:, at], NN)
        copies[t, j].wait()
        spot = spots[t, j]
        if (t, j) in grads:
            spot[...] = spot[...] - 0.5 * grad - 0.5 * grads[t, j][...].astype(jnp.float32)
            writes.append(pltpu.make_async_copy(spot, updated.at[:, at], out_sems.at[len(writes)]))
            writes[-1].start()
        else:
            spot[...] = spot[...] - 0.5 * grad
    for q in range(2):
        @pl.when(side == q)
        def _():
            for i in range(half):
                residual_ref[side * half + i] = res_mine[i, :, q * own_width:(q + 1) * own_width]
                residual_ref[(1 - side) * half + i] = res_other[i, :, q * own_width:(q + 1) * own_width]
    for w in writes:
        w.wait()


def finish_kernel(count, cut, masks, later, *refs):
    grads = refs[:len(masks)]
    _, updated, buf, sems = refs[len(masks):]
    block = updated.shape[1] // count
    writes = []
    height = updated.shape[0]
    strip = height // 2 if height % 16 == 0 else height
    for n, j in enumerate(masks):
        at = columns(position()[0] ^ j, block, cut)
        for half, top in enumerate(range(0, height, strip)):
            rows = slice(top, top + strip)
            buf[n, rows] = later[j - 2, rows] - 0.5 * grads[n][rows].astype(jnp.float32)
            writes.append(pltpu.make_async_copy(buf.at[n, rows], updated.at[rows, at], sems.at[n, half]))
            writes[-1].start()
    for w in writes:
        w.wait()


def step_of(coefficients, measured, ray_voxels, ray_weights, angle_ids, angle_table, harmonics):
    coef_local, cols = coefficients.shape
    projections, _, rays, channels = measured.shape
    rows = projections * rays
    samples = ray_voxels.shape[2]
    count = lax.axis_size("coef")
    me = lax.axis_index("coef")
    half = projections // 2
    block = cols // count
    cuts = cuts_of(block)
    bf16, f32 = jnp.bfloat16, jnp.float32
    shape = jax.ShapeDtypeStruct

    def kernel(body_of, ins, outs, out_shape, scratch=(), grant=12, aliases={}):
        return pl.pallas_call(
            body_of,
            in_specs=ins,
            out_specs=outs,
            out_shape=out_shape,
            scratch_shapes=list(scratch),
            input_output_aliases=aliases,
            compiler_params=pltpu.CompilerParams(vmem_limit_bytes=grant << 20),
        )

    group_bits = 1 if lax.axis_size("groups") % 2 == 0 else 0
    slab_count = lax.axis_size("slab")
    slab_bits = 1 if slab_count % 2 == 0 else 0
    pieces = 1 << (group_bits + slab_bits)
    width = harmonics.shape[1] // pieces
    rows_shape = (rows, samples)
    coef_far, measured_far, vox_far, wgt_far, ids_far, table_far, harm_far = [
        pltpu.with_memory_space_constraint(v, pltpu.HBM)
        for v in (
            coefficients,
            measured.reshape(projections, rays, channels),
            ray_voxels.reshape(rows_shape),
            ray_weights.reshape(rows_shape),
            angle_ids,
            angle_table,
            harmonics,
        )
    ]

    piece = kernel(
        piece_kernel, [HBM], VMEM, shape((coef_local, width), bf16), [pltpu.SemaphoreType.DMA(())], grant=4
    )(harm_far)
    fetched = {m: [swap(piece, "coef", m)] for m in range(2, count, 2)}
    table_shape = shape((half,) + angle_table.shape[1:], bf16)
    *parts, own, vox, wgt, table_mine, table_other, harm_own = kernel(
        lambda *refs: prepare_kernel(count, cuts, *refs),
        [HBM] * 6,
        [VMEM] * (count + len(cuts) + 3),
        [shape((coef_local, block), bf16)] * (count - 3)
        + [shape((coef_local, cut[1]), bf16) for cut in cuts]
        + [shape((coef_local, cols), bf16)]
        + [shape((rows // 2, samples), jnp.int32)] * 2
        + [table_shape] * 2
        + [shape(harmonics.shape, bf16)],
        [
            pltpu.VMEM((count, coef_local, block), f32),
            pltpu.SMEM(angle_ids.shape, jnp.int32),
            pltpu.SemaphoreType.DMA((count + 4 + projections,)),
        ],
    )(ids_far, coef_far, vox_far, wgt_far, table_far, harm_far)
    received = []
    for t in range(len(cuts)):
        if t == 0:
            early = [swap(parts[m - 2], "coef", m) for m in range(2, count - 1)]
        received.append(early + [swap(parts[count - 3 + t], "coef", count - 1)])
    partner = swap(own, "coef", 1)
    near = swap(harm_own, "coef", 1)
    table_partner = swap(table_other, "coef", 1)
    moves = [(0, 1)] * slab_bits + [(1, 0)] * group_bits + [(1, 1)] * (slab_bits * group_bits)
    for m in fetched:
        for up, along in moves:
            total = lax.axis_size("groups") * slab_count
            pairs = [(i, (((i // slab_count) ^ up) * slab_count) + ((i % slab_count) ^ along)) for i in range(total)]
            fetched[m].append(lax.ppermute(fetched[m][0], ("groups", "slab"), pairs))

    top = kernel(
        build_kernel,
        [VMEM, VMEM],
        VMEM,
        shape((rows // 2, cols), bf16),
        [pltpu.VMEM((GROUP * cols // LANES, LANES), f32)],
    )(vox, wgt)
    low = swap(top, "coef", 1)
    for m in list(fetched):
        fetched[m ^ 1] = [swap(v, "coef", 1) for v in fetched[m]]
    far = [v for m in range(2, count) for v in fetched[m]]

    total, send = kernel(
        lambda *refs: sums_kernel(count, *refs),
        [VMEM] * 5 + [HBM],
        [VMEM, VMEM],
        [shape((half, rays, channels // 2), f32)] * 2,
        [pltpu.VMEM((half, rays, channels), f32), pltpu.SemaphoreType.DMA(())],
    )(top, own, partner, table_mine, table_partner, measured_far)

    masks = [1 << n for n in range(1, count.bit_length() - 1)]
    for mask in masks[::-1]:
        if mask < count // 2:
            width = total.shape[2] // 2
            bit = jnp.where((me & mask) == 0, 0, 1)
            send = lax.dynamic_slice_in_dim(total, (1 - bit) * width, width, 2)
            total = lax.dynamic_slice_in_dim(total, bit * width, width, 2)
        total = total + swap(send, "coef", mask)

    wide = shape((count * coef_local, harmonics.shape[1]), bf16)
    returned = []
    for t, cut in enumerate(cuts):
        first = t == 0
        extra = [harm_own, near, *far] if first else [waves]
        outs = kernel(
            lambda *refs: penalty_kernel(count, pieces, cut, first, *refs),
            [VMEM] * (count + len(extra)),
            [VMEM] * (count + first),
            [shape((coef_local, cut[1]), bf16)] * count + [wide] * first,
            [
                pltpu.VMEM((count * coef_local, cut[1]), bf16),
                pltpu.VMEM((cut[1], count * coef_local), bf16),
                pltpu.VMEM((count * coef_local, cut[1]), f32),
            ],
        )(own, partner, *received[t], *extra)
        if first:
            waves = outs[-1]
        back = [outs[0]]
        for m in range(1, count):
            back.append(swap(outs[m], "coef", m))
        returned.append(back)
        if first:
            half_mine = [total.astype(bf16)]
            for mask in masks:
                other = [swap(v, "coef", mask) for v in half_mine]
                if total.shape[2] % LANES == 0:
                    half_mine = half_mine + other
                    continue
                low_bit, pair = (me & mask) == 0, (half_mine[0], other[0])
                ordered = [jnp.where(low_bit, *pair), jnp.where(low_bit, *pair[::-1])]
                half_mine = [jnp.concatenate(ordered, 2)]
    res_other = swap(total, "coef", 1)
    half_other = [swap(v, "coef", 1) for v in half_mine]

    ready = [(t, j) for t in range(len(cuts)) for j in range(count) if t == 0 or j < 2]
    updated, residual, *later = kernel(
        lambda *refs: data_kernel(count, cuts, len(half_mine), *refs),
        [VMEM] * (2 * len(half_mine) + 6) + [HBM] + [VMEM] * len(ready),
        [HBM] + [VMEM] * len(cuts),
        [shape((coef_local, cols), f32), shape((projections, rays, channels // count), f32)]
        + [shape((count - 2, coef_local, cut[1]), f32) for cut in cuts[1:]],
        [
            pltpu.VMEM((coef_local, rows // 2), bf16),
            pltpu.VMEM((coef_local, rows // 2), bf16),
            pltpu.VMEM((len(ready), coef_local, max(cut[1] for cut in cuts)), f32),
            pltpu.SemaphoreType.DMA((len(cuts) * count,)),
            pltpu.SemaphoreType.DMA((len(ready),)),
        ],
    )(
        *half_mine,
        *half_other,
        total,
        res_other,
        table_mine,
        table_other,
        top,
        low,
        coef_far,
        *[returned[t][j] for t, j in ready],
    )
    remote = list(range(2, count))
    middle = len(remote) // 2
    for t, cut in list(enumerate(cuts))[1:]:
        for masks in (remote[:middle], remote[middle:]):
            if not masks:
                continue
            updated = kernel(
                lambda *refs: finish_kernel(count, cut, masks, *refs),
                [VMEM] * (len(masks) + 1) + [HBM],
                HBM,
                shape((coef_local, cols), f32),
                [pltpu.VMEM((len(masks), coef_local, cut[1]), f32), pltpu.SemaphoreType.DMA((len(masks), 2))],
                aliases={len(masks) + 1: 0},
            )(later[t - 1], *[returned[t][m] for m in masks], updated)
    return (updated, residual[:, None])


def solution(mesh):
    in_specs = (
        P("coef", ("groups", "slab")),
        P("groups", "slab", None, None),
        P(),
        P(),
        P(),
        P(None, "coef", None),
        P("coef", None),
    )
    out_specs = (P("coef", ("groups", "slab")), P("groups", "slab", None, "coef"))
    return jax.shard_map(step_of, mesh=mesh, in_specs=in_specs, out_specs=out_specs, check_vma=False)
```
